32 devices in a mesh: seq: 4 (over y, x), dp: 8 (over z, core).
Axes of the slice: x: 2, y: 2, z: 4, core: 2. Of those that a mesh axis runs over, the one named last changes fastest.
Arguments:
- layer_input: bfloat16 [8, 1024, 2048], P('dp', 'seq'), may hold values from -6 to 6
- out_cotangent: bfloat16 [8, 1024, 2048], P('dp', 'seq'), may hold values from -6 to 6
- gain_attention: float32 [2048], replicated, may hold values from 0.5 to 1.5
- gain_query: float32 [128], replicated, may hold values from 1 to 2
- gain_key: float32 [128], replicated, may hold values from 1 to 2
- gain_ffn: float32 [2048], replicated, may hold values from 0.5 to 1.5
- w_qkv: bfloat16 [3, 2048, 2048], P(None, None, ('seq', 'dp')), may hold values from -0.125 to 0.125
- w_output: bfloat16 [2048, 2048], P(('seq', 'dp')), may hold values from -0.5 to 0.5
- a_attention: bfloat16 [4, 2048, 128], P(None, ('seq', 'dp')), may hold values from -0.125 to 0.125
- b_attention: bfloat16 [4, 128, 2048], P(None, None, ('seq', 'dp')), may hold values from -0.75 to 0.75
- expert_w_in: bfloat16 [16, 2, 2048, 1024], P('dp'), may hold values from -0.125 to 0.125
- expert_w_down: bfloat16 [16, 1024, 2048], P('dp'), may hold values from -0.75 to 0.75
- expert_a_in: bfloat16 [16, 2, 2048, 128], P('dp'), may hold values from -0.125 to 0.125
- expert_b_in: bfloat16 [16, 2, 128, 1024], P('dp'), may hold values from -0.75 to 0.75
- expert_a_down: bfloat16 [16, 1024, 128], P('dp'), may hold values from -0.1875 to 0.1875
- expert_b_down: bfloat16 [16, 128, 2048], P('dp'), may hold values from -0.75 to 0.75
- route_experts: int32 [8, 1024, 8], P('dp', 'seq'), may hold values from 0 to 15, all different within a row; in each aligned block of 256 rows (0 to 255, 256 to 511, ..., all dimensions but the last counted through in order) at most 144 rows name the same one
- route_gates: float32 [8, 1024, 8], P('dp', 'seq'), may hold values from 0.0625 to 0.1875
- doc_lengths: int32 [8, 8], P('dp'), may hold values from 1 to 512, 1024 in all within a row
- adapter_ids: int32 [8, 8], P('dp'), may hold values from 0 to 7
Outputs:
- layer_output: bfloat16 [8, 1024, 2048], P('dp', 'seq')
- input_grad: bfloat16 [8, 1024, 2048], P('dp', 'seq')
- grad_a_attention: float32 [4, 2048, 128], P(None, ('seq', 'dp'))
- grad_b_attention: float32 [4, 128, 2048], P(None, None, ('seq', 'dp'))
- grad_expert_a_in: float32 [16, 2, 2048, 128], P('dp', None, 'seq')
- grad_expert_b_in: float32 [16, 2, 128, 1024], P('dp', None, None, 'seq')
- grad_expert_a_down: float32 [16, 1024, 128], P('dp', 'seq')
- grad_expert_b_down: float32 [16, 128, 2048], P('dp', None, 'seq')
The draws below stay inside these ranges and needn't reach their ends.
Inputs may be any that keep to these rules, and one draw needn't show every extreme that they name: `route_experts`: each row names 8 different experts; within the rows of one device no expert is named more than 144 times, and in some device's rows one expert is named exactly 144 times. `doc_lengths`: each sequence's 8 lengths sum to 1024, and its longest document has 512 tokens.
All inputs are finite; a program needn't handle non-finite values.
Results may differ from the reference program's by a relative error of at most 0.024.
Values may be sent and summed in bfloat16 or wider, within the bound.
A program may use at most 320 MiB of HBM per device.

```python
import math
import jax
import jax.numpy as jnp
import numpy as np
from jax import lax

D = 2048
H = 16
HD = 128
FF = 1024
TOP = 8
R = 16
SETS = 8
DOCS = 8
TOK_DEV = 256
LENGTH = 1024
SEQS = 8
EXPERTS = 16
CAP = 144
N_SEQ = 4
N_DP = 8


def touch_ends(drawn, key, low, high):
    place = [jax.random.randint(jax.random.fold_in(key, axis), (), 0, length) for axis, length in enumerate(drawn.shape)]
    main_axis = drawn.shape.index(max(drawn.shape))
    next_to = place[:main_axis] + [(place[main_axis] + 1) % drawn.shape[main_axis]] + place[main_axis + 1:]
    return drawn.at[tuple(place)].set(low).at[tuple(next_to)].set(high)


def steps_of(stream_key, dims, shards, least, high):
    def one(dim, parts):
        heights = jax.random.uniform(jax.random.fold_in(jax.random.fold_in(stream_key, 6), dim), (parts,), jnp.float32, least / len(shards), high / len(shards))
        return jnp.repeat(jnp.exp(heights), dims[dim] // parts).reshape((-1,) + (1,) * (len(dims) - dim - 1))

    loudness = one(*shards[0])
    for cut in shards[1:]:
        loudness = loudness * one(*cut)
    return loudness


def length_profile(amount, total, bound, lean):
    portions = [(1 << 20) // math.isqrt(grade ** lean) + 1 for grade in range(2, amount + 1)]
    rest, given = total - bound - (amount - 1), [1] * (amount - 1)
    while rest > 0:
        candidates = [i for i in range(amount - 1) if given[i] < bound]
        mass, remaining = sum([portions[i] for i in candidates]), rest
        for i in candidates:
            more = min(bound - given[i], max(1, remaining * portions[i] // mass), rest)
            given[i] = given[i] + more
            rest = rest - more
    return np.array([bound] + given)


def uneven_parts(own_key, count, total, limit, lean):
    if count == 2:
        one = jax.random.randint(own_key, (), max(1, total - limit), min(limit, total - 1) + 1)
        return jnp.stack([one, total - one])
    sizes = jnp.asarray(length_profile(count, total, limit, lean), jnp.int32)
    couples = (count - 1) // 2
    giver, taker = sizes[1:1 + 2 * couples:2], sizes[2:2 + 2 * couples:2]
    slack = jnp.minimum(giver - 1, limit - taker)
    shifted = jax.random.randint(jax.random.fold_in(own_key, 1), (couples,), 0, 1 << 20) % (slack + 1)
    sizes = sizes.at[1:1 + 2 * couples:2].set(giver - shifted).at[2:2 + 2 * couples:2].set(taker + shifted)
    return sizes[jax.random.permutation(jax.random.fold_in(own_key, 2), count)]


def shared_out(key, own, number, rows, amount, top, bound, skew):
    sequence = jax.random.permutation(key, amount)
    crowded, common = load_shares(amount, rows * top, bound, skew, True), load_shares(amount, rows * top, bound, skew, False)
    places = jnp.arange(amount)

    def named(sizes, offset_by):
        used = int((sizes > 0).sum())
        fixed = max(1, used // 4)
        shifted = fixed + (places - fixed + offset_by * (used - fixed)) % max(1, amount - fixed)
        return jnp.zeros((amount,), jnp.int32).at[sequence[jnp.where(places < fixed, places, shifted)]].set(jnp.asarray(sizes, jnp.int32))

    sizes = jnp.where(number % 4 == 0, named(crowded, number // 4), named(common, number - number // 4 - 1))
    mixed = jax.random.permutation(jax.random.fold_in(own, 3), amount)
    donor, sink = mixed[0:amount // 2 * 2:2], mixed[1:amount // 2 * 2:2]
    room = jnp.minimum(sizes[donor] - 1, bound - sizes[sink]) // 2
    room = jnp.where((donor == sequence[0]) | (sink == sequence[0]) | (sizes[sink] == 0), 0, jnp.maximum(room, 0))
    shifted = jax.random.randint(jax.random.fold_in(own, 4), (amount // 2,), 0, 1 << 20) % (room + 1)
    sizes = sizes.at[donor].add(-shifted).at[sink].add(shifted)
    members = jnp.searchsorted(jnp.cumsum(sizes), jnp.arange(rows * top), side="right").astype(jnp.int32)
    listing = members.reshape(top, rows).T
    listing = listing[jax.random.permutation(jax.random.fold_in(own, 1), rows)]
    offset_by = jax.random.randint(jax.random.fold_in(own, 2), (rows, 1), 0, top)
    return jnp.take_along_axis(listing, (jnp.arange(top)[None, :] + offset_by) % top, axis=1)


def load_shares(number_of, total, most, skew, full):
    portions = [(1 << 20) // math.isqrt(rank ** skew) + 1 for rank in range(1, number_of + 1)]
    largest = most if full else min(most, max(-(-total // number_of), total * portions[0] // sum(portions)))
    least = 1 if total - largest >= number_of - 1 else 0
    given, spare = [largest] + [least] * (number_of - 1), total - largest - least * (number_of - 1)
    while spare > 0:
        candidates = [i for i in range(1, number_of) if given[i] < largest] or [i for i in range(1, number_of) if given[i] < most]
        whole, remaining = sum([portions[i] for i in candidates]), spare
        for i in candidates:
            more = min(most - given[i], max(1, remaining * portions[i] // whole), spare)
            given[i] = given[i] + more
            spare = spare - more
    return np.array(given)


def scatter_about(rng, extent, scale, bound, pieces=(), kind=jnp.bfloat16):
    values = jax.random.normal(rng, extent, jnp.float32) * scale
    if len(pieces) > 0:
        values = steps_of(rng, extent, pieces, -0.22, 0.18) * values
    return jnp.clip(values, min=-bound, max=bound).astype(kind)


def setup_inputs(seed: int = 0) -> dict:
    key_of = jax.random.split(jax.random.key(seed), 21)
    layer_input = scatter_about(key_of[0], (SEQS, LENGTH, D), 1.0, 6.0, ((0, 8), (1, 4)))
    out_cotangent = scatter_about(key_of[1], (SEQS, LENGTH, D), 1.0, 6.0, ((0, 8), (1, 4)))
    gain_attention = jnp.clip(1.0 + 0.1 * jax.random.normal(key_of[2], (D,), jnp.float32), 0.5, 1.5)
    gain_query = jnp.clip(jnp.exp(jax.random.uniform(key_of[3], (HD,), jnp.float32, math.log(1.0), math.log(2.0))), 1.0, 2.0)
    gain_key = jnp.clip(jnp.exp(jax.random.uniform(key_of[4], (HD,), jnp.float32, math.log(1.0), math.log(2.0))), 1.0, 2.0)
    gain_ffn = jnp.clip(1.0 + 0.1 * jax.random.normal(key_of[5], (D,), jnp.float32), 0.5, 1.5)
    w_qkv = scatter_about(key_of[6], (3, D, D), D ** -0.5, 0.125, ((2, 32),))
    w_output = scatter_about(key_of[7], (D, D), (D // 16) ** -0.5, 0.5, ((0, 32),))
    a_attention = scatter_about(key_of[8], (4, D, SETS * R), D ** -0.5, 0.125, ((1, 32),))
    b_attention = scatter_about(key_of[9], (4, SETS * R, D), (4 * R) ** -0.5, 0.75, ((2, 32),))
    expert_w_in = scatter_about(key_of[10], (EXPERTS, 2, D, FF), D ** -0.5, 0.125, ((0, 8),))
    expert_w_down = scatter_about(key_of[11], (EXPERTS, FF, D), (FF // 16) ** -0.5, 0.75, ((0, 8),))
    expert_a_in = scatter_about(key_of[12], (EXPERTS, 2, D, SETS * R), D ** -0.5, 0.125, ((0, 8),))
    expert_b_in = scatter_about(key_of[13], (EXPERTS, 2, SETS * R, FF), (4 * R) ** -0.5, 0.75, ((0, 8),))
    expert_a_down = scatter_about(key_of[14], (EXPERTS, FF, SETS * R), FF ** -0.5, 0.1875, ((0, 8),))
    expert_b_down = scatter_about(key_of[15], (EXPERTS, SETS * R, D), (4 * R) ** -0.5, 0.75, ((0, 8),))
    route_experts_keys = jax.random.split(jax.random.fold_in(key_of[16], 1), SEQS * LENGTH // TOK_DEV)
    route_experts_turns = jax.random.permutation(jax.random.fold_in(key_of[16], 3), SEQS * LENGTH // TOK_DEV)
    route_experts = jax.vmap(lambda own, number: shared_out(jax.random.fold_in(key_of[16], 2), own, number, TOK_DEV, EXPERTS, TOP, CAP, 1))(route_experts_keys, route_experts_turns).reshape((SEQS, LENGTH, TOP))
    route_gates = jnp.clip(0.0625 + 0.125 * jax.random.uniform(key_of[17], (SEQS, LENGTH, TOP), jnp.float32) ** steps_of(key_of[17], (SEQS, LENGTH, TOP), ((0, 8), (1, 4)), -0.2, 0.2), 0.0625, 0.1875)
    doc_lengths = jax.vmap(lambda own: uneven_parts(own, DOCS, LENGTH, LENGTH // 2, 1))(jax.random.split(key_of[18], SEQS)).reshape((SEQS, DOCS)).astype(jnp.int32)
    adapter_ids = touch_ends(jax.random.randint(key_of[19], (SEQS, DOCS), 0, SETS), jax.random.fold_in(key_of[19], 1), 0, SETS - 1).astype(jnp.int32)
    return dict(layer_input=layer_input, out_cotangent=out_cotangent, gain_attention=gain_attention, gain_query=gain_query, gain_key=gain_key, gain_ffn=gain_ffn, w_qkv=w_qkv, w_output=w_output, a_attention=a_attention, b_attention=b_attention, expert_w_in=expert_w_in, expert_w_down=expert_w_down, expert_a_in=expert_a_in, expert_b_in=expert_b_in, expert_a_down=expert_a_down, expert_b_down=expert_b_down, route_experts=route_experts, route_gates=route_gates, doc_lengths=doc_lengths, adapter_ids=adapter_ids)


@jax.custom_vjp
def low(v):
    return lax.optimization_barrier(v.astype(jnp.bfloat16)).astype(jnp.float32)

@jax.custom_vjp
def low_back(v):
    return v

def low_keep(v):
    return (low(v), None)

def low_pass(kept, grad):
    return (grad,)

def back_keep(v):
    return (v, None)

def back_low(kept, grad):
    return (low(grad),)
low.defvjp(low_keep, low_pass)
low_back.defvjp(back_keep, back_low)
norm_epsilon = 1e-06
rope_base = 10000.0
masked_score = -1000000000.0

def matmul(left, right):
    return jnp.dot(left, right, precision=lax.Precision.HIGHEST, preferred_element_type=jnp.float32)

def rms_scale(values, gain_vector):
    return values * lax.rsqrt(lax.optimization_barrier(jnp.mean(values * values, axis=-1, keepdims=True)) + norm_epsilon) * gain_vector

def rotate(values, offset):
    full_width = values.shape[-1]
    half_width = full_width // 2
    frequency = rope_base ** (-(jnp.arange(half_width, dtype=jnp.float32) * 2.0) / full_width)
    angles = offset.astype(jnp.float32)[:, None] * frequency[None, :]
    cosine = jnp.concatenate([jnp.cos(angles), jnp.cos(angles)], axis=-1)[:, None, :]
    sine_table = jnp.concatenate([jnp.sin(angles), jnp.sin(angles)], axis=-1)[:, None, :]
    turned = jnp.concatenate([-values[..., half_width:], values[..., :half_width]], axis=-1)
    return values * cosine + turned * sine_table

def head_prepare(raw_heads, gain_vector, offset):
    return rotate(rms_scale(raw_heads, gain_vector), offset)

def doc_layout(lengths, chosen, length):
    doc_ends = jnp.cumsum(lengths).astype(jnp.int32)
    starts = (doc_ends - lengths).astype(jnp.int32)
    position = jnp.arange(length, dtype=jnp.int32)
    segment = lax.optimization_barrier(jnp.sum((position[:, None] >= doc_ends[None, :]).astype(jnp.int32), axis=1)).astype(jnp.int32)
    doc_pick = (segment[:, None] == jnp.arange(lengths.shape[0], dtype=jnp.int32)[None, :]).astype(jnp.int32)
    offset = (position - lax.optimization_barrier(jnp.sum(doc_pick * starts[None, :], axis=1))).astype(jnp.int32)
    adapter = lax.optimization_barrier(jnp.sum(doc_pick * chosen[None, :], axis=1)).astype(jnp.int32)
    return (segment, offset, adapter)

def column_mask(adapter, columns):
    groups = jnp.arange(columns, dtype=jnp.int32) // R
    return (groups[None, :] == adapter[:, None]).astype(jnp.float32)

def adapted(inputs, weight, down_map, up_map, set_mask):
    reduced = low_back(low(set_mask * matmul(inputs, down_map)))
    return low_back(matmul(inputs, weight) + matmul(reduced, up_map))

def head_attention(operand):
    query_head, key_head, value_head, segment = operand
    scores = matmul(query_head, key_head.T) * HD ** (-0.5)
    same_doc = segment[:, None] == segment[None, :]
    scores = low_back(jnp.where(same_doc, scores, masked_score))
    row_max = lax.optimization_barrier(jnp.max(scores, axis=-1, keepdims=True))
    row_exp = jnp.exp(scores - row_max)
    soft_weights = row_exp / lax.optimization_barrier(jnp.sum(row_exp, axis=-1, keepdims=True))
    return matmul(low(soft_weights), value_head)

def reference(layer_input, out_cotangent, gain_attention, gain_query, gain_key, gain_ffn, w_qkv, w_output, a_attention, b_attention, expert_w_in, expert_w_down, expert_a_in, expert_b_in, expert_a_down, expert_b_down, route_experts, route_gates, doc_lengths, adapter_ids):
    token_count = SEQS * LENGTH
    rank_columns = SETS * R
    segment, offset, adapter = jax.vmap(lambda lengths, chosen: doc_layout(lengths, chosen, LENGTH))(doc_lengths, adapter_ids)
    offset_flat = offset.reshape(-1)
    set_mask = column_mask(adapter.reshape(-1), rank_columns)
    mask_padded = jnp.concatenate([set_mask, jnp.zeros((1, rank_columns), jnp.float32)], axis=0)
    pair_expert = route_experts.reshape(-1)
    pair_count = token_count * TOP
    rows_limit = N_DP * N_SEQ * CAP
    picks = lax.map(lambda expert_id: jnp.nonzero(pair_expert == expert_id, size=rows_limit, fill_value=pair_count)[0].astype(jnp.int32), jnp.arange(EXPERTS, dtype=jnp.int32))
    pick_token = (picks // TOP).astype(jnp.int32)
    gate_padded = jnp.concatenate([route_gates.reshape(-1).astype(jnp.float32), jnp.zeros((1,), jnp.float32)])
    pick_gate = gate_padded[picks]
    qkv_weights = w_qkv.astype(jnp.float32)
    out_weight = w_output.astype(jnp.float32)
    in_weights = expert_w_in.astype(jnp.float32)
    down_weights = expert_w_down.astype(jnp.float32)

    def arrange(values):
        return values.reshape(SEQS, LENGTH, H, HD).transpose(0, 2, 1, 3).reshape(SEQS * H, LENGTH, HD)

    def forward(tokens, att_down, att_up, in_down, in_up, out_down, out_up):
        flat_tokens = tokens.reshape(token_count, D)
        normed = low(rms_scale(flat_tokens, gain_attention))
        raw_list = [adapted(normed, qkv_weights[member], att_down[member], att_up[member], set_mask) for member in range(3)]
        query = low_back(low(head_prepare(raw_list[0].reshape(token_count, H, HD), gain_query, offset_flat)))
        key = low_back(low(head_prepare(raw_list[1].reshape(token_count, H, HD), gain_key, offset_flat)))
        value = low(raw_list[2]).reshape(token_count, H, HD)
        segment_heads = jnp.repeat(segment, H, axis=0)
        mixed = lax.map(jax.checkpoint(head_attention), (arrange(query), arrange(key), arrange(value), segment_heads))
        mixed = low_back(low(mixed))
        mixed = mixed.reshape(SEQS, H, LENGTH, HD).transpose(0, 2, 1, 3).reshape(token_count, D)
        hidden = flat_tokens + adapted(mixed, out_weight, att_down[3], att_up[3], set_mask)
        normed_ffn = low(rms_scale(hidden, gain_ffn))
        padded = jnp.concatenate([normed_ffn, jnp.zeros((1, D), jnp.float32)], axis=0)

        def one_expert(operand):
            token_rows, row_gates, w_in, w_down, a_in, b_in, a_down, b_down = operand
            inputs = low_back(padded[token_rows])
            row_mask = mask_padded[token_rows]
            gate_raw = adapted(inputs, w_in[0], a_in[0], b_in[0], row_mask)
            up_raw = adapted(inputs, w_in[1], a_in[1], b_in[1], row_mask)
            activated = low(jax.nn.silu(gate_raw) * up_raw)
            produced = low(adapted(activated, w_down, a_down, b_down, row_mask))
            return produced * row_gates[:, None]
        weighted = lax.map(jax.checkpoint(one_expert), (pick_token, pick_gate, in_weights, down_weights, in_down, in_up, out_down, out_up))
        combined = jnp.zeros((token_count + 1, D), jnp.float32).at[pick_token.reshape(-1)].add(weighted.reshape(-1, D))
        return (hidden + combined[:token_count]).reshape(SEQS, LENGTH, D)
    primals = (layer_input.astype(jnp.float32), a_attention.astype(jnp.float32), b_attention.astype(jnp.float32), expert_a_in.astype(jnp.float32), expert_b_in.astype(jnp.float32), expert_a_down.astype(jnp.float32), expert_b_down.astype(jnp.float32))
    result, pullback = jax.vjp(forward, *primals)
    grads = pullback(out_cotangent.astype(jnp.float32))
    return (result.astype(jnp.bfloat16), grads[0].astype(jnp.bfloat16), grads[1], grads[2], grads[3], grads[4], grads[5], grads[6])
```

```python
import jax
import jax.numpy as jnp
from jax import lax
from jax.sharding import PartitionSpec as P

H = 16
HD = 128
TOP = 8
R = 16


norm_epsilon = 1e-06
rope_base = 10000.0
masked_score = -1000000000.0


def rms_scale(values, gain_vector):
    return (
        values
        * lax.rsqrt(jnp.mean(values * values, axis=-1, keepdims=True) + norm_epsilon)
        * gain_vector
    )


def rotate(values, offset):
    full_width = values.shape[-1]
    half_width = full_width // 2
    frequency = rope_base ** (-(jnp.arange(half_width, dtype=jnp.float32) * 2.0) / full_width)
    angles = offset.astype(jnp.float32)[:, None] * frequency[None, :]
    cosine = jnp.concatenate([jnp.cos(angles), jnp.cos(angles)], axis=-1)[:, None, :]
    sine_table = jnp.concatenate([jnp.sin(angles), jnp.sin(angles)], axis=-1)[:, None, :]
    turned = jnp.concatenate([-values[..., half_width:], values[..., :half_width]], axis=-1)
    return values * cosine + turned * sine_table


def head_prepare(raw_heads, gain_vector, offset):
    return rotate(rms_scale(raw_heads, gain_vector), offset)


def doc_layout(lengths, chosen, position):
    slots = jnp.arange(lengths.shape[0], dtype=jnp.int32)
    doc_ends = jnp.sum(jnp.where(slots[:, None] >= slots[None, :], lengths[None, :], 0), axis=1)
    starts = doc_ends - lengths
    segment = jnp.sum((position[:, None] >= doc_ends[None, :]).astype(jnp.int32), axis=1)
    doc_pick = (segment[:, None] == slots[None, :]).astype(jnp.int32)
    offset = position - jnp.sum(doc_pick * starts[None, :], axis=1)
    adapter = jnp.sum(doc_pick * chosen[None, :], axis=1)
    return (segment, offset, adapter)


def column_mask(adapter, columns):
    groups = jnp.arange(columns, dtype=jnp.int32) // R
    return (groups[None, :] == adapter[:, None]).astype(jnp.float32)


def project(inputs, weight, down_map, up_map, set_mask):
    reduced = (set_mask * jnp.dot(inputs, down_map, preferred_element_type=jnp.float32)).astype(
        jnp.bfloat16
    )
    result = jnp.dot(inputs, weight, preferred_element_type=jnp.float32) + jnp.dot(
        reduced, up_map, preferred_element_type=jnp.float32
    )
    return (result, reduced)


def project_back(inputs, weight, down_map, up_map, set_mask, reduced, grad_result):
    grad_up = jnp.dot(reduced.T, grad_result, preferred_element_type=jnp.float32)
    grad_reduced = (
        set_mask * jnp.dot(grad_result, up_map.T, preferred_element_type=jnp.float32)
    ).astype(jnp.bfloat16)
    grad_down = jnp.dot(inputs.T, grad_reduced, preferred_element_type=jnp.float32)
    grad_inputs = jnp.dot(grad_result, weight.T, preferred_element_type=jnp.float32) + jnp.dot(
        grad_reduced, down_map.T, preferred_element_type=jnp.float32
    )
    return (grad_inputs, grad_down, grad_up)


def block_scores(query_part, part_segment, key, segment):
    score_scale = query_part.shape[-1] ** (-0.5)
    scores = (
        jnp.einsum("qhd,khd->hqk", query_part, key, preferred_element_type=jnp.float32)
        * score_scale
    )
    same_doc = part_segment[:, None] == segment[None, :]
    return jnp.where(same_doc[None], scores, masked_score)


def attend(query, key, value, segment):
    length = query.shape[0]
    block_rows = min(512, length)
    block_count = length // block_rows

    def one_block(operand):
        query_part, part_segment = operand
        scores = block_scores(query_part, part_segment, key, segment)
        row_max = jnp.max(scores, axis=-1, keepdims=True)
        row_exp = jnp.exp(scores - row_max)
        row_total = jnp.sum(row_exp, axis=-1, keepdims=True)
        soft_low = (row_exp / row_total).astype(jnp.bfloat16)
        mixed_part = jnp.einsum("hqk,khd->qhd", soft_low, value, preferred_element_type=jnp.float32)
        return (mixed_part, (row_max + jnp.log(row_total))[..., 0])

    mixed, logsum = lax.map(
        one_block,
        (
            query.reshape((block_count, block_rows) + query.shape[1:]),
            segment.reshape(block_count, block_rows),
        ),
    )
    return (mixed.reshape(query.shape), logsum)


def attend_back(query, key, value, segment, logsum, grad_mixed):
    length = query.shape[0]
    block_rows = min(512, length)
    block_count = length // block_rows
    score_scale = query.shape[-1] ** (-0.5)

    def one_block(running, operand):
        grad_key, grad_value = running
        query_part, part_segment, part_logsum, part_grad = operand
        scores = block_scores(query_part, part_segment, key, segment)
        soft_full = jnp.exp(scores - part_logsum[..., None])
        soft_low = soft_full.astype(jnp.bfloat16)
        grad_soft = jnp.einsum("qhd,khd->hqk", part_grad, value, preferred_element_type=jnp.float32)
        row_delta = jnp.sum(soft_full * grad_soft, axis=-1, keepdims=True)
        grad_scores = (soft_full * (grad_soft - row_delta)).astype(jnp.bfloat16)
        grad_part = (
            jnp.einsum("hqk,khd->qhd", grad_scores, key, preferred_element_type=jnp.float32)
            * score_scale
        )
        grad_key = (
            grad_key
            + jnp.einsum(
                "hqk,qhd->khd", grad_scores, query_part, preferred_element_type=jnp.float32
            )
            * score_scale
        )
        grad_value = grad_value + jnp.einsum(
            "hqk,qhd->khd", soft_low, part_grad, preferred_element_type=jnp.float32
        )
        return ((grad_key, grad_value), grad_part)

    zeros_heads = jnp.zeros(query.shape, jnp.float32)
    block_shape = (block_count, block_rows) + query.shape[1:]
    (grad_key, grad_value), grad_query = lax.scan(
        one_block,
        (zeros_heads, zeros_heads),
        (
            query.reshape(block_shape),
            segment.reshape(block_count, block_rows),
            logsum,
            grad_mixed.reshape(block_shape),
        ),
    )
    return (grad_query.reshape(query.shape), grad_key, grad_value)


def expert_forward(inputs, set_mask, w_in, w_down, a_in, b_in, a_down, b_down):
    gate_raw, gate_reduced = project(inputs, w_in[0], a_in[0], b_in[0], set_mask)
    up_raw, up_reduced = project(inputs, w_in[1], a_in[1], b_in[1], set_mask)
    activated = (jax.nn.silu(gate_raw) * up_raw).astype(jnp.bfloat16)
    down_raw, down_reduced = project(activated, w_down, a_down, b_down, set_mask)
    return (
        down_raw.astype(jnp.bfloat16),
        (gate_raw, up_raw, gate_reduced, up_reduced, activated, down_reduced),
    )


def expert_backward(inputs, set_mask, w_in, w_down, a_in, b_in, a_down, b_down, kept, grad_rows):
    gate_raw, up_raw, gate_reduced, up_reduced, activated, down_reduced = kept
    grad_act, grad_a_down, grad_b_down = project_back(
        activated, w_down, a_down, b_down, set_mask, down_reduced, grad_rows
    )
    unused, pull_gated = jax.vjp(
        lambda gate_in, up_in: jax.nn.silu(gate_in) * up_in, gate_raw, up_raw
    )
    grad_gate, grad_up = pull_gated(grad_act)
    grad_from_gate, grad_a_gate, grad_b_gate = project_back(
        inputs, w_in[0], a_in[0], b_in[0], set_mask, gate_reduced, grad_gate.astype(jnp.bfloat16)
    )
    grad_from_up, grad_a_up, grad_b_up = project_back(
        inputs, w_in[1], a_in[1], b_in[1], set_mask, up_reduced, grad_up.astype(jnp.bfloat16)
    )
    grad_inputs = (grad_from_gate + grad_from_up).astype(jnp.bfloat16)
    return (
        grad_inputs,
        jnp.stack([grad_a_gate, grad_a_up]),
        jnp.stack([grad_b_gate, grad_b_up]),
        grad_a_down,
        grad_b_down,
    )


def swap(values, axis, distance, count):
    return lax.ppermute(values, axis, [(i, i ^ distance) for i in range(count)])


def spread(values, axis, count):
    return [values] + [swap(values, axis, k, count) for k in range(1, count)]


def collect(blocks, axis, count):
    total = blocks[0].astype(jnp.float32)
    for k in range(1, count):
        total = total + swap(blocks[k], axis, k, count).astype(jnp.float32)
    return total


def after(values, *earlier):
    return lax.optimization_barrier((values,) + earlier)[0]


def local(
    layer_input,
    out_cotangent,
    gain_attention,
    gain_query,
    gain_key,
    gain_ffn,
    w_qkv,
    w_output,
    a_attention,
    b_attention,
    expert_w_in,
    expert_w_down,
    expert_a_in,
    expert_b_in,
    expert_a_down,
    expert_b_down,
    route_experts,
    route_gates,
    doc_lengths,
    adapter_ids,
):
    low = jnp.bfloat16
    f32 = jnp.float32
    own_rows = layer_input.shape[1]
    full_width = layer_input.shape[2]
    n = lax.axis_size("seq")
    dp_count = lax.axis_size("dp")
    s = lax.axis_index("seq")
    d = lax.axis_index("dp")
    length = own_rows * n
    rank_columns = a_attention.shape[2]
    group_width = full_width // n
    group_heads = H // n
    piece = group_width // dp_count
    group_start = s * group_width
    order = s ^ jnp.arange(n, dtype=jnp.int32)
    position = (order[:, None] * own_rows + jnp.arange(own_rows, dtype=jnp.int32)[None, :]).reshape(-1)
    segment, offset, adapter = doc_layout(doc_lengths[0], adapter_ids[0], position)
    own_adapter = adapter[:own_rows]
    own_mask = column_mask(own_adapter, rank_columns)
    full_mask = column_mask(adapter, rank_columns)

    ab_piece = jnp.concatenate([a_attention, jnp.swapaxes(b_attention, 1, 2)], axis=0)
    ab_group = lax.all_gather(ab_piece, "dp", axis=0)
    ab_group = jnp.swapaxes(ab_group, 0, 1).reshape(8, group_width, rank_columns)
    wt_piece = jnp.swapaxes(w_qkv, 1, 2)
    w_group = [lax.all_gather(wt_piece[m], "dp", axis=0, tiled=True) for m in range(3)]
    wo_group = lax.all_gather(w_output, "dp", axis=0, tiled=True)
    meta = jnp.concatenate(
        [
            route_experts[0].T.astype(f32),
            route_gates[0].T,
            own_adapter[None, :].astype(f32),
            jnp.zeros((7, own_rows), f32),
        ],
        axis=0,
    )
    meta_all = lax.all_gather(meta, "dp", axis=0)
    grad_all_tokens = lax.all_gather(
        after(out_cotangent[0], wo_group), "dp", axis=0
    )

    tokens = layer_input[0].astype(f32)
    normed = rms_scale(tokens, gain_attention).astype(low)
    normed_blocks = spread(normed, "seq", n)
    normed_all = jnp.concatenate(normed_blocks, axis=0)
    share = jnp.concatenate([ab_group[0:3], ab_group[7:8]], axis=0)
    share_blocks = jnp.stack(spread(share, "seq", n))
    share_full = share_blocks[order]
    share_full = jnp.swapaxes(share_full, 0, 1).reshape(4, full_width, rank_columns)
    down_cat = jnp.swapaxes(share_full[0:3], 0, 1).reshape(full_width, 3 * rank_columns)
    upt_output = share_full[3]
    upt_group = ab_group[4:7]
    down_rows = ab_group[3]

    dot = lambda a, b: jnp.dot(a, b, preferred_element_type=f32)
    dot_t = lambda a, b: lax.dot_general(a, b, (((1,), (1,)), ((), ())), preferred_element_type=f32)
    dot_l = lambda a, b: lax.dot_general(a, b, (((0,), (0,)), ((), ())), preferred_element_type=f32)

    reduced_cat = (jnp.tile(full_mask, (1, 3)) * dot(normed_all, down_cat)).astype(low)
    reduced_list = [reduced_cat[:, m * rank_columns : (m + 1) * rank_columns] for m in range(3)]
    raw_list = [
        dot_t(normed_all, w_group[m]) + dot_t(reduced_list[m], upt_group[m]) for m in range(3)
    ]
    query_raw = raw_list[0].reshape(length, group_heads, HD)
    key_raw = raw_list[1].reshape(length, group_heads, HD)
    query_heads = head_prepare(query_raw, gain_query, offset).astype(low)
    key_heads = head_prepare(key_raw, gain_key, offset).astype(low)
    value_heads = raw_list[2].astype(low).reshape(length, group_heads, HD)
    mixed, logsum = attend(query_heads, key_heads, value_heads, segment)
    mixed_group = mixed.astype(low).reshape(length, group_width)

    out_maps = jnp.concatenate([wo_group, down_rows], axis=1)
    partial_out = dot(mixed_group, out_maps).astype(low).reshape(n, own_rows, full_width + rank_columns)
    summed = collect([partial_out[k] for k in range(n)], "seq", n)
    output_reduced = (own_mask * summed[:, full_width:]).astype(low)
    attended = summed[:, :full_width] + dot_t(output_reduced, upt_output)
    hidden = tokens + attended
    normed_ffn = rms_scale(hidden, gain_ffn).astype(low)
    rows_all = lax.all_gather(normed_ffn, "dp", axis=0)

    local_count = expert_w_in.shape[0]
    expert_count = local_count * dp_count
    capacity = own_rows * TOP // expert_count * 9 // 8
    named = meta_all[:, 0:TOP, :].astype(jnp.int32)
    gates_all = meta_all[:, TOP : 2 * TOP, :]
    sets_all = meta_all[:, 2 * TOP, :]
    mine = d * local_count + jnp.arange(local_count, dtype=jnp.int32)
    hit = (named[None] == mine[:, None, None, None]).astype(f32)
    member = jnp.sum(hit, axis=2)
    token_gate = jnp.sum(hit * gates_all[None], axis=2)
    t_index = jnp.arange(own_rows, dtype=jnp.int32)
    upto = (t_index[:, None] <= t_index[None, :]).astype(low)
    rank = jnp.einsum("ejt,tu->eju", member.astype(low), upto, preferred_element_type=f32) - 1.0
    slots = jnp.arange(capacity, dtype=jnp.int32).astype(f32)
    pick = (slots[None, None, :, None] == rank[:, :, None, :]) & (member[:, :, None, :] > 0.5)
    slot_gate = jnp.sum(jnp.where(pick, token_gate[:, :, None, :], 0.0), axis=-1)
    slot_set = jnp.sum(jnp.where(pick, sets_all[None, :, None, :], 0.0), axis=-1)
    pick = pick.astype(low)

    slot_rows = dp_count * capacity
    outs = []
    backs = []
    adapter_parts = []
    for e in range(local_count):
        inputs = jnp.einsum(
            "jct,jtd->jcd", pick[e], rows_all, preferred_element_type=f32
        ).astype(low).reshape(slot_rows, full_width)
        grad_picked = jnp.einsum("jct,jtd->jcd", pick[e], grad_all_tokens, preferred_element_type=f32)
        grad_rows = (slot_gate[e][:, :, None] * grad_picked).astype(low).reshape(slot_rows, full_width)
        row_mask = column_mask(slot_set[e].reshape(-1).astype(jnp.int32), rank_columns)
        weights = (
            expert_w_in[e],
            expert_w_down[e],
            expert_a_in[e],
            expert_b_in[e],
            expert_a_down[e],
            expert_b_down[e],
        )
        produced, kept = expert_forward(inputs, row_mask, *weights)
        scaled = (slot_gate[e].reshape(-1)[:, None] * produced).astype(low)
        outs.append(scaled.reshape(dp_count, capacity, full_width))
        grad_inputs, ga_in, gb_in, ga_down, gb_down = expert_backward(
            inputs, row_mask, *weights, kept, grad_rows
        )
        backs.append(grad_inputs.reshape(dp_count, capacity, full_width))
        adapter_parts.append((ga_in, gb_in, ga_down, gb_down))

    def put_back(parts):
        total = None
        for e in range(local_count):
            term = jnp.einsum("jct,jcd->jtd", pick[e], parts[e], preferred_element_type=f32)
            total = term if total is None else total + term
        return total.astype(low).reshape(dp_count * own_rows, full_width)

    mixture = lax.psum_scatter(put_back(outs), "dp", scatter_dimension=0, tiled=True)
    grad_normed_ffn = lax.psum_scatter(put_back(backs), "dp", scatter_dimension=0, tiled=True).astype(f32)
    layer_output = (hidden + mixture.astype(f32)).astype(low)[None]

    grad_out = out_cotangent[0].astype(f32)
    unused, pull_ffn = jax.vjp(lambda values: rms_scale(values, gain_ffn), hidden)
    grad_hidden = grad_out + pull_ffn(grad_normed_ffn)[0]
    grad_hidden_low = grad_hidden.astype(low)
    grad_reduced_output = (own_mask * dot(grad_hidden_low, upt_output)).astype(low)
    grad_pack = jnp.concatenate([grad_hidden_low, grad_reduced_output, output_reduced], axis=1)
    grad_pack_all = jnp.concatenate(spread(grad_pack, "seq", n), axis=0)
    grad_all = grad_pack_all[:, :full_width]
    grad_reduced_all = grad_pack_all[:, full_width : full_width + rank_columns]
    output_reduced_all = grad_pack_all[:, full_width + rank_columns :]
    grad_mixed_group = dot_t(grad_pack_all[:, : full_width + rank_columns], out_maps).astype(low)
    grad_cols = lax.dynamic_slice_in_dim(grad_all, group_start, group_width, 1)
    grad_upt_output = dot_l(grad_cols, output_reduced_all)
    grad_down_output = dot_l(mixed_group, grad_reduced_all)
    grad_query, grad_key, grad_value = attend_back(
        query_heads,
        key_heads,
        value_heads,
        segment,
        logsum,
        grad_mixed_group.reshape(length, group_heads, HD),
    )
    unused_query, pull_query = jax.vjp(
        lambda values: head_prepare(values, gain_query, offset), query_raw
    )
    unused_key, pull_key = jax.vjp(lambda values: head_prepare(values, gain_key, offset), key_raw)
    grad_raw_list = [
        pull_query(grad_query.astype(low).astype(f32))[0].reshape(length, group_width).astype(low),
        pull_key(grad_key.astype(low).astype(f32))[0].reshape(length, group_width).astype(low),
        grad_value.astype(low).reshape(length, group_width),
    ]
    partial_normed = jnp.zeros((length, full_width), f32)
    partial_reduced = []
    grad_upt = []
    for m in range(3):
        partial_normed = partial_normed + dot(grad_raw_list[m], w_group[m])
        partial_reduced.append(dot(grad_raw_list[m], upt_group[m]))
        grad_upt.append(dot_l(grad_raw_list[m], reduced_list[m]))
    back_pack = jnp.concatenate([partial_normed] + partial_reduced, axis=1).astype(low)
    back_pack = back_pack.reshape(n, own_rows, -1)
    summed_back = collect([back_pack[k] for k in range(n)], "seq", n)
    grad_reduced = (jnp.tile(own_mask, (1, 3)) * summed_back[:, full_width:]).astype(low)
    grad_normed = summed_back[:, :full_width] + dot_t(grad_reduced, down_cat)
    unused_input, pull_input = jax.vjp(lambda values: rms_scale(values, gain_attention), tokens)
    input_grad = (grad_hidden + pull_input(grad_normed)[0]).astype(low)[None]

    grad_reduced_full = jnp.concatenate(spread(grad_reduced, "seq", n), axis=0)
    normed_cols = lax.dynamic_slice_in_dim(normed_all, group_start, group_width, 1)
    grad_down_cat = dot_l(normed_cols, grad_reduced_full)

    def over_dp(parts):
        stacked = jnp.stack(parts).astype(low).reshape(len(parts), dp_count, piece, rank_columns)
        stacked = jnp.swapaxes(stacked, 0, 1)
        return lax.psum_scatter(stacked, "dp", scatter_dimension=0).astype(f32)

    early = over_dp([grad_down_output] + grad_upt + [grad_upt_output])
    late = over_dp([grad_down_cat[:, m * rank_columns : (m + 1) * rank_columns] for m in range(3)])
    grad_a_attention = jnp.concatenate([late, early[0:1]], axis=0)
    grad_b_attention = jnp.swapaxes(early[1:5], 1, 2)

    flat = []
    for ga_in, gb_in, ga_down, gb_down in adapter_parts:
        flat.append(ga_in.astype(low).reshape(2, n, -1, rank_columns))
        flat.append(jnp.swapaxes(gb_in, 1, 2).astype(low).reshape(2, n, -1, rank_columns))
        flat.append(ga_down.astype(low).reshape(1, n, -1, rank_columns))
        flat.append(jnp.swapaxes(gb_down, 0, 1).astype(low).reshape(1, n, -1, rank_columns))
    sizes = [x.shape[0] * x.shape[2] for x in flat]
    flat = jnp.concatenate(
        [jnp.swapaxes(x, 0, 1).reshape(n, -1, rank_columns) for x in flat], axis=1
    )
    flat = lax.psum_scatter(flat, "seq", scatter_dimension=0).astype(f32)
    pieces = []
    start = 0
    for size in sizes:
        pieces.append(flat[start : start + size])
        start += size
    grad_a_in = jnp.stack([pieces[4 * e].reshape(2, -1, rank_columns) for e in range(local_count)])
    grad_b_in = jnp.stack(
        [jnp.swapaxes(pieces[4 * e + 1].reshape(2, -1, rank_columns), 1, 2) for e in range(local_count)]
    )
    grad_a_down = jnp.stack([pieces[4 * e + 2] for e in range(local_count)])
    grad_b_down = jnp.stack([pieces[4 * e + 3].T for e in range(local_count)])
    return (
        layer_output,
        input_grad,
        grad_a_attention,
        grad_b_attention,
        grad_a_in,
        grad_b_in,
        grad_a_down,
        grad_b_down,
    )


def solution(mesh):
    return jax.shard_map(
        local,
        mesh=mesh,
        in_specs=(
            P("dp", "seq", None),
            P("dp", "seq", None),
            P(),
            P(),
            P(),
            P(),
            P(None, None, ("seq", "dp")),
            P(("seq", "dp"), None),
            P(None, ("seq", "dp"), None),
            P(None, None, ("seq", "dp")),
            P("dp", None, None, None),
            P("dp", None, None),
            P("dp", None, None, None),
            P("dp", None, None, None),
            P("dp", None, None),
            P("dp", None, None),
            P("dp", "seq", None),
            P("dp", "seq", None),
            P("dp", None),
            P("dp", None),
        ),
        out_specs=(
            P("dp", "seq", None),
            P("dp", "seq", None),
            P(None, ("seq", "dp"), None),
            P(None, None, ("seq", "dp")),
            P("dp", None, "seq", None),
            P("dp", None, None, "seq"),
            P("dp", "seq", None),
            P("dp", None, "seq"),
        ),
        check_vma=False,
    )
```

```python
import functools

import jax
import jax.numpy as jnp
from jax import lax
from jax.experimental import pallas as pl
from jax.experimental.pallas import tpu as pltpu
from jax.sharding import PartitionSpec as P

H = 16
HD = 128
TOP = 8
R = 16


norm_epsilon = 1e-06
rope_base = 10000.0
masked_score = -1000000000.0


def rms_scale(values, gain_vector):
    return (
        values
        * lax.rsqrt(jnp.mean(values * values, axis=-1, keepdims=True) + norm_epsilon)
        * gain_vector
    )


def rope_tables(offset, width):
    half = width // 2
    frequency = rope_base ** (-(jnp.arange(half, dtype=jnp.float32) * 2.0) / width)
    angles = offset.astype(jnp.float32)[:, None] * frequency[None, :]
    cosine = jnp.cos(angles)
    sine = jnp.sin(angles)
    return jnp.concatenate([cosine, cosine], axis=1), jnp.concatenate([-sine, sine], axis=1)


def dot_nn(a, b):
    return lax.dot_general(a, b, (((1,), (0,)), ((), ())), preferred_element_type=jnp.float32)


def dot_nt(a, b):
    return lax.dot_general(a, b, (((1,), (1,)), ((), ())), preferred_element_type=jnp.float32)


def dot_tn(a, b):
    return lax.dot_general(a, b, (((0,), (0,)), ((), ())), preferred_element_type=jnp.float32)


def normed_head(raw, gain):
    inverse = lax.rsqrt(jnp.mean(raw * raw, axis=-1, keepdims=True) + norm_epsilon)
    return raw * inverse * gain, inverse


def turned_head(values, cosine, sine):
    return values * cosine + pltpu.roll(values, values.shape[-1] // 2, 1) * sine


def unturned_head(grad, cosine, sine):
    return grad * cosine + pltpu.roll(grad * sine, grad.shape[-1] // 2, 1)


def attend_kernel(
    tile, q_raw, k_raw, v_raw, cosine, sine, gain_q, gain_k, seg_col, seg_row, mixed, query, key, value, stat
):
    rows = q_raw.shape[0]
    scale = HD ** (-0.5)
    cos_all = cosine[...]
    sin_all = sine[...]
    normed_q, unused = normed_head(q_raw[...], gain_q[...])
    query[...] = turned_head(normed_q, cos_all, sin_all).astype(jnp.bfloat16)
    normed_k, unused = normed_head(k_raw[...], gain_k[...])
    keys = turned_head(normed_k, cos_all, sin_all).astype(jnp.bfloat16)
    key[...] = keys
    values = v_raw[...].astype(jnp.bfloat16)
    value[...] = values
    values_t = values.T
    for start in range(0, rows, tile):
        part = slice(start, start + tile)
        scores = dot_nt(keys, query[part, :]) * scale
        scores = jnp.where(seg_col[...] == seg_row[:, part], scores, masked_score)
        top = jnp.max(scores, axis=0, keepdims=True)
        weight = jnp.exp(scores - top)
        total = jnp.sum(weight, axis=0, keepdims=True)
        soft = (weight * (1.0 / total)).astype(jnp.bfloat16)
        mixed[part, :] = dot_nn(values_t, soft).T.astype(jnp.bfloat16)
        stat[0, :, part] = top + jnp.log(total)


def attend(raw, cosine, sine, gain_q, gain_k, segment):
    unused, length, width = raw.shape
    heads = width // HD
    tile = min(256, length)
    head = pl.BlockSpec((length, HD), lambda h: (0, h))
    raw_head = [pl.BlockSpec((None, length, HD), functools.partial(lambda m, h: (m, 0, h), m)) for m in range(3)]
    fixed = lambda shape: pl.BlockSpec(shape, lambda h: (0, 0))
    seg = segment.astype(jnp.float32)
    low = jax.ShapeDtypeStruct((length, width), jnp.bfloat16)
    return pl.pallas_call(
        functools.partial(attend_kernel, tile),
        grid=(heads,),
        in_specs=raw_head + [fixed((length, HD)), fixed((length, HD)), fixed((1, HD)), fixed((1, HD)),
                  fixed((length, 1)), fixed((1, length))],
        out_specs=[head, head, head, head, pl.BlockSpec((1, 1, length), lambda h: (h, 0, 0))],
        out_shape=[low, low, low, low, jax.ShapeDtypeStruct((heads, 1, length), jnp.float32)],
        cost_estimate=pl.CostEstimate(
            flops=4 * heads * length * length * HD, bytes_accessed=20 * length * width, transcendentals=heads * length * length
        ),
        name="attend",
    )(raw, raw, raw, cosine, sine, gain_q[None, :], gain_k[None, :], seg[:, None], seg[None, :])


def attend_back_kernel(
    tile, query, key, value, grad_mixed, stat, q_raw, k_raw, cosine, sine, gain_q, gain_k, seg_col, seg_row,
    grad_q, grad_k, grad_v, sum_k, sum_v
):
    rows = q_raw.shape[0]
    scale = HD ** (-0.5)
    keys = key[...]
    values = value[...]
    keys_t = keys.T

    def through(grad, raw_ref, gain_ref, part):
        grad = grad.astype(jnp.bfloat16).astype(jnp.float32)
        raw = raw_ref[part, :]
        gain = gain_ref[...]
        inverse = lax.rsqrt(jnp.mean(raw * raw, axis=-1, keepdims=True) + norm_epsilon)
        grad = unturned_head(grad, cosine[part, :], sine[part, :]) * gain
        dots = jnp.mean(grad * raw, axis=-1, keepdims=True)
        return (inverse * (grad - raw * (inverse * inverse * dots))).astype(jnp.bfloat16)

    for start in range(0, rows, tile):
        part = slice(start, start + tile)
        queries = query[part, :]
        grads = grad_mixed[part, :]
        scores = dot_nt(keys, queries) * scale
        scores = jnp.where(seg_col[...] == seg_row[:, part], scores, masked_score)
        soft = jnp.exp(scores - stat[0, :, part])
        grad_soft = dot_nt(values, grads)
        delta = jnp.sum(soft * grad_soft, axis=0, keepdims=True)
        grad_scores = (soft * (grad_soft - delta)).astype(jnp.bfloat16)
        term_k = dot_nn(grad_scores, queries)
        term_v = dot_nn(soft.astype(jnp.bfloat16), grads)
        if start == 0:
            sum_k[...] = term_k
            sum_v[...] = term_v
        else:
            sum_k[...] += term_k
            sum_v[...] += term_v
        grad_q[part, :] = through(dot_nn(keys_t, grad_scores).T * scale, q_raw, gain_q, part)
    for start in range(0, rows, tile):
        part = slice(start, start + tile)
        grad_k[part, :] = through(sum_k[part, :] * scale, k_raw, gain_k, part)
        grad_v[part, :] = sum_v[part, :].astype(jnp.bfloat16)


def attend_back(kept, grad_mixed, raw, cosine, sine, gain_q, gain_k, segment):
    query, key, value, stat = kept
    unused, length, width = raw.shape
    heads = width // HD
    tile = min(256, length)
    head = pl.BlockSpec((length, HD), lambda h: (0, h))
    raw_head = [pl.BlockSpec((None, length, HD), functools.partial(lambda m, h: (m, 0, h), m)) for m in range(3)]
    fixed = lambda shape: pl.BlockSpec(shape, lambda h: (0, 0))
    seg = segment.astype(jnp.float32)
    low = jax.ShapeDtypeStruct((length, width), jnp.bfloat16)
    return pl.pallas_call(
        functools.partial(attend_back_kernel, tile),
        grid=(heads,),
        in_specs=[head, head, head, head, pl.BlockSpec((1, 1, length), lambda h: (h, 0, 0)), raw_head[0], raw_head[1],
                  fixed((length, HD)), fixed((length, HD)), fixed((1, HD)), fixed((1, HD)),
                  fixed((length, 1)), fixed((1, length))],
        out_specs=[head, head, head],
        out_shape=[low, low, low],
        scratch_shapes=[pltpu.VMEM((length, HD), jnp.float32), pltpu.VMEM((length, HD), jnp.float32)],
        cost_estimate=pl.CostEstimate(
            flops=10 * heads * length * length * HD, bytes_accessed=24 * length * width, transcendentals=heads * length * length
        ),
        name="attend_back",
    )(query, key, value, grad_mixed, stat, raw, raw, cosine, sine, gain_q[None, :], gain_k[None, :],
      seg[:, None], seg[None, :])


def doc_layout(lengths, chosen, position):
    slots = jnp.arange(lengths.shape[0], dtype=jnp.int32)
    doc_ends = jnp.sum(jnp.where(slots[:, None] >= slots[None, :], lengths[None, :], 0), axis=1)
    starts = doc_ends - lengths
    segment = jnp.sum((position[:, None] >= doc_ends[None, :]).astype(jnp.int32), axis=1)
    doc_pick = (segment[:, None] == slots[None, :]).astype(jnp.int32)
    offset = position - jnp.sum(doc_pick * starts[None, :], axis=1)
    adapter = jnp.sum(doc_pick * chosen[None, :], axis=1)
    return (segment, offset, adapter)


def column_mask(adapter, columns):
    groups = jnp.arange(columns, dtype=jnp.int32) // R
    return (groups[None, :] == adapter[:, None]).astype(jnp.float32)


def qkv_kernel(x_ref, reduced_ref, w_ref, up_ref, out_ref):
    width = w_ref.shape[0] * w_ref.shape[1]
    weights = w_ref[...].reshape(width, x_ref.shape[1])
    out_ref[0] = dot_nt(x_ref[...], weights) + dot_nt(reduced_ref[...], up_ref[0])


def qkv_project(normed_all, reduced_cat, w_group, up_group):
    length, width = normed_all.shape
    dp_count, unused, piece, unused = w_group.shape
    group = dp_count * piece
    rank = up_group.shape[2]
    half = dp_count // 2
    return pl.pallas_call(
        qkv_kernel,
        grid=(3, 2),
        in_specs=[
            pl.BlockSpec((length, width), lambda m, p: (0, 0)),
            pl.BlockSpec((length, rank), lambda m, p: (0, m)),
            pl.BlockSpec((half, None, piece, width), lambda m, p: (p, m, 0, 0)),
            pl.BlockSpec((1, group // 2, rank), lambda m, p: (m, p, 0)),
        ],
        out_specs=pl.BlockSpec((1, length, group // 2), lambda m, p: (m, 0, p)),
        out_shape=jax.ShapeDtypeStruct((3, length, group), jnp.float32),
        cost_estimate=pl.CostEstimate(
            flops=6 * length * width * group, bytes_accessed=2 * length * width + 12 * length * group + 6 * group * width,
            transcendentals=0,
        ),
        name="qkv_project",
    )(normed_all, reduced_cat, w_group, up_group)


def qkv_back_kernel(a_ref, b_ref, c_ref, w_ref, out_ref):
    dp_count, unused, piece, cols = w_ref.shape
    total = None
    for m, ref in enumerate((a_ref, b_ref, c_ref)):
        term = dot_nn(ref[...], w_ref[:, m].reshape(dp_count * piece, cols))
        total = term if total is None else total + term
    out_ref[...] = total.astype(jnp.bfloat16)


def qkv_back(grads, w_group):
    length, group = grads[0].shape
    dp_count, unused, piece, width = w_group.shape
    tile = min(256, width)
    whole = pl.BlockSpec((length, group), lambda i: (0, 0))
    return pl.pallas_call(
        qkv_back_kernel,
        grid=(width // tile,),
        in_specs=[whole, whole, whole, pl.BlockSpec((dp_count, 3, piece, tile), lambda i: (0, 0, 0, i))],
        out_specs=pl.BlockSpec((length, tile), lambda i: (0, i)),
        out_shape=jax.ShapeDtypeStruct((length, width), jnp.bfloat16),
        cost_estimate=pl.CostEstimate(
            flops=6 * length * width * group, bytes_accessed=2 * length * width + 6 * length * group + 6 * group * width,
            transcendentals=0,
        ),
        name="qkv_back",
    )(grads[0], grads[1], grads[2], w_group)


def expert_kernel(kept_in, *refs):
    (x_a, x_b, g_a, g_b, pick, pick_t, slot, w_in, w_down, a_in, b_in, a_down, b_down) = refs[:13]
    refs = refs[13 + kept_in:]
    (out_a, out_b, back_a, back_b, xs, ps, act_o, gate_o, up_o, reds) = refs[:10]
    (red_g, red_u, gred_d, down_acc, down_red, gx_acc, gred_g, gred_u, sum_out_a, sum_out_b, sum_back_a, sum_back_b) = refs[10:]
    low = jnp.bfloat16
    e = pl.program_id(0)
    f = pl.program_id(1)
    last = pl.num_programs(1) - 1
    cap = pick.shape[2]
    rank = a_in.shape[3]
    rows = xs.shape[1]
    groups = lax.shift_right_logical(lax.broadcasted_iota(jnp.int32, (rows, rank), 1), R.bit_length() - 1)
    mask = jnp.where(groups.astype(jnp.float32) == slot[0, :, 1:2], 1.0, 0.0)

    @pl.when(f == 0)
    def _():
        for b, (x_ref, g_ref) in enumerate(((x_a, g_a), (x_b, g_b))):
            part = slice(b * cap, (b + 1) * cap)
            xs[0, part, :] = dot_nn(pick[0, b], x_ref[...]).astype(low)
            ps[0, part, :] = (slot[0, part, 0:1] * dot_nn(pick[0, b], g_ref[...])).astype(low)
        red_g[...] = (mask * dot_nn(xs[0], a_in[0, 0])).astype(low)
        red_u[...] = (mask * dot_nn(xs[0], a_in[0, 1])).astype(low)
        gred_d[...] = (mask * dot_nt(ps[0], b_down[0])).astype(low)

    x = xs[0]
    p = ps[0]
    gate = dot_nn(x, w_in[0, 0]) + dot_nn(red_g[...], b_in[0, 0])
    up = dot_nn(x, w_in[0, 1]) + dot_nn(red_u[...], b_in[0, 1])
    grad_act = dot_nt(p, w_down[0]) + dot_nt(gred_d[...], a_down[0])
    sigma = 1.0 / (1.0 + jnp.exp(-gate))
    silu = gate * sigma
    act = (silu * up).astype(low)
    grad_gate = (grad_act * up * (sigma * (1.0 + gate * (1.0 - sigma)))).astype(low)
    grad_up = (grad_act * silu).astype(low)
    act_o[0] = act
    gate_o[0] = grad_gate
    up_o[0] = grad_up
    down_term = dot_nn(act, w_down[0])
    down_red_term = dot_nn(act, a_down[0])
    gx_term = dot_nt(grad_gate, w_in[0, 0]) + dot_nt(grad_up, w_in[0, 1])
    gred_g_term = dot_nt(grad_gate, b_in[0, 0])
    gred_u_term = dot_nt(grad_up, b_in[0, 1])

    @pl.when(f == 0)
    def _():
        down_acc[...] = down_term
        down_red[...] = down_red_term
        gx_acc[...] = gx_term
        gred_g[...] = gred_g_term
        gred_u[...] = gred_u_term

    @pl.when(f > 0)
    def _():
        down_acc[...] += down_term
        down_red[...] += down_red_term
        gx_acc[...] += gx_term
        gred_g[...] += gred_g_term
        gred_u[...] += gred_u_term

    @pl.when(f == last)
    def _():
        reduced_d = (mask * down_red[...]).astype(low)
        back_g = (mask * gred_g[...]).astype(low)
        back_u = (mask * gred_u[...]).astype(low)
        for i, value in enumerate((red_g[...], red_u[...], reduced_d, back_g, back_u, gred_d[...])):
            reds[0, :, i * rank : (i + 1) * rank] = value
        produced = down_acc[...] + dot_nn(reduced_d, b_down[0])
        scaled = (slot[0, :, 0:1] * produced).astype(low)
        grads = (gx_acc[...] + dot_nt(back_g, a_in[0, 0]) + dot_nt(back_u, a_in[0, 1])).astype(low)
        for b, (out_ref, out_sum, back_ref, back_sum) in enumerate(
            ((out_a, sum_out_a, back_a, sum_back_a), (out_b, sum_out_b, back_b, sum_back_b))
        ):
            part = slice(b * cap, (b + 1) * cap)
            for values, total, result in ((scaled, out_sum, out_ref), (grads, back_sum, back_ref)):
                term = dot_nn(pick_t[0, b], values[part, :])

                @pl.when(e == 0)
                def _():
                    total[...] = term

                @pl.when(e > 0)
                def _():
                    total[...] += term

                @pl.when(e == pl.num_programs(0) - 1)
                def _():
                    result[...] = total[...].astype(low)


def run_experts(chunk, x_pair, g_pair, pick, pick_t, slot, weights, kept):
    w_in, w_down, a_in, b_in, a_down, b_down = weights
    experts, unused, width, ff = w_in.shape
    unused, dp_count, cap, own_rows = pick.shape
    rank = a_down.shape[2]
    rows = 2 * cap
    tile = min(256, ff)
    low = jnp.bfloat16
    f32 = jnp.float32
    token = pl.BlockSpec((own_rows, width), lambda e, f: (0, 0), pipeline_mode=pl.Buffered(1))
    stored = [
        ((experts, dp_count * cap, width), (1, rows, width), lambda e, f: (e, chunk, 0)),
        ((experts, dp_count * cap, width), (1, rows, width), lambda e, f: (e, chunk, 0)),
        ((experts, dp_count * cap, ff), (1, rows, tile), lambda e, f: (e, chunk, f)),
        ((experts, dp_count * cap, ff), (1, rows, tile), lambda e, f: (e, chunk, f)),
        ((experts, dp_count * cap, ff), (1, rows, tile), lambda e, f: (e, chunk, f)),
        ((experts, dp_count * cap, 6 * rank), (1, rows, 6 * rank), lambda e, f: (e, chunk, 0)),
    ]
    in_specs = [
        token, token, token, token,
        pl.BlockSpec((1, 2, cap, own_rows), lambda e, f: (e, chunk, 0, 0)),
        pl.BlockSpec((1, 2, own_rows, cap), lambda e, f: (e, chunk, 0, 0)),
        pl.BlockSpec((1, rows, 2), lambda e, f: (e, chunk, 0)),
        pl.BlockSpec((1, 2, width, tile), lambda e, f: (e, 0, 0, f)),
        pl.BlockSpec((1, tile, width), lambda e, f: (e, f, 0)),
        pl.BlockSpec((1, 2, width, rank), lambda e, f: (e, 0, 0, 0)),
        pl.BlockSpec((1, 2, rank, tile), lambda e, f: (e, 0, 0, f)),
        pl.BlockSpec((1, tile, rank), lambda e, f: (e, f, 0)),
        pl.BlockSpec((1, rank, width), lambda e, f: (e, 0, 0)),
    ] + [pl.BlockSpec(memory_space=pl.ANY) for unused in kept]
    part = jax.ShapeDtypeStruct((own_rows, width), low)
    results = pl.pallas_call(
        functools.partial(expert_kernel, len(kept)),
        grid=(experts, ff // tile),
        in_specs=in_specs,
        out_specs=[pl.BlockSpec((own_rows, width), lambda e, f: (0, 0), pipeline_mode=pl.Buffered(1))] * 4
        + [pl.BlockSpec(block, index) for unused, block, index in stored],
        out_shape=[part] * 4 + [jax.ShapeDtypeStruct(shape, low) for shape, unused, unused2 in stored],
        scratch_shapes=[
            pltpu.VMEM((rows, rank), low),
            pltpu.VMEM((rows, rank), low),
            pltpu.VMEM((rows, rank), low),
            pltpu.VMEM((rows, width), f32),
            pltpu.VMEM((rows, rank), f32),
            pltpu.VMEM((rows, width), f32),
            pltpu.VMEM((rows, rank), f32),
            pltpu.VMEM((rows, rank), f32),
        ] + [pltpu.VMEM((own_rows, width), f32) for unused in range(4)],
        input_output_aliases={13 + i: 4 + i for i in range(len(kept))},
        cost_estimate=pl.CostEstimate(
            flops=14 * experts * rows * width * ff, bytes_accessed=experts * (6 * width * ff + 8 * rows * width), transcendentals=experts * rows * ff
        ),
        compiler_params=pltpu.CompilerParams(vmem_limit_bytes=60 * 1024 * 1024),
        name="experts",
    )(*x_pair, *g_pair, pick, pick_t, slot, *weights, *kept)
    return results[:4], results[4:]


def swap(values, axis, distance, count):
    return lax.ppermute(values, axis, [(i, i ^ distance) for i in range(count)])


def spread(values, axis, count):
    return [values] + [swap(values, axis, k, count) for k in range(1, count)]


def collect(blocks, axis, count):
    total = blocks[0].astype(jnp.float32)
    for k in range(1, count):
        total = total + swap(blocks[k], axis, k, count).astype(jnp.float32)
    return total


def spread_pairs(values, count):
    blocks = []
    for c in range(count // 2):
        same = values if c == 0 else swap(values, "dp", 2 * c, count)
        blocks += [same, swap(same, "dp", 1, count)]
    return blocks


def collect_pairs(blocks, count):
    total = None
    for c in range(count // 2):
        pair = blocks[2 * c].astype(jnp.float32) + swap(blocks[2 * c + 1], "dp", 1, count).astype(jnp.float32)
        if c > 0:
            pair = swap(pair.astype(jnp.bfloat16), "dp", 2 * c, count).astype(jnp.float32)
        total = pair if total is None else total + pair
    return total


def after(values, *earlier):
    return lax.optimization_barrier((values,) + earlier)[0]


def local(
    layer_input,
    out_cotangent,
    gain_attention,
    gain_query,
    gain_key,
    gain_ffn,
    w_qkv,
    w_output,
    a_attention,
    b_attention,
    expert_w_in,
    expert_w_down,
    expert_a_in,
    expert_b_in,
    expert_a_down,
    expert_b_down,
    route_experts,
    route_gates,
    doc_lengths,
    adapter_ids,
):
    low = jnp.bfloat16
    f32 = jnp.float32
    own_rows = layer_input.shape[1]
    full_width = layer_input.shape[2]
    n = lax.axis_size("seq")
    dp_count = lax.axis_size("dp")
    s = lax.axis_index("seq")
    d = lax.axis_index("dp")
    length = own_rows * n
    rank_columns = a_attention.shape[2]
    group_width = full_width // n
    group_heads = H // n
    piece = group_width // dp_count
    group_start = s * group_width
    order = s ^ jnp.arange(n, dtype=jnp.int32)
    position = (order[:, None] * own_rows + jnp.arange(own_rows, dtype=jnp.int32)[None, :]).reshape(-1)
    segment, offset, adapter = doc_layout(doc_lengths[0], adapter_ids[0], position)
    own_adapter = adapter[:own_rows]
    own_mask = column_mask(own_adapter, rank_columns)
    full_mask = column_mask(adapter, rank_columns)

    ab_piece = jnp.concatenate([a_attention, jnp.swapaxes(b_attention, 1, 2)], axis=0)
    ab_group = lax.all_gather(ab_piece, "dp", axis=0)
    ab_group = jnp.swapaxes(ab_group, 0, 1).reshape(8, group_width, rank_columns)
    wt_piece = jnp.swapaxes(w_qkv, 1, 2)
    w_group = lax.all_gather(after(wt_piece, ab_group), "dp", axis=0)
    wo_group = lax.all_gather(after(w_output, w_group), "dp", axis=0, tiled=True)
    gates = route_gates[0].T
    gates_high = gates.astype(low)
    meta = jnp.concatenate(
        [
            route_experts[0].T.astype(low),
            gates_high,
            (gates - gates_high.astype(f32)).astype(low),
            own_adapter[None, :].astype(low),
            jnp.zeros((7, own_rows), low),
        ],
        axis=0,
    )
    meta_rows = -(-meta.size // full_width)
    pad_rows = -(-meta_rows // 16) * 16
    meta_flat = jnp.pad(meta.reshape(-1), (0, pad_rows * full_width - meta.size))
    grad_send = jnp.concatenate([out_cotangent[0], meta_flat.reshape(pad_rows, full_width)], axis=0)
    grad_blocks = spread_pairs(after(grad_send, wo_group), dp_count)

    tokens = layer_input[0].astype(f32)
    normed = rms_scale(tokens, gain_attention).astype(low)
    normed_blocks = spread(normed, "seq", n)
    normed_all = jnp.concatenate(normed_blocks, axis=0)
    share = jnp.concatenate([ab_group[0:3], ab_group[7:8]], axis=0)
    share_blocks = jnp.stack(spread(share, "seq", n))
    share_full = share_blocks[order]
    share_full = jnp.swapaxes(share_full, 0, 1).reshape(4, full_width, rank_columns)
    down_cat = jnp.swapaxes(share_full[0:3], 0, 1).reshape(full_width, 3 * rank_columns)
    upt_output = share_full[3]
    upt_group = ab_group[4:7]
    down_rows = ab_group[3]

    dot = lambda a, b: jnp.dot(a, b, preferred_element_type=f32)
    dot_t = lambda a, b: lax.dot_general(a, b, (((1,), (1,)), ((), ())), preferred_element_type=f32)
    dot_l = lambda a, b: lax.dot_general(a, b, (((0,), (0,)), ((), ())), preferred_element_type=f32)

    reduced_cat = (jnp.tile(full_mask, (1, 3)) * dot(normed_all, down_cat)).astype(low)
    reduced_list = [reduced_cat[:, m * rank_columns : (m + 1) * rank_columns] for m in range(3)]
    raw = qkv_project(normed_all, reduced_cat, w_group, upt_group)
    cosine, sine = rope_tables(offset, HD)
    mixed_group, query_heads, key_heads, value_heads, stat = attend(
        raw, cosine, sine, gain_query, gain_key, segment
    )

    out_maps = jnp.concatenate([wo_group, down_rows], axis=1)
    partial_out = dot(mixed_group, out_maps).astype(low).reshape(n, own_rows, full_width + rank_columns)
    summed = collect([partial_out[k] for k in range(n)], "seq", n)
    output_reduced = (own_mask * summed[:, full_width:]).astype(low)
    attended = summed[:, :full_width] + dot_t(output_reduced, upt_output)
    hidden = tokens + attended
    normed_ffn = rms_scale(hidden, gain_ffn).astype(low)
    local_count = expert_w_in.shape[0]
    expert_count = local_count * dp_count
    capacity = own_rows * TOP // expert_count * 9 // 8
    capacity = -(-capacity // 16) * 16
    meta_all = jnp.stack(
        [
            x[own_rows:].reshape(-1)[: meta.size].reshape(meta.shape).astype(f32)
            for x in grad_blocks
        ]
    )
    named = meta_all[:, 0:TOP, :].astype(jnp.int32)
    gates_all = meta_all[:, TOP : 2 * TOP, :] + meta_all[:, 2 * TOP : 3 * TOP, :]
    sets_all = meta_all[:, 3 * TOP, :]
    mine = d * local_count + jnp.arange(local_count, dtype=jnp.int32)
    hit = (named[None] == mine[:, None, None, None]).astype(f32)
    member = jnp.sum(hit, axis=2)
    token_gate = jnp.sum(hit * gates_all[None], axis=2)
    t_index = jnp.arange(own_rows, dtype=jnp.int32)
    upto = (t_index[:, None] <= t_index[None, :]).astype(low)
    rank = jnp.einsum("ejt,tu->eju", member.astype(low), upto, preferred_element_type=f32) - 1.0
    slots = jnp.arange(capacity, dtype=jnp.int32).astype(f32)
    rank = jnp.where(member > 0.5, rank, -1.0)
    pick = slots[None, None, :, None] == rank[:, :, None, :]
    pick_t = (rank[:, :, :, None] == slots[None, None, None, :]).astype(low)
    slot_gate = jnp.sum(jnp.where(pick, token_gate[:, :, None, :], 0.0), axis=-1)
    slot_set = jnp.sum(jnp.where(pick, sets_all[None, :, None, :], 0.0), axis=-1)
    slot = jnp.stack([slot_gate, slot_set], axis=-1).reshape(local_count, dp_count * capacity, 2)
    pick = pick.astype(low)

    row_blocks = spread_pairs(normed_ffn, dp_count)
    weights = (expert_w_in, expert_w_down, expert_a_in, expert_b_in, expert_a_down, expert_b_down)
    outs = []
    backs = []
    kept = ()
    for c in range(dp_count // 2):
        (out_a, out_b, back_a, back_b), kept = run_experts(
            c, row_blocks[2 * c : 2 * c + 2], grad_blocks[2 * c : 2 * c + 2], pick, pick_t, slot, weights, kept
        )
        outs += [out_a, out_b]
        backs += [back_a, back_b]
    grad_normed_ffn = collect_pairs(backs, dp_count)

    grad_out = out_cotangent[0].astype(f32)
    unused, pull_ffn = jax.vjp(lambda values: rms_scale(values, gain_ffn), hidden)
    grad_hidden = grad_out + pull_ffn(grad_normed_ffn)[0]
    grad_hidden_low = grad_hidden.astype(low)
    grad_reduced_output = (own_mask * dot(grad_hidden_low, upt_output)).astype(low)
    grad_pack = jnp.concatenate([grad_hidden_low, grad_reduced_output, output_reduced], axis=1)
    grad_pack_all = jnp.concatenate(spread(grad_pack, "seq", n), axis=0)
    outs = list(after(tuple(outs), grad_pack_all))
    mixture = collect_pairs(outs, dp_count)
    layer_output = (hidden + mixture).astype(low)[None]
    grad_all = grad_pack_all[:, :full_width]
    grad_reduced_all = grad_pack_all[:, full_width : full_width + rank_columns]
    output_reduced_all = grad_pack_all[:, full_width + rank_columns :]
    grad_mixed_group = dot_t(grad_pack_all[:, : full_width + rank_columns], out_maps).astype(low)
    grad_cols = lax.dynamic_slice_in_dim(grad_all, group_start, group_width, 1)
    grad_upt_output = dot_l(grad_cols, output_reduced_all)
    grad_down_output = dot_l(mixed_group, grad_reduced_all)
    grad_raw_list = attend_back(
        (query_heads, key_heads, value_heads, stat),
        grad_mixed_group,
        raw,
        cosine,
        sine,
        gain_query,
        gain_key,
        segment,
    )
    partial_reduced = jnp.concatenate(
        [dot(grad_raw_list[m], upt_group[m]) for m in range(3)], axis=1
    ).astype(low).reshape(n, own_rows, 3 * rank_columns)
    summed_reduced = collect([partial_reduced[k] for k in range(n)], "seq", n)
    grad_reduced = (jnp.tile(own_mask, (1, 3)) * summed_reduced).astype(low)
    grad_reduced_full = jnp.concatenate(spread(grad_reduced, "seq", n), axis=0)
    partial_normed = qkv_back(grad_raw_list, w_group).reshape(n, own_rows, full_width)
    summed_back = collect([partial_normed[k] for k in range(n)], "seq", n)
    grad_normed = summed_back + dot_t(grad_reduced, down_cat)
    unused_input, pull_input = jax.vjp(lambda values: rms_scale(values, gain_attention), tokens)
    input_grad = (grad_hidden + pull_input(grad_normed)[0]).astype(low)[None]

    grad_upt = [dot_l(grad_raw_list[m], reduced_list[m]) for m in range(3)]
    normed_cols = lax.dynamic_slice_in_dim(normed_all, group_start, group_width, 1)
    grad_down_cat = dot_l(normed_cols, grad_reduced_full)
    parts = [grad_down_cat[:, m * rank_columns : (m + 1) * rank_columns] for m in range(3)]
    parts += [grad_down_output] + grad_upt + [grad_upt_output]
    stacked = jnp.stack([x.astype(low).reshape(dp_count, piece, rank_columns) for x in parts], axis=1)
    own_parts = lax.psum_scatter(stacked, "dp", scatter_dimension=0).astype(f32)
    grad_a_attention = own_parts[0:4]
    grad_b_attention = jnp.swapaxes(own_parts[4:8], 1, 2)

    xs, ps, act_rows, gate_rows, up_rows, reds = kept
    flat = []
    for e in range(local_count):
        red = [reds[e][:, i * rank_columns : (i + 1) * rank_columns] for i in range(6)]
        terms = [
            (reds[e][:, 3 * rank_columns : 5 * rank_columns], xs[e]),
            (red[0], gate_rows[e]),
            (red[1], up_rows[e]),
            (red[5], act_rows[e]),
            (red[2], ps[e]),
        ]
        flat += [dot_l(a, b).astype(low).reshape(-1, rank_columns, b.shape[1]) for a, b in terms]
    widths = [(x.shape[0], x.shape[2] // n) for x in flat]
    flat = jnp.concatenate(
        [
            x.reshape(x.shape[0], rank_columns, n, -1).transpose(2, 0, 1, 3).reshape(n, -1)
            for x in flat
        ],
        axis=1,
    ).reshape(n, -1, rank_columns)
    flat = lax.psum_scatter(flat, "seq", scatter_dimension=0).astype(f32).reshape(-1)
    pieces = []
    start = 0
    for count, width in widths:
        size = count * rank_columns * width
        pieces.append(flat[start : start + size].reshape(count, rank_columns, width))
        start += size
    per = [pieces[5 * e : 5 * e + 5] for e in range(local_count)]
    grad_a_in = jnp.stack([jnp.swapaxes(p[0], 1, 2) for p in per])
    grad_b_in = jnp.stack([jnp.concatenate([p[1], p[2]], axis=0) for p in per])
    grad_a_down = jnp.stack([p[3][0].T for p in per])
    grad_b_down = jnp.stack([p[4][0] for p in per])
    return (
        layer_output,
        input_grad,
        grad_a_attention,
        grad_b_attention,
        grad_a_in,
        grad_b_in,
        grad_a_down,
        grad_b_down,
    )


def solution(mesh):
    return jax.shard_map(
        local,
        mesh=mesh,
        in_specs=(
            P("dp", "seq", None),
            P("dp", "seq", None),
            P(),
            P(),
            P(),
            P(),
            P(None, None, ("seq", "dp")),
            P(("seq", "dp"), None),
            P(None, ("seq", "dp"), None),
            P(None, None, ("seq", "dp")),
            P("dp", None, None, None),
            P("dp", None, None),
            P("dp", None, None, None),
            P("dp", None, None, None),
            P("dp", None, None),
            P("dp", None, None),
            P("dp", "seq", None),
            P("dp", "seq", None),
            P("dp", None),
            P("dp", None),
        ),
        out_specs=(
            P("dp", "seq", None),
            P("dp", "seq", None),
            P(None, ("seq", "dp"), None),
            P(None, None, ("seq", "dp")),
            P("dp", None, "seq", None),
            P("dp", None, None, "seq"),
            P("dp", "seq", None),
            P("dp", None, "seq"),
        ),
        check_vma=False,
    )
```

```python
import functools

import jax
import jax.numpy as jnp
from jax import lax
from jax.experimental import pallas as pl
from jax.experimental.pallas import tpu as pltpu
from jax.sharding import PartitionSpec as P

H = 16
HD = 128
TOP = 8
R = 16


norm_epsilon = 1e-06
rope_base = 10000.0
masked_score = -1000000000.0


def rms_scale(values, gain_vector):
    return (
        values
        * lax.rsqrt(jnp.mean(values * values, axis=-1, keepdims=True) + norm_epsilon)
        * gain_vector
    )


def rope_tables(offset, width):
    half = width // 2
    frequency = rope_base ** (-(jnp.arange(half, dtype=jnp.float32) * 2.0) / width)
    angles = offset.astype(jnp.float32)[:, None] * frequency[None, :]
    cosine = jnp.cos(angles)
    sine = jnp.sin(angles)
    return jnp.concatenate([cosine, cosine], axis=1), jnp.concatenate([-sine, sine], axis=1)


def dot_nn(a, b):
    return lax.dot_general(a, b, (((1,), (0,)), ((), ())), preferred_element_type=jnp.float32)


def dot_nt(a, b):
    return lax.dot_general(a, b, (((1,), (1,)), ((), ())), preferred_element_type=jnp.float32)


def dot_tn(a, b):
    return lax.dot_general(a, b, (((0,), (0,)), ((), ())), preferred_element_type=jnp.float32)


def normed_head(raw, gain):
    inverse = lax.rsqrt(jnp.mean(raw * raw, axis=-1, keepdims=True) + norm_epsilon)
    return raw * inverse * gain, inverse


def turned_head(values, cosine, sine):
    return values * cosine + pltpu.roll(values, values.shape[-1] // 2, 1) * sine


def unturned_head(grad, cosine, sine):
    return grad * cosine + pltpu.roll(grad * sine, grad.shape[-1] // 2, 1)


def attend_kernel(
    tile, q_raw, k_raw, v_raw, cosine, sine, gain_q, gain_k, seg_col, seg_row, mixed, query, key, value, stat
):
    rows = q_raw.shape[0]
    scale = HD ** (-0.5)
    cos_all = cosine[...]
    sin_all = sine[...]
    normed_q, unused = normed_head(q_raw[...], gain_q[...])
    query[...] = turned_head(normed_q, cos_all, sin_all).astype(jnp.bfloat16)
    normed_k, unused = normed_head(k_raw[...], gain_k[...])
    keys = turned_head(normed_k, cos_all, sin_all).astype(jnp.bfloat16)
    key[...] = keys
    values = v_raw[...].astype(jnp.bfloat16)
    value[...] = values
    values_t = values.T
    for start in range(0, rows, tile):
        part = slice(start, start + tile)
        scores = dot_nt(keys, query[part, :]) * scale
        scores = jnp.where(seg_col[...] == seg_row[:, part], scores, masked_score)
        top = jnp.max(scores, axis=0, keepdims=True)
        weight = jnp.exp(scores - top)
        total = jnp.sum(weight, axis=0, keepdims=True)
        soft = (weight * (1.0 / total)).astype(jnp.bfloat16)
        mixed[part, :] = dot_nn(values_t, soft).T.astype(jnp.bfloat16)
        stat[0, :, part] = top + jnp.log(total)


def attend(raw, cosine, sine, gain_q, gain_k, segment):
    unused, length, width = raw.shape
    heads = width // HD
    tile = min(256, length)
    head = pl.BlockSpec((length, HD), lambda h: (0, h))
    raw_head = [pl.BlockSpec((None, length, HD), functools.partial(lambda m, h: (m, 0, h), m)) for m in range(3)]
    fixed = lambda shape: pl.BlockSpec(shape, lambda h: (0, 0))
    seg = segment.astype(jnp.float32)
    low = jax.ShapeDtypeStruct((length, width), jnp.bfloat16)
    return pl.pallas_call(
        functools.partial(attend_kernel, tile),
        grid=(heads,),
        in_specs=raw_head + [fixed((length, HD)), fixed((length, HD)), fixed((1, HD)), fixed((1, HD)),
                  fixed((length, 1)), fixed((1, length))],
        out_specs=[head, head, head, head, pl.BlockSpec((1, 1, length), lambda h: (h, 0, 0))],
        out_shape=[low, low, low, low, jax.ShapeDtypeStruct((heads, 1, length), jnp.float32)],
        cost_estimate=pl.CostEstimate(
            flops=4 * heads * length * length * HD, bytes_accessed=20 * length * width, transcendentals=heads * length * length
        ),
        name="attend",
    )(raw, raw, raw, cosine, sine, gain_q[None, :], gain_k[None, :], seg[:, None], seg[None, :])


def attend_back_kernel(
    tile, query, key, value, grad_mixed, stat, q_raw, k_raw, cosine, sine, gain_q, gain_k, seg_col, seg_row,
    grad_q, grad_k, grad_v, sum_k, sum_v
):
    rows = q_raw.shape[0]
    scale = HD ** (-0.5)
    keys = key[...]
    values = value[...]
    keys_t = keys.T

    def through(grad, raw_ref, gain_ref, part):
        grad = grad.astype(jnp.bfloat16).astype(jnp.float32)
        raw = raw_ref[part, :]
        gain = gain_ref[...]
        inverse = lax.rsqrt(jnp.mean(raw * raw, axis=-1, keepdims=True) + norm_epsilon)
        grad = unturned_head(grad, cosine[part, :], sine[part, :]) * gain
        dots = jnp.mean(grad * raw, axis=-1, keepdims=True)
        return (inverse * (grad - raw * (inverse * inverse * dots))).astype(jnp.bfloat16)

    for start in range(0, rows, tile):
        part = slice(start, start + tile)
        queries = query[part, :]
        grads = grad_mixed[part, :]
        scores = dot_nt(keys, queries) * scale
        scores = jnp.where(seg_col[...] == seg_row[:, part], scores, masked_score)
        soft = jnp.exp(scores - stat[0, :, part])
        grad_soft = dot_nt(values, grads)
        delta = jnp.sum(soft * grad_soft, axis=0, keepdims=True)
        grad_scores = (soft * (grad_soft - delta)).astype(jnp.bfloat16)
        term_k = dot_nn(grad_scores, queries)
        term_v = dot_nn(soft.astype(jnp.bfloat16), grads)
        if start == 0:
            sum_k[...] = term_k
            sum_v[...] = term_v
        else:
            sum_k[...] += term_k
            sum_v[...] += term_v
        grad_q[part, :] = through(dot_nn(keys_t, grad_scores).T * scale, q_raw, gain_q, part)
    for start in range(0, rows, tile):
        part = slice(start, start + tile)
        grad_k[part, :] = through(sum_k[part, :] * scale, k_raw, gain_k, part)
        grad_v[part, :] = sum_v[part, :].astype(jnp.bfloat16)


def attend_back(kept, grad_mixed, raw, cosine, sine, gain_q, gain_k, segment):
    query, key, value, stat = kept
    unused, length, width = raw.shape
    heads = width // HD
    tile = min(256, length)
    head = pl.BlockSpec((length, HD), lambda h: (0, h))
    raw_head = [pl.BlockSpec((None, length, HD), functools.partial(lambda m, h: (m, 0, h), m)) for m in range(3)]
    fixed = lambda shape: pl.BlockSpec(shape, lambda h: (0, 0))
    seg = segment.astype(jnp.float32)
    low = jax.ShapeDtypeStruct((length, width), jnp.bfloat16)
    return pl.pallas_call(
        functools.partial(attend_back_kernel, tile),
        grid=(heads,),
        in_specs=[head, head, head, head, pl.BlockSpec((1, 1, length), lambda h: (h, 0, 0)), raw_head[0], raw_head[1],
                  fixed((length, HD)), fixed((length, HD)), fixed((1, HD)), fixed((1, HD)),
                  fixed((length, 1)), fixed((1, length))],
        out_specs=[head, head, head],
        out_shape=[low, low, low],
        scratch_shapes=[pltpu.VMEM((length, HD), jnp.float32), pltpu.VMEM((length, HD), jnp.float32)],
        cost_estimate=pl.CostEstimate(
            flops=heads * length * HD, bytes_accessed=length * width, transcendentals=0
        ),
        name="attend_back",
    )(query, key, value, grad_mixed, stat, raw, raw, cosine, sine, gain_q[None, :], gain_k[None, :],
      seg[:, None], seg[None, :])


def doc_layout(lengths, chosen, position):
    slots = jnp.arange(lengths.shape[0], dtype=jnp.int32)
    doc_ends = jnp.sum(jnp.where(slots[:, None] >= slots[None, :], lengths[None, :], 0), axis=1)
    starts = doc_ends - lengths
    segment = jnp.sum((position[:, None] >= doc_ends[None, :]).astype(jnp.int32), axis=1)
    doc_pick = (segment[:, None] == slots[None, :]).astype(jnp.int32)
    offset = position - jnp.sum(doc_pick * starts[None, :], axis=1)
    adapter = jnp.sum(doc_pick * chosen[None, :], axis=1)
    return (segment, offset, adapter)


def column_mask(adapter, columns):
    groups = jnp.arange(columns, dtype=jnp.int32) // R
    return (groups[None, :] == adapter[:, None]).astype(jnp.float32)


def qkv_kernel(x_ref, reduced_ref, w_ref, up_ref, out_ref):
    width = w_ref.shape[0] * w_ref.shape[1]
    weights = w_ref[...].reshape(width, x_ref.shape[1])
    out_ref[0] = dot_nt(x_ref[...], weights) + dot_nt(reduced_ref[...], up_ref[0])


def qkv_project(normed_all, reduced_cat, w_group, up_group):
    length, width = normed_all.shape
    dp_count, unused, piece, unused = w_group.shape
    group = dp_count * piece
    rank = up_group.shape[2]
    half = dp_count // 2
    return pl.pallas_call(
        qkv_kernel,
        grid=(3, 2),
        in_specs=[
            pl.BlockSpec((length, width), lambda m, p: (0, 0)),
            pl.BlockSpec((length, rank), lambda m, p: (0, m)),
            pl.BlockSpec((half, None, piece, width), lambda m, p: (p, m, 0, 0)),
            pl.BlockSpec((1, group // 2, rank), lambda m, p: (m, p, 0)),
        ],
        out_specs=pl.BlockSpec((1, length, group // 2), lambda m, p: (m, 0, p)),
        out_shape=jax.ShapeDtypeStruct((3, length, group), jnp.float32),
        cost_estimate=pl.CostEstimate(
            flops=6 * length * width * group, bytes_accessed=2 * length * width + 12 * length * group + 6 * group * width,
            transcendentals=0,
        ),
        name="qkv_project",
    )(normed_all, reduced_cat, w_group, up_group)


def qkv_back_kernel(a_ref, b_ref, c_ref, w_ref, out_ref):
    dp_count, unused, piece, cols = w_ref.shape
    total = None
    for m, ref in enumerate((a_ref, b_ref, c_ref)):
        term = dot_nn(ref[...], w_ref[:, m].reshape(dp_count * piece, cols))
        total = term if total is None else total + term
    out_ref[...] = total.astype(jnp.bfloat16)


def qkv_back(grads, w_group):
    length, group = grads[0].shape
    dp_count, unused, piece, width = w_group.shape
    tile = min(256, width)
    whole = pl.BlockSpec((length, group), lambda i: (0, 0))
    return pl.pallas_call(
        qkv_back_kernel,
        grid=(width // tile,),
        in_specs=[whole, whole, whole, pl.BlockSpec((dp_count, 3, piece, tile), lambda i: (0, 0, 0, i))],
        out_specs=pl.BlockSpec((length, tile), lambda i: (0, i)),
        out_shape=jax.ShapeDtypeStruct((length, width), jnp.bfloat16),
        cost_estimate=pl.CostEstimate(flops=length * width, bytes_accessed=length * width, transcendentals=0),
        name="qkv_back",
    )(grads[0], grads[1], grads[2], w_group)


def expert_kernel(kept_in, *refs):
    (x_a, x_b, g_a, g_b, pick, pick_t, slot, w_in, w_down, a_in, b_in, a_down, b_down) = refs[:13]
    refs = refs[13 + kept_in:]
    (out_a, out_b, back_a, back_b, xs, ps, act_o, gate_o, up_o, reds) = refs[:10]
    (red_g, red_u, gred_d, down_acc, down_red, gx_acc, gred_g, gred_u, sum_out_a, sum_out_b, sum_back_a, sum_back_b) = refs[10:]
    low = jnp.bfloat16
    e = pl.program_id(0)
    f = pl.program_id(1)
    last = pl.num_programs(1) - 1
    cap = pick.shape[2]
    rank = a_in.shape[3]
    rows = xs.shape[1]
    groups = lax.shift_right_logical(lax.broadcasted_iota(jnp.int32, (rows, rank), 1), R.bit_length() - 1)
    mask = jnp.where(groups.astype(jnp.float32) == slot[0, :, 1:2], 1.0, 0.0)

    @pl.when(f == 0)
    def _():
        for b, (x_ref, g_ref) in enumerate(((x_a, g_a), (x_b, g_b))):
            part = slice(b * cap, (b + 1) * cap)
            xs[0, part, :] = dot_nn(pick[0, b], x_ref[...]).astype(low)
            ps[0, part, :] = (slot[0, part, 0:1] * dot_nn(pick[0, b], g_ref[...])).astype(low)
        red_g[...] = (mask * dot_nn(xs[0], a_in[0, 0])).astype(low)
        red_u[...] = (mask * dot_nn(xs[0], a_in[0, 1])).astype(low)
        gred_d[...] = (mask * dot_nt(ps[0], b_down[0])).astype(low)

    x = xs[0]
    p = ps[0]
    gate = dot_nn(x, w_in[0, 0]) + dot_nn(red_g[...], b_in[0, 0])
    up = dot_nn(x, w_in[0, 1]) + dot_nn(red_u[...], b_in[0, 1])
    grad_act = dot_nt(p, w_down[0]) + dot_nt(gred_d[...], a_down[0])
    sigma = 1.0 / (1.0 + jnp.exp(-gate))
    silu = gate * sigma
    act = (silu * up).astype(low)
    grad_gate = (grad_act * up * (sigma * (1.0 + gate * (1.0 - sigma)))).astype(low)
    grad_up = (grad_act * silu).astype(low)
    act_o[0] = act
    gate_o[0] = grad_gate
    up_o[0] = grad_up
    down_term = dot_nn(act, w_down[0])
    down_red_term = dot_nn(act, a_down[0])
    gx_term = dot_nt(grad_gate, w_in[0, 0]) + dot_nt(grad_up, w_in[0, 1])
    gred_g_term = dot_nt(grad_gate, b_in[0, 0])
    gred_u_term = dot_nt(grad_up, b_in[0, 1])

    @pl.when(f == 0)
    def _():
        down_acc[...] = down_term
        down_red[...] = down_red_term
        gx_acc[...] = gx_term
        gred_g[...] = gred_g_term
        gred_u[...] = gred_u_term

    @pl.when(f > 0)
    def _():
        down_acc[...] += down_term
        down_red[...] += down_red_term
        gx_acc[...] += gx_term
        gred_g[...] += gred_g_term
        gred_u[...] += gred_u_term

    @pl.when(f == last)
    def _():
        reduced_d = (mask * down_red[...]).astype(low)
        back_g = (mask * gred_g[...]).astype(low)
        back_u = (mask * gred_u[...]).astype(low)
        for i, value in enumerate((red_g[...], red_u[...], reduced_d, back_g, back_u, gred_d[...])):
            reds[0, :, i * rank : (i + 1) * rank] = value
        produced = down_acc[...] + dot_nn(reduced_d, b_down[0])
        scaled = (slot[0, :, 0:1] * produced).astype(low)
        grads = (gx_acc[...] + dot_nt(back_g, a_in[0, 0]) + dot_nt(back_u, a_in[0, 1])).astype(low)
        for b, (out_ref, out_sum, back_ref, back_sum) in enumerate(
            ((out_a, sum_out_a, back_a, sum_back_a), (out_b, sum_out_b, back_b, sum_back_b))
        ):
            part = slice(b * cap, (b + 1) * cap)
            for values, total, result in ((scaled, out_sum, out_ref), (grads, back_sum, back_ref)):
                term = dot_nn(pick_t[0, b], values[part, :])

                @pl.when(e == 0)
                def _():
                    total[...] = term

                @pl.when(e > 0)
                def _():
                    total[...] += term

                @pl.when(e == pl.num_programs(0) - 1)
                def _():
                    result[...] = total[...].astype(low)


def run_experts(chunk, x_pair, g_pair, pick, pick_t, slot, weights, kept):
    w_in, w_down, a_in, b_in, a_down, b_down = weights
    experts, unused, width, ff = w_in.shape
    unused, dp_count, cap, own_rows = pick.shape
    rank = a_down.shape[2]
    rows = 2 * cap
    tile = min(256, ff)
    low = jnp.bfloat16
    f32 = jnp.float32
    token = pl.BlockSpec((own_rows, width), lambda e, f: (0, 0), pipeline_mode=pl.Buffered(1))
    stored = [
        ((experts, dp_count * cap, width), (1, rows, width), lambda e, f: (e, chunk, 0)),
        ((experts, dp_count * cap, width), (1, rows, width), lambda e, f: (e, chunk, 0)),
        ((experts, dp_count * cap, ff), (1, rows, tile), lambda e, f: (e, chunk, f)),
        ((experts, dp_count * cap, ff), (1, rows, tile), lambda e, f: (e, chunk, f)),
        ((experts, dp_count * cap, ff), (1, rows, tile), lambda e, f: (e, chunk, f)),
        ((experts, dp_count * cap, 6 * rank), (1, rows, 6 * rank), lambda e, f: (e, chunk, 0)),
    ]
    in_specs = [
        token, token, token, token,
        pl.BlockSpec((1, 2, cap, own_rows), lambda e, f: (e, chunk, 0, 0)),
        pl.BlockSpec((1, 2, own_rows, cap), lambda e, f: (e, chunk, 0, 0)),
        pl.BlockSpec((1, rows, 2), lambda e, f: (e, chunk, 0)),
        pl.BlockSpec((1, 2, width, tile), lambda e, f: (e, 0, 0, f)),
        pl.BlockSpec((1, tile, width), lambda e, f: (e, f, 0)),
        pl.BlockSpec((1, 2, width, rank), lambda e, f: (e, 0, 0, 0)),
        pl.BlockSpec((1, 2, rank, tile), lambda e, f: (e, 0, 0, f)),
        pl.BlockSpec((1, tile, rank), lambda e, f: (e, f, 0)),
        pl.BlockSpec((1, rank, width), lambda e, f: (e, 0, 0)),
    ] + [pl.BlockSpec(memory_space=pl.ANY) for unused in kept]
    part = jax.ShapeDtypeStruct((own_rows, width), low)
    results = pl.pallas_call(
        functools.partial(expert_kernel, len(kept)),
        grid=(experts, ff // tile),
        in_specs=in_specs,
        out_specs=[pl.BlockSpec((own_rows, width), lambda e, f: (0, 0), pipeline_mode=pl.Buffered(1))] * 4
        + [pl.BlockSpec(block, index) for unused, block, index in stored],
        out_shape=[part] * 4 + [jax.ShapeDtypeStruct(shape, low) for shape, unused, unused2 in stored],
        scratch_shapes=[
            pltpu.VMEM((rows, rank), low),
            pltpu.VMEM((rows, rank), low),
            pltpu.VMEM((rows, rank), low),
            pltpu.VMEM((rows, width), f32),
            pltpu.VMEM((rows, rank), f32),
            pltpu.VMEM((rows, width), f32),
            pltpu.VMEM((rows, rank), f32),
            pltpu.VMEM((rows, rank), f32),
        ] + [pltpu.VMEM((own_rows, width), f32) for unused in range(4)],
        input_output_aliases={13 + i: 4 + i for i in range(len(kept))},
        cost_estimate=pl.CostEstimate(
            flops=experts * rows * width, bytes_accessed=experts * rows * width, transcendentals=0
        ),
        compiler_params=pltpu.CompilerParams(vmem_limit_bytes=60 * 1024 * 1024),
        name="experts",
    )(*x_pair, *g_pair, pick, pick_t, slot, *weights, *kept)
    return results[:4], results[4:]


def swap(values, axis, distance, count):
    return lax.ppermute(values, axis, [(i, i ^ distance) for i in range(count)])


def spread(values, axis, count):
    return [values] + [swap(values, axis, k, count) for k in range(1, count)]


def collect(blocks, axis, count):
    total = blocks[0].astype(jnp.float32)
    for k in range(1, count):
        total = total + swap(blocks[k], axis, k, count).astype(jnp.float32)
    return total


def pin(*values):
    return lax.optimization_barrier(values)


def local(
    layer_input,
    out_cotangent,
    gain_attention,
    gain_query,
    gain_key,
    gain_ffn,
    w_qkv,
    w_output,
    a_attention,
    b_attention,
    expert_w_in,
    expert_w_down,
    expert_a_in,
    expert_b_in,
    expert_a_down,
    expert_b_down,
    route_experts,
    route_gates,
    doc_lengths,
    adapter_ids,
):
    low = jnp.bfloat16
    f32 = jnp.float32
    own_rows = layer_input.shape[1]
    full_width = layer_input.shape[2]
    n = lax.axis_size("seq")
    dp_count = lax.axis_size("dp")
    s = lax.axis_index("seq")
    d = lax.axis_index("dp")
    length = own_rows * n
    rank_columns = a_attention.shape[2]
    group_width = full_width // n
    group_heads = H // n
    piece = group_width // dp_count
    group_start = s * group_width
    order = s ^ jnp.arange(n, dtype=jnp.int32)
    position = (order[:, None] * own_rows + jnp.arange(own_rows, dtype=jnp.int32)[None, :]).reshape(-1)
    segment, offset, adapter = doc_layout(doc_lengths[0], adapter_ids[0], position)
    own_adapter = adapter[:own_rows]
    own_mask = column_mask(own_adapter, rank_columns)
    full_mask = column_mask(adapter, rank_columns)

    gates = route_gates[0].T
    gates_high = gates.astype(low)
    meta = jnp.concatenate(
        [
            route_experts[0].T.astype(low),
            gates_high,
            (gates - gates_high.astype(f32)).astype(low),
            own_adapter[None, :].astype(low),
            jnp.zeros((7, own_rows), low),
        ],
        axis=0,
    )
    ab_piece = jnp.concatenate([a_attention[0:3], jnp.swapaxes(b_attention, 1, 2)], axis=0).reshape(-1, rank_columns)
    ab_rows = ab_piece.shape[0]
    ab_piece = jnp.concatenate([ab_piece, meta.reshape(-1, rank_columns)], axis=0)
    ab_got = lax.all_gather(ab_piece, "dp", axis=0)
    out_piece = jnp.concatenate([w_output, a_attention[3]], axis=1)
    out_piece, ab_got = pin(out_piece, ab_got)
    dp_order = d ^ jnp.arange(dp_count, dtype=jnp.int32)
    meta_all = ab_got[:, ab_rows:].reshape((dp_count,) + meta.shape)[dp_order].astype(f32)
    ab_group = ab_got[:, :ab_rows].reshape(dp_count, 7, piece, rank_columns)
    ab_group = jnp.swapaxes(ab_group, 0, 1).reshape(7, group_width, rank_columns)
    out_maps = lax.all_gather(out_piece, "dp", axis=0, tiled=True)
    wt_piece = jnp.swapaxes(w_qkv, 1, 2)
    wt_piece, out_maps = pin(wt_piece, out_maps)
    w_group = lax.all_gather(wt_piece, "dp", axis=0)

    local_count = expert_w_in.shape[0]
    expert_count = local_count * dp_count
    capacity = own_rows * TOP // expert_count * 9 // 8
    capacity = -(-capacity // 16) * 16
    named = meta_all[:, 0:TOP, :].astype(jnp.int32)
    gates_all = meta_all[:, TOP : 2 * TOP, :] + meta_all[:, 2 * TOP : 3 * TOP, :]
    sets_all = meta_all[:, 3 * TOP, :]
    mine = d * local_count + jnp.arange(local_count, dtype=jnp.int32)
    hit = (named[None] == mine[:, None, None, None]).astype(f32)
    member = jnp.sum(hit, axis=2)
    token_gate = jnp.sum(hit * gates_all[None], axis=2)
    t_index = jnp.arange(own_rows, dtype=jnp.int32)
    upto = (t_index[:, None] <= t_index[None, :]).astype(low)
    rank = jnp.einsum("ejt,tu->eju", member.astype(low), upto, preferred_element_type=f32) - 1.0
    slots = jnp.arange(capacity, dtype=jnp.int32).astype(f32)
    rank = jnp.where(member > 0.5, rank, -1.0)
    pick = slots[None, None, :, None] == rank[:, :, None, :]
    pick_t = (rank[:, :, :, None] == slots[None, None, None, :]).astype(low)
    slot_gate = jnp.sum(jnp.where(pick, token_gate[:, :, None, :], 0.0), axis=-1)
    slot_set = jnp.sum(jnp.where(pick, sets_all[None, :, None, :], 0.0), axis=-1)
    slot = jnp.stack([slot_gate, slot_set], axis=-1).reshape(local_count, dp_count * capacity, 2)
    pick = pick.astype(low)

    cosine, sine = rope_tables(offset, HD)
    tokens = layer_input[0].astype(f32)
    normed = rms_scale(tokens, gain_attention).astype(low)
    normed_blocks = spread(normed, "seq", n)
    share = jnp.concatenate([ab_group[0:3], ab_group[6:7]], axis=0)
    share_blocks = spread(share, "seq", n)
    grad_send, w_group, pick, pick_t, slot, cosine, sine, *early = pin(
        out_cotangent[0], w_group, pick, pick_t, slot, cosine, sine, *normed_blocks, *share_blocks
    )
    grad_got = lax.all_gather(grad_send, "dp", axis=0)
    grad_blocks = [lax.dynamic_index_in_dim(grad_got, dp_order[k], 0, keepdims=False) for k in range(dp_count)]
    normed_all = jnp.concatenate(early[:n], axis=0)
    share_blocks = jnp.stack(early[n:])
    share_full = share_blocks[order]
    share_full = jnp.swapaxes(share_full, 0, 1).reshape(4, full_width, rank_columns)
    down_cat = jnp.swapaxes(share_full[0:3], 0, 1).reshape(full_width, 3 * rank_columns)
    upt_output = share_full[3]
    upt_group = ab_group[3:6]

    dot = lambda a, b: jnp.dot(a, b, preferred_element_type=f32)
    dot_t = lambda a, b: lax.dot_general(a, b, (((1,), (1,)), ((), ())), preferred_element_type=f32)
    dot_l = lambda a, b: lax.dot_general(a, b, (((0,), (0,)), ((), ())), preferred_element_type=f32)

    reduced_cat = (jnp.tile(full_mask, (1, 3)) * dot(normed_all, down_cat)).astype(low)
    reduced_list = [reduced_cat[:, m * rank_columns : (m + 1) * rank_columns] for m in range(3)]
    raw = qkv_project(normed_all, reduced_cat, w_group, upt_group)
    mixed_group, query_heads, key_heads, value_heads, stat = attend(
        raw, cosine, sine, gain_query, gain_key, segment
    )

    partial_out = dot(mixed_group, out_maps).astype(low).reshape(n, own_rows, full_width + rank_columns)
    summed = collect([partial_out[k] for k in range(n)], "seq", n)
    output_reduced = (own_mask * summed[:, full_width:]).astype(low)
    attended = summed[:, :full_width] + dot_t(output_reduced, upt_output)
    hidden = tokens + attended
    normed_ffn = rms_scale(hidden, gain_ffn).astype(low)
    weights = (expert_w_in, expert_w_down, expert_a_in, expert_b_in, expert_a_down, expert_b_down)
    chips = dp_count // 2
    turns = [0] + list(range(chips // 2, chips)) + list(range(1, chips // 2))
    outs = [None] * dp_count
    kept = ()
    rows = normed_ffn
    here = normed_ffn
    arrived = swap(rows, "dp", 2 * turns[1], dp_count)
    other = swap(here, "dp", 1, dp_count)
    leaving = None
    flying = None
    grad_normed_ffn = None
    for i, c in enumerate(turns):
        if i > 0:
            here = arrived
            if flying is not None:
                here, flying = pin(here, flying)
                grad_normed_ffn = grad_normed_ffn + flying.astype(f32)
            other = swap(here, "dp", 1, dp_count)
            rows, here, other, leaving = pin(rows, here, other, leaving)
            if i < chips - 1:
                arrived = swap(rows, "dp", 2 * turns[i + 1], dp_count)
            if i == 1:
                grad_normed_ffn = leaving
            else:
                flying = swap(leaving, "dp", 2 * turns[i - 1], dp_count)
        (outs[2 * c], outs[2 * c + 1], back, back_other), kept = run_experts(
            c, (here, other), grad_blocks[2 * c : 2 * c + 2], pick, pick_t, slot, weights, kept
        )
        if i == chips - 1 and flying is not None:
            flying, back_other = pin(flying, back_other)
        leaving = back.astype(f32) + swap(back_other, "dp", 1, dp_count).astype(f32)
        if i > 0:
            leaving = leaving.astype(low)
    if flying is not None:
        grad_normed_ffn = grad_normed_ffn + flying.astype(f32)
    leaving, *kept = pin(leaving, *kept)
    flying = swap(leaving, "dp", 2 * turns[-1], dp_count)
    flying, *kept_later = pin(flying, *kept)
    grad_normed_ffn = grad_normed_ffn + flying.astype(f32)

    outs_all = jnp.stack(outs)[dp_order]
    outs_all, grad_normed_ffn = pin(outs_all, grad_normed_ffn)
    mixture = lax.psum_scatter(outs_all, "dp", scatter_dimension=0)
    grad_out = out_cotangent[0].astype(f32)
    unused, pull_ffn = jax.vjp(lambda values: rms_scale(values, gain_ffn), hidden)
    grad_hidden = grad_out + pull_ffn(grad_normed_ffn)[0]
    grad_hidden_low = grad_hidden.astype(low)
    grad_reduced_output = (own_mask * dot(grad_hidden_low, upt_output)).astype(low)
    grad_pack = jnp.concatenate([grad_hidden_low, grad_reduced_output, output_reduced], axis=1)
    flat = []
    for e in range(local_count):
        xs, ps, act_rows, gate_rows, up_rows, reds = kept if e == 0 else kept_later
        red = [reds[e][:, i * rank_columns : (i + 1) * rank_columns] for i in range(6)]
        terms = [
            (reds[e][:, 3 * rank_columns : 5 * rank_columns], xs[e]),
            (red[0], gate_rows[e]),
            (red[1], up_rows[e]),
            (red[5], act_rows[e]),
            (red[2], ps[e]),
        ]
        flat += [dot_l(a, b).astype(low).reshape(-1, rank_columns, b.shape[1]) for a, b in terms]
    widths = [(x.shape[0], x.shape[2] // n) for x in flat]
    flat = jnp.concatenate(
        [
            x.reshape(x.shape[0], rank_columns, n, -1).transpose(2, 0, 1, 3).reshape(n, -1)
            for x in flat
        ],
        axis=1,
    ).reshape(n, -1, rank_columns)
    grad_packs = spread(grad_pack, "seq", n)
    flat, *grad_packs = pin(flat, *grad_packs)
    expert_terms = [lax.dynamic_index_in_dim(flat, order[k], 0, keepdims=False) for k in range(n)]
    expert_terms = expert_terms[:1] + [swap(expert_terms[k], "seq", k, n) for k in range(1, n)]
    grad_pack_all = jnp.concatenate(grad_packs, axis=0)
    grad_all = grad_pack_all[:, :full_width]
    grad_reduced_all = grad_pack_all[:, full_width : full_width + rank_columns]
    output_reduced_all = grad_pack_all[:, full_width + rank_columns :]
    grad_mixed_group = dot_t(grad_pack_all[:, : full_width + rank_columns], out_maps).astype(low)
    grad_cols = lax.dynamic_slice_in_dim(grad_all, group_start, group_width, 1)
    grad_upt_output = dot_l(grad_cols, output_reduced_all)
    grad_down_output = dot_l(mixed_group, grad_reduced_all)
    grad_raw_list = attend_back(
        (query_heads, key_heads, value_heads, stat),
        grad_mixed_group,
        raw,
        cosine,
        sine,
        gain_query,
        gain_key,
        segment,
    )
    expert_terms[-1], *grad_raw_list = pin(expert_terms[-1], *grad_raw_list)
    partial_reduced = jnp.concatenate(
        [dot(grad_raw_list[m], upt_group[m]) for m in range(3)], axis=1
    ).astype(low).reshape(n, own_rows, 3 * rank_columns)
    summed_reduced = collect([partial_reduced[k] for k in range(n)], "seq", n)
    grad_reduced = (jnp.tile(own_mask, (1, 3)) * summed_reduced).astype(low)
    grad_reduced_full = jnp.concatenate(spread(grad_reduced, "seq", n), axis=0)
    partial_normed = qkv_back(grad_raw_list, w_group).reshape(n, own_rows, full_width)
    partial_normed, *expert_terms = pin(partial_normed, *expert_terms)
    summed_back = collect([partial_normed[k] for k in range(n)], "seq", n)
    summed_back, mixture, hidden = pin(summed_back, mixture, hidden)
    layer_output = (hidden + mixture.astype(f32)).astype(low)[None]
    grad_normed = summed_back + dot_t(grad_reduced, down_cat)
    unused_input, pull_input = jax.vjp(lambda values: rms_scale(values, gain_attention), tokens)
    input_grad = (grad_hidden + pull_input(grad_normed)[0]).astype(low)[None]

    grad_upt = [dot_l(grad_raw_list[m], reduced_list[m]) for m in range(3)]
    normed_cols = lax.dynamic_slice_in_dim(normed_all, group_start, group_width, 1)
    grad_down_cat = dot_l(normed_cols, grad_reduced_full)
    parts = [grad_down_cat[:, m * rank_columns : (m + 1) * rank_columns] for m in range(3)]
    parts += [grad_down_output] + grad_upt + [grad_upt_output]
    stacked = jnp.stack([x.astype(low).reshape(dp_count, piece, rank_columns) for x in parts], axis=1)
    own_parts = lax.psum_scatter(stacked, "dp", scatter_dimension=0)
    own_parts, input_grad = pin(own_parts, input_grad)
    own_parts = own_parts.astype(f32)
    grad_a_attention = own_parts[0:4]
    grad_b_attention = jnp.swapaxes(own_parts[4:8], 1, 2)

    flat = sum(x.astype(f32) for x in expert_terms).reshape(-1)
    pieces = []
    start = 0
    for count, width in widths:
        size = count * rank_columns * width
        pieces.append(flat[start : start + size].reshape(count, rank_columns, width))
        start += size
    per = [pieces[5 * e : 5 * e + 5] for e in range(local_count)]
    grad_a_in = jnp.stack([jnp.swapaxes(p[0], 1, 2) for p in per])
    grad_b_in = jnp.stack([jnp.concatenate([p[1], p[2]], axis=0) for p in per])
    grad_a_down = jnp.stack([p[3][0].T for p in per])
    grad_b_down = jnp.stack([p[4][0] for p in per])
    return (
        layer_output,
        input_grad,
        grad_a_attention,
        grad_b_attention,
        grad_a_in,
        grad_b_in,
        grad_a_down,
        grad_b_down,
    )


def solution(mesh):
    return jax.shard_map(
        local,
        mesh=mesh,
        in_specs=(
            P("dp", "seq", None),
            P("dp", "seq", None),
            P(),
            P(),
            P(),
            P(),
            P(None, None, ("seq", "dp")),
            P(("seq", "dp"), None),
            P(None, ("seq", "dp"), None),
            P(None, None, ("seq", "dp")),
            P("dp", None, None, None),
            P("dp", None, None),
            P("dp", None, None, None),
            P("dp", None, None, None),
            P("dp", None, None),
            P("dp", None, None),
            P("dp", "seq", None),
            P("dp", "seq", None),
            P("dp", None),
            P("dp", None),
        ),
        out_specs=(
            P("dp", "seq", None),
            P("dp", "seq", None),
            P(None, ("seq", "dp"), None),
            P(None, None, ("seq", "dp")),
            P("dp", None, "seq", None),
            P("dp", None, None, "seq"),
            P("dp", "seq", None),
            P("dp", None, "seq"),
        ),
        check_vma=False,
    )
```

```python
import functools

import jax
import jax.numpy as jnp
from jax import lax
from jax.experimental import pallas as pl
from jax.experimental.pallas import tpu as pltpu
from jax.sharding import PartitionSpec as P

H = 16
HD = 128
TOP = 8
R = 16


norm_epsilon = 1e-06
rope_base = 10000.0
masked_score = -1000000000.0
half_from = 200000


def rms_scale(values, gain_vector):
    return (
        values
        * lax.rsqrt(jnp.mean(values * values, axis=-1, keepdims=True) + norm_epsilon)
        * gain_vector
    )


def rope_tables(offset, width):
    half = width // 2
    frequency = rope_base ** (-(jnp.arange(half, dtype=jnp.float32) * 2.0) / width)
    angles = offset.astype(jnp.float32)[:, None] * frequency[None, :]
    cosine = jnp.cos(angles)
    sine = jnp.sin(angles)
    return jnp.concatenate([cosine, cosine], axis=1), jnp.concatenate([-sine, sine], axis=1)


def dot_nn(a, b):
    return lax.dot_general(a, b, (((1,), (0,)), ((), ())), preferred_element_type=jnp.float32)


def dot_nt(a, b):
    return lax.dot_general(a, b, (((1,), (1,)), ((), ())), preferred_element_type=jnp.float32)


def dot_tn(a, b):
    return lax.dot_general(a, b, (((0,), (0,)), ((), ())), preferred_element_type=jnp.float32)


def normed_head(raw, gain):
    inverse = lax.rsqrt(jnp.mean(raw * raw, axis=-1, keepdims=True) + norm_epsilon)
    return raw * inverse * gain, inverse


def turned_head(values, cosine, sine):
    return values * cosine + pltpu.roll(values, values.shape[-1] // 2, 1) * sine


def unturned_head(grad, cosine, sine):
    return grad * cosine + pltpu.roll(grad * sine, grad.shape[-1] // 2, 1)


def attend_kernel(
    tile, q_raw, k_raw, v_raw, cosine, sine, gain_q, gain_k, seg_col, seg_row, mixed, query, key, value, stat
):
    rows = q_raw.shape[0]
    scale = HD ** (-0.5)
    cos_all = cosine[...]
    sin_all = sine[...]
    normed_q, unused = normed_head(q_raw[...], gain_q[...])
    query[...] = turned_head(normed_q, cos_all, sin_all).astype(jnp.bfloat16)
    normed_k, unused = normed_head(k_raw[...], gain_k[...])
    keys = turned_head(normed_k, cos_all, sin_all).astype(jnp.bfloat16)
    key[...] = keys
    values = v_raw[...].astype(jnp.bfloat16)
    value[...] = values
    values_t = values.T
    for start in range(0, rows, tile):
        part = slice(start, start + tile)
        scores = dot_nt(keys, query[part, :]) * scale
        scores = jnp.where(seg_col[...] == seg_row[:, part], scores, masked_score)
        top = jnp.max(scores, axis=0, keepdims=True)
        weight = jnp.exp(scores - top)
        total = jnp.sum(weight, axis=0, keepdims=True)
        soft = (weight * (1.0 / total)).astype(jnp.bfloat16)
        mixed[part, :] = dot_nn(values_t, soft).T.astype(jnp.bfloat16)
        stat[0, :, part] = top + jnp.log(total)


def attend(raw, cosine, sine, gain_q, gain_k, segment):
    unused, length, width = raw.shape
    heads = width // HD
    tile = min(256, length)
    head = pl.BlockSpec((length, HD), lambda h: (0, h))
    raw_head = [pl.BlockSpec((None, length, HD), functools.partial(lambda m, h: (m, 0, h), m)) for m in range(3)]
    fixed = lambda shape: pl.BlockSpec(shape, lambda h: (0, 0))
    seg = segment.astype(jnp.float32)
    low = jax.ShapeDtypeStruct((length, width), jnp.bfloat16)
    return pl.pallas_call(
        functools.partial(attend_kernel, tile),
        grid=(heads,),
        in_specs=raw_head + [fixed((length, HD)), fixed((length, HD)), fixed((1, HD)), fixed((1, HD)),
                  fixed((length, 1)), fixed((1, length))],
        out_specs=[head, head, head, head, pl.BlockSpec((1, 1, length), lambda h: (h, 0, 0))],
        out_shape=[low, low, low, low, jax.ShapeDtypeStruct((heads, 1, length), jnp.float32)],
        cost_estimate=pl.CostEstimate(
            flops=4 * heads * length * length * HD, bytes_accessed=20 * length * width, transcendentals=heads * length * length
        ),
        name="attend",
    )(raw, raw, raw, cosine, sine, gain_q[None, :], gain_k[None, :], seg[:, None], seg[None, :])


def attend_back_kernel(
    tile, query, key, value, grad_mixed, stat, q_raw, k_raw, cosine, sine, gain_q, gain_k, seg_col, seg_row,
    grad_q, grad_k, grad_v, sum_k, sum_v
):
    rows = q_raw.shape[0]
    scale = HD ** (-0.5)
    keys = key[...]
    values = value[...]
    keys_t = keys.T

    def through(grad, raw_ref, gain_ref, part):
        grad = grad.astype(jnp.bfloat16).astype(jnp.float32)
        raw = raw_ref[part, :]
        gain = gain_ref[...]
        inverse = lax.rsqrt(jnp.mean(raw * raw, axis=-1, keepdims=True) + norm_epsilon)
        grad = unturned_head(grad, cosine[part, :], sine[part, :]) * gain
        dots = jnp.mean(grad * raw, axis=-1, keepdims=True)
        return (inverse * (grad - raw * (inverse * inverse * dots))).astype(jnp.bfloat16)

    for start in range(0, rows, tile):
        part = slice(start, start + tile)
        queries = query[part, :]
        grads = grad_mixed[part, :]
        scores = dot_nt(keys, queries) * scale
        scores = jnp.where(seg_col[...] == seg_row[:, part], scores, masked_score)
        soft = jnp.exp(scores - stat[0, :, part])
        grad_soft = dot_nt(values, grads)
        delta = jnp.sum(soft * grad_soft, axis=0, keepdims=True)
        grad_scores = (soft * (grad_soft - delta)).astype(jnp.bfloat16)
        term_k = dot_nn(grad_scores, queries)
        term_v = dot_nn(soft.astype(jnp.bfloat16), grads)
        if start == 0:
            sum_k[...] = term_k
            sum_v[...] = term_v
        else:
            sum_k[...] += term_k
            sum_v[...] += term_v
        grad_q[part, :] = through(dot_nn(keys_t, grad_scores).T * scale, q_raw, gain_q, part)
    for start in range(0, rows, tile):
        part = slice(start, start + tile)
        grad_k[part, :] = through(sum_k[part, :] * scale, k_raw, gain_k, part)
        grad_v[part, :] = sum_v[part, :].astype(jnp.bfloat16)


def attend_back(kept, grad_mixed, raw, cosine, sine, gain_q, gain_k, segment):
    query, key, value, stat = kept
    unused, length, width = raw.shape
    heads = width // HD
    tile = min(256, length)
    head = pl.BlockSpec((length, HD), lambda h: (0, h))
    raw_head = [pl.BlockSpec((None, length, HD), functools.partial(lambda m, h: (m, 0, h), m)) for m in range(3)]
    fixed = lambda shape: pl.BlockSpec(shape, lambda h: (0, 0))
    seg = segment.astype(jnp.float32)
    low = jax.ShapeDtypeStruct((length, width), jnp.bfloat16)
    return pl.pallas_call(
        functools.partial(attend_back_kernel, tile),
        grid=(heads,),
        in_specs=[head, head, head, head, pl.BlockSpec((1, 1, length), lambda h: (h, 0, 0)), raw_head[0], raw_head[1],
                  fixed((length, HD)), fixed((length, HD)), fixed((1, HD)), fixed((1, HD)),
                  fixed((length, 1)), fixed((1, length))],
        out_specs=[head, head, head],
        out_shape=[low, low, low],
        scratch_shapes=[pltpu.VMEM((length, HD), jnp.float32), pltpu.VMEM((length, HD), jnp.float32)],
        cost_estimate=pl.CostEstimate(
            flops=heads * length * HD, bytes_accessed=length * width, transcendentals=0
        ),
        name="attend_back",
    )(query, key, value, grad_mixed, stat, raw, raw, cosine, sine, gain_q[None, :], gain_k[None, :],
      seg[:, None], seg[None, :])


def doc_layout(lengths, chosen, position):
    slots = jnp.arange(lengths.shape[0], dtype=jnp.int32)
    doc_ends = jnp.sum(jnp.where(slots[:, None] >= slots[None, :], lengths[None, :], 0), axis=1)
    starts = doc_ends - lengths
    segment = jnp.sum((position[:, None] >= doc_ends[None, :]).astype(jnp.int32), axis=1)
    doc_pick = (segment[:, None] == slots[None, :]).astype(jnp.int32)
    offset = position - jnp.sum(doc_pick * starts[None, :], axis=1)
    adapter = jnp.sum(doc_pick * chosen[None, :], axis=1)
    return (segment, offset, adapter)


def column_mask(adapter, columns):
    groups = jnp.arange(columns, dtype=jnp.int32) // R
    return (groups[None, :] == adapter[:, None]).astype(jnp.float32)


def qkv_kernel(x_ref, reduced_ref, w_ref, up_ref, out_ref):
    width = w_ref.shape[0] * w_ref.shape[1]
    weights = w_ref[...].reshape(width, x_ref.shape[1])
    out_ref[0] = dot_nt(x_ref[...], weights) + dot_nt(reduced_ref[...], up_ref[0])


def qkv_project(normed_all, reduced_cat, w_group, up_group):
    length, width = normed_all.shape
    dp_count, unused, piece, unused = w_group.shape
    group = dp_count * piece
    rank = up_group.shape[2]
    half = dp_count // 2
    return pl.pallas_call(
        qkv_kernel,
        grid=(3, 2),
        in_specs=[
            pl.BlockSpec((length, width), lambda m, p: (0, 0)),
            pl.BlockSpec((length, rank), lambda m, p: (0, m)),
            pl.BlockSpec((half, None, piece, width), lambda m, p: (p, m, 0, 0)),
            pl.BlockSpec((1, group // 2, rank), lambda m, p: (m, p, 0)),
        ],
        out_specs=pl.BlockSpec((1, length, group // 2), lambda m, p: (m, 0, p)),
        out_shape=jax.ShapeDtypeStruct((3, length, group), jnp.float32),
        cost_estimate=pl.CostEstimate(
            flops=6 * length * width * group, bytes_accessed=2 * length * width + 12 * length * group + 6 * group * width,
            transcendentals=0,
        ),
        name="qkv_project",
    )(normed_all, reduced_cat, w_group, up_group)


def qkv_back_kernel(a_ref, b_ref, c_ref, w_ref, out_ref):
    dp_count, unused, piece, cols = w_ref.shape
    total = None
    for m, ref in enumerate((a_ref, b_ref, c_ref)):
        term = dot_nn(ref[...], w_ref[:, m].reshape(dp_count * piece, cols))
        total = term if total is None else total + term
    out_ref[...] = total.astype(jnp.bfloat16)


def qkv_back(grads, w_group):
    length, group = grads[0].shape
    dp_count, unused, piece, width = w_group.shape
    tile = min(256, width)
    whole = pl.BlockSpec((length, group), lambda i: (0, 0))
    return pl.pallas_call(
        qkv_back_kernel,
        grid=(width // tile,),
        in_specs=[whole, whole, whole, pl.BlockSpec((dp_count, 3, piece, tile), lambda i: (0, 0, 0, i))],
        out_specs=pl.BlockSpec((length, tile), lambda i: (0, i)),
        out_shape=jax.ShapeDtypeStruct((length, width), jnp.bfloat16),
        cost_estimate=pl.CostEstimate(flops=length * width, bytes_accessed=length * width, transcendentals=0),
        name="qkv_back",
    )(grads[0], grads[1], grads[2], w_group)


def expert_kernel(kept_in, *refs):
    (x_a, x_b, g_a, g_b, pick, pick_t, slot, w_in, w_down, a_in, b_in, a_down, b_down) = refs[:13]
    refs = refs[13 + kept_in:]
    (out_a, out_b, back_a, back_b, xs, ps, act_o, gate_o, up_o, reds) = refs[:10]
    (red_g, red_u, gred_d, down_acc, down_red, gx_acc, gred_g, gred_u, sum_out_a, sum_out_b, sum_back_a, sum_back_b) = refs[10:]
    low = jnp.bfloat16
    e = pl.program_id(0)
    f = pl.program_id(1)
    last = pl.num_programs(1) - 1
    cap = pick.shape[2]
    rank = a_in.shape[3]
    rows = xs.shape[1]
    groups = lax.shift_right_logical(lax.broadcasted_iota(jnp.int32, (rows, rank), 1), R.bit_length() - 1)
    mask = jnp.where(groups.astype(jnp.float32) == slot[0, :, 1:2], 1.0, 0.0)

    @pl.when(f == 0)
    def _():
        for b, (x_ref, g_ref) in enumerate(((x_a, g_a), (x_b, g_b))):
            part = slice(b * cap, (b + 1) * cap)
            xs[0, part, :] = dot_nn(pick[0, b], x_ref[...]).astype(low)
            ps[0, part, :] = (slot[0, part, 0:1] * dot_nn(pick[0, b], g_ref[...])).astype(low)
        red_g[...] = (mask * dot_nn(xs[0], a_in[0, 0])).astype(low)
        red_u[...] = (mask * dot_nn(xs[0], a_in[0, 1])).astype(low)
        gred_d[...] = (mask * dot_nt(ps[0], b_down[0])).astype(low)

    x = xs[0]
    p = ps[0]
    gate = dot_nn(x, w_in[0, 0]) + dot_nn(red_g[...], b_in[0, 0])
    up = dot_nn(x, w_in[0, 1]) + dot_nn(red_u[...], b_in[0, 1])
    grad_act = dot_nt(p, w_down[0]) + dot_nt(gred_d[...], a_down[0])
    sigma = 1.0 / (1.0 + jnp.exp(-gate))
    silu = gate * sigma
    act = (silu * up).astype(low)
    grad_gate = (grad_act * up * (sigma * (1.0 + gate * (1.0 - sigma)))).astype(low)
    grad_up = (grad_act * silu).astype(low)
    act_o[0] = act
    gate_o[0] = grad_gate
    up_o[0] = grad_up
    down_term = dot_nn(act, w_down[0])
    down_red_term = dot_nn(act, a_down[0])
    gx_term = dot_nt(grad_gate, w_in[0, 0]) + dot_nt(grad_up, w_in[0, 1])
    gred_g_term = dot_nt(grad_gate, b_in[0, 0])
    gred_u_term = dot_nt(grad_up, b_in[0, 1])

    @pl.when(f == 0)
    def _():
        down_acc[...] = down_term
        down_red[...] = down_red_term
        gx_acc[...] = gx_term
        gred_g[...] = gred_g_term
        gred_u[...] = gred_u_term

    @pl.when(f > 0)
    def _():
        down_acc[...] += down_term
        down_red[...] += down_red_term
        gx_acc[...] += gx_term
        gred_g[...] += gred_g_term
        gred_u[...] += gred_u_term

    @pl.when(f == last)
    def _():
        reduced_d = (mask * down_red[...]).astype(low)
        back_g = (mask * gred_g[...]).astype(low)
        back_u = (mask * gred_u[...]).astype(low)
        for i, value in enumerate((red_g[...], red_u[...], reduced_d, back_g, back_u, gred_d[...])):
            reds[0, :, i * rank : (i + 1) * rank] = value
        produced = down_acc[...] + dot_nn(reduced_d, b_down[0])
        scaled = (slot[0, :, 0:1] * produced).astype(low)
        grads = (gx_acc[...] + dot_nt(back_g, a_in[0, 0]) + dot_nt(back_u, a_in[0, 1])).astype(low)
        for b, (out_ref, out_sum, back_ref, back_sum) in enumerate(
            ((out_a, sum_out_a, back_a, sum_back_a), (out_b, sum_out_b, back_b, sum_back_b))
        ):
            part = slice(b * cap, (b + 1) * cap)
            for values, total, result in ((scaled, out_sum, out_ref), (grads, back_sum, back_ref)):
                term = dot_nn(pick_t[0, b], values[part, :])

                @pl.when(e == 0)
                def _():
                    total[...] = term

                @pl.when(e > 0)
                def _():
                    total[...] += term

                @pl.when(e == pl.num_programs(0) - 1)
                def _():
                    result[...] = total[...].astype(low)


def run_experts(chunk, x_pair, g_pair, pick, pick_t, slot, weights, kept):
    w_in, w_down, a_in, b_in, a_down, b_down = weights
    experts, unused, width, ff = w_in.shape
    unused, dp_count, cap, own_rows = pick.shape
    rank = a_down.shape[2]
    rows = 2 * cap
    tile = min(256, ff)
    low = jnp.bfloat16
    f32 = jnp.float32
    token = pl.BlockSpec((own_rows, width), lambda e, f: (0, 0), pipeline_mode=pl.Buffered(1))
    stored = [
        ((experts, dp_count * cap, width), (1, rows, width), lambda e, f: (e, chunk, 0)),
        ((experts, dp_count * cap, width), (1, rows, width), lambda e, f: (e, chunk, 0)),
        ((experts, dp_count * cap, ff), (1, rows, tile), lambda e, f: (e, chunk, f)),
        ((experts, dp_count * cap, ff), (1, rows, tile), lambda e, f: (e, chunk, f)),
        ((experts, dp_count * cap, ff), (1, rows, tile), lambda e, f: (e, chunk, f)),
        ((experts, dp_count * cap, 6 * rank), (1, rows, 6 * rank), lambda e, f: (e, chunk, 0)),
    ]
    in_specs = [
        token, token, token, token,
        pl.BlockSpec((1, 2, cap, own_rows), lambda e, f: (e, chunk, 0, 0)),
        pl.BlockSpec((1, 2, own_rows, cap), lambda e, f: (e, chunk, 0, 0)),
        pl.BlockSpec((1, rows, 2), lambda e, f: (e, chunk, 0)),
        pl.BlockSpec((1, 2, width, tile), lambda e, f: (e, 0, 0, f)),
        pl.BlockSpec((1, tile, width), lambda e, f: (e, f, 0)),
        pl.BlockSpec((1, 2, width, rank), lambda e, f: (e, 0, 0, 0)),
        pl.BlockSpec((1, 2, rank, tile), lambda e, f: (e, 0, 0, f)),
        pl.BlockSpec((1, tile, rank), lambda e, f: (e, f, 0)),
        pl.BlockSpec((1, rank, width), lambda e, f: (e, 0, 0)),
    ] + [pl.BlockSpec(memory_space=pl.ANY) for unused in kept]
    part = jax.ShapeDtypeStruct((own_rows, width), low)
    results = pl.pallas_call(
        functools.partial(expert_kernel, len(kept)),
        grid=(experts, ff // tile),
        in_specs=in_specs,
        out_specs=[pl.BlockSpec((own_rows, width), lambda e, f: (0, 0), pipeline_mode=pl.Buffered(1))] * 4
        + [pl.BlockSpec(block, index) for unused, block, index in stored],
        out_shape=[part] * 4 + [jax.ShapeDtypeStruct(shape, low) for shape, unused, unused2 in stored],
        scratch_shapes=[
            pltpu.VMEM((rows, rank), low),
            pltpu.VMEM((rows, rank), low),
            pltpu.VMEM((rows, rank), low),
            pltpu.VMEM((rows, width), f32),
            pltpu.VMEM((rows, rank), f32),
            pltpu.VMEM((rows, width), f32),
            pltpu.VMEM((rows, rank), f32),
            pltpu.VMEM((rows, rank), f32),
        ] + [pltpu.VMEM((own_rows, width), f32) for unused in range(4)],
        input_output_aliases={13 + i: 4 + i for i in range(len(kept))},
        cost_estimate=pl.CostEstimate(
            flops=experts * rows * width, bytes_accessed=experts * rows * width, transcendentals=0
        ),
        compiler_params=pltpu.CompilerParams(vmem_limit_bytes=60 * 1024 * 1024),
        name="experts",
    )(*x_pair, *g_pair, pick, pick_t, slot, *weights, *kept)
    return results[:4], results[4:]


def swap(values, axis, distance, count):
    return lax.ppermute(values, axis, [(i, i ^ distance) for i in range(count)])


def near(values, axis, count):
    return [swap(values, axis, 1, count), swap(values, axis, 2, count)]


def spread(values, axis, count, close=None):
    one, two = near(values, axis, count) if close is None else close
    if count == 4 and values.size >= half_from:
        half = values.shape[0] // 2
        three = [swap(two[:half], axis, 1, count), swap(one[half:], axis, 2, count)]
        return [values, one, two, jnp.concatenate(three, axis=0)]
    return [values, one, two] + [swap(values, axis, k, count) for k in range(3, count)]


def collect(blocks, axis, count):
    f32 = jnp.float32
    if count == 4 and blocks[0].size >= half_from:
        half = blocks[0].shape[0] // 2
        over_one = swap(blocks[3][:half], axis, 1, count)
        over_two = swap(blocks[3][half:], axis, 2, count)
        top = blocks[0][:half].astype(f32) + swap(blocks[1][:half], axis, 1, count).astype(f32)
        low = blocks[0][half:].astype(f32) + swap(blocks[2][half:], axis, 2, count).astype(f32)
        to_two = (blocks[2][:half].astype(f32) + over_one.astype(f32)).astype(blocks[2].dtype)
        to_one = (blocks[1][half:].astype(f32) + over_two.astype(f32)).astype(blocks[1].dtype)
        to_two, to_one = pin(to_two, to_one)
        top = top + swap(to_two, axis, 2, count).astype(f32)
        low = low + swap(to_one, axis, 1, count).astype(f32)
        return jnp.concatenate([top, low], axis=0)
    total = blocks[0].astype(f32)
    for k in range(1, count):
        total = total + swap(blocks[k], axis, k, count).astype(f32)
    return total


def pin(*values):
    return lax.optimization_barrier(values)


def local(
    layer_input,
    out_cotangent,
    gain_attention,
    gain_query,
    gain_key,
    gain_ffn,
    w_qkv,
    w_output,
    a_attention,
    b_attention,
    expert_w_in,
    expert_w_down,
    expert_a_in,
    expert_b_in,
    expert_a_down,
    expert_b_down,
    route_experts,
    route_gates,
    doc_lengths,
    adapter_ids,
):
    low = jnp.bfloat16
    f32 = jnp.float32
    own_rows = layer_input.shape[1]
    full_width = layer_input.shape[2]
    n = lax.axis_size("seq")
    dp_count = lax.axis_size("dp")
    s = lax.axis_index("seq")
    d = lax.axis_index("dp")
    length = own_rows * n
    rank_columns = a_attention.shape[2]
    group_width = full_width // n
    group_heads = H // n
    piece = group_width // dp_count
    group_start = s * group_width
    order = s ^ jnp.arange(n, dtype=jnp.int32)
    position = (order[:, None] * own_rows + jnp.arange(own_rows, dtype=jnp.int32)[None, :]).reshape(-1)
    segment, offset, adapter = doc_layout(doc_lengths[0], adapter_ids[0], position)
    own_adapter = adapter[:own_rows]
    own_mask = column_mask(own_adapter, rank_columns)
    full_mask = column_mask(adapter, rank_columns)

    gates = route_gates[0].T
    gates_high = gates.astype(low)
    meta = jnp.concatenate(
        [
            route_experts[0].T.astype(low),
            gates_high,
            (gates - gates_high.astype(f32)).astype(low),
            own_adapter[None, :].astype(low),
            jnp.zeros((7, own_rows), low),
        ],
        axis=0,
    )
    ab_piece = jnp.concatenate([a_attention[0:3], jnp.swapaxes(b_attention, 1, 2)], axis=0).reshape(-1, rank_columns)
    ab_rows = ab_piece.shape[0]
    ab_piece = jnp.concatenate([ab_piece, meta.reshape(-1, rank_columns)], axis=0)
    ab_got = lax.all_gather(ab_piece, "dp", axis=0)
    tokens = layer_input[0].astype(f32)
    normed = rms_scale(tokens, gain_attention).astype(low)
    wt_piece = jnp.swapaxes(w_qkv, 1, 2)
    wt_piece, ab_got, *close = pin(wt_piece, ab_got, *near(normed, "seq", n))
    w_group = lax.all_gather(wt_piece, "dp", axis=0)
    dp_order = d ^ jnp.arange(dp_count, dtype=jnp.int32)
    meta_all = ab_got[:, ab_rows:].reshape((dp_count,) + meta.shape)[dp_order].astype(f32)
    ab_group = ab_got[:, :ab_rows].reshape(dp_count, 7, piece, rank_columns)
    ab_group = jnp.swapaxes(ab_group, 0, 1).reshape(7, group_width, rank_columns)
    local_count = expert_w_in.shape[0]
    expert_count = local_count * dp_count
    capacity = own_rows * TOP // expert_count * 9 // 8
    capacity = -(-capacity // 16) * 16
    named = meta_all[:, 0:TOP, :].astype(jnp.int32)
    gates_all = meta_all[:, TOP : 2 * TOP, :] + meta_all[:, 2 * TOP : 3 * TOP, :]
    sets_all = meta_all[:, 3 * TOP, :]
    mine = d * local_count + jnp.arange(local_count, dtype=jnp.int32)
    hit = (named[None] == mine[:, None, None, None]).astype(f32)
    member = jnp.sum(hit, axis=2)
    token_gate = jnp.sum(hit * gates_all[None], axis=2)
    t_index = jnp.arange(own_rows, dtype=jnp.int32)
    upto = (t_index[:, None] <= t_index[None, :]).astype(low)
    rank = jnp.einsum("ejt,tu->eju", member.astype(low), upto, preferred_element_type=f32) - 1.0
    slots = jnp.arange(capacity, dtype=jnp.int32).astype(f32)
    rank = jnp.where(member > 0.5, rank, -1.0)
    pick = slots[None, None, :, None] == rank[:, :, None, :]
    pick_t = (rank[:, :, :, None] == slots[None, None, None, :]).astype(low)
    slot_gate = jnp.sum(jnp.where(pick, token_gate[:, :, None, :], 0.0), axis=-1)
    slot_set = jnp.sum(jnp.where(pick, sets_all[None, :, None, :], 0.0), axis=-1)
    slot = jnp.stack([slot_gate, slot_set], axis=-1).reshape(local_count, dp_count * capacity, 2)
    pick = pick.astype(low)

    cosine, sine = rope_tables(offset, HD)

    dot = lambda a, b: jnp.dot(a, b, preferred_element_type=f32)
    dot_t = lambda a, b: lax.dot_general(a, b, (((1,), (1,)), ((), ())), preferred_element_type=f32)
    dot_l = lambda a, b: lax.dot_general(a, b, (((0,), (0,)), ((), ())), preferred_element_type=f32)

    share = jnp.concatenate([ab_group[0:3], ab_group[6:7]], axis=0)
    share_full = jnp.stack(spread(share, "seq", n))[order]
    share_full = jnp.swapaxes(share_full, 0, 1).reshape(4, full_width, rank_columns)
    down_cat = jnp.swapaxes(share_full[0:3], 0, 1).reshape(full_width, 3 * rank_columns)
    upt_output = share_full[3]
    upt_group = ab_group[3:6]
    normed_all = jnp.concatenate(spread(normed, "seq", n, close), axis=0)
    reduced_cat = (jnp.tile(full_mask, (1, 3)) * dot(normed_all, down_cat)).astype(low)
    out_piece = jnp.concatenate([w_output, a_attention[3]], axis=1)
    out_piece, w_group, pick, pick_t, slot, cosine, sine, normed_all, reduced_cat, upt_group, upt_output = pin(
        out_piece, w_group, pick, pick_t, slot, cosine, sine, normed_all, reduced_cat, upt_group, upt_output
    )
    out_maps = lax.all_gather(out_piece, "dp", axis=0, tiled=True)
    reduced_list = [reduced_cat[:, m * rank_columns : (m + 1) * rank_columns] for m in range(3)]
    raw = qkv_project(normed_all, reduced_cat, w_group, upt_group)
    grad_send, raw = pin(out_cotangent[0], raw)
    grad_got = lax.all_gather(grad_send, "dp", axis=0)
    grad_own = [out_cotangent[0], swap(out_cotangent[0], "dp", 1, dp_count)]
    grad_blocks = grad_own + [
        lax.dynamic_index_in_dim(grad_got, dp_order[k], 0, keepdims=False) for k in range(2, dp_count)
    ]
    mixed_group, query_heads, key_heads, value_heads, stat = attend(
        raw, cosine, sine, gain_query, gain_key, segment
    )

    partial_out = dot(mixed_group, out_maps).astype(low).reshape(n, own_rows, full_width + rank_columns)
    summed = collect([partial_out[k] for k in range(n)], "seq", n)
    output_reduced = (own_mask * summed[:, full_width:]).astype(low)
    attended = summed[:, :full_width] + dot_t(output_reduced, upt_output)
    hidden = tokens + attended
    normed_ffn = rms_scale(hidden, gain_ffn).astype(low)
    weights = (expert_w_in, expert_w_down, expert_a_in, expert_b_in, expert_a_down, expert_b_down)
    chips = dp_count // 2
    turns = [0] + list(range(chips // 2, chips)) + list(range(1, chips // 2))
    outs = [None] * dp_count
    kept = ()
    rows = normed_ffn
    here = normed_ffn
    arrived = swap(rows, "dp", 2 * turns[1], dp_count)
    other = swap(here, "dp", 1, dp_count)
    leaving = None
    flying = None
    grad_normed_ffn = None
    for i, c in enumerate(turns):
        if i > 0:
            here = arrived
            if flying is not None:
                here, flying = pin(here, flying)
                grad_normed_ffn = grad_normed_ffn + flying.astype(f32)
            other = swap(here, "dp", 1, dp_count)
            rows, here, other, leaving = pin(rows, here, other, leaving)
            if i < chips - 1:
                arrived = swap(rows, "dp", 2 * turns[i + 1], dp_count)
            if i == 1:
                grad_normed_ffn = leaving
            else:
                flying = swap(leaving, "dp", 2 * turns[i - 1], dp_count)
        (outs[2 * c], outs[2 * c + 1], back, back_other), kept = run_experts(
            c, (here, other), grad_blocks[2 * c : 2 * c + 2], pick, pick_t, slot, weights, kept
        )
        if i == chips - 1 and flying is not None:
            flying, back_other = pin(flying, back_other)
        leaving = back.astype(f32) + swap(back_other, "dp", 1, dp_count).astype(f32)
        if i > 0:
            leaving = leaving.astype(low)
    if flying is not None:
        grad_normed_ffn = grad_normed_ffn + flying.astype(f32)
    leaving, *kept = pin(leaving, *kept)
    flying = swap(leaving, "dp", 2 * turns[-1], dp_count)
    flying, *kept_later = pin(flying, *kept)
    grad_normed_ffn = grad_normed_ffn + flying.astype(f32)

    outs_all = jnp.stack(outs)[dp_order]
    outs_all, grad_normed_ffn = pin(outs_all, grad_normed_ffn)
    mixture = lax.psum_scatter(outs_all, "dp", scatter_dimension=0)
    grad_out = out_cotangent[0].astype(f32)
    unused, pull_ffn = jax.vjp(lambda values: rms_scale(values, gain_ffn), hidden)
    grad_hidden = grad_out + pull_ffn(grad_normed_ffn)[0]
    grad_hidden_low = grad_hidden.astype(low)
    grad_reduced_output = (own_mask * dot(grad_hidden_low, upt_output)).astype(low)
    grad_pack = jnp.concatenate([grad_hidden_low, grad_reduced_output, output_reduced], axis=1)
    flat = []
    for e in range(local_count):
        xs, ps, act_rows, gate_rows, up_rows, reds = kept if e == 0 else kept_later
        red = [reds[e][:, i * rank_columns : (i + 1) * rank_columns] for i in range(6)]
        terms = [
            (reds[e][:, 3 * rank_columns : 5 * rank_columns], xs[e]),
            (red[0], gate_rows[e]),
            (red[1], up_rows[e]),
            (red[5], act_rows[e]),
            (red[2], ps[e]),
        ]
        flat += [dot_l(a, b).astype(low).reshape(-1, rank_columns, b.shape[1]) for a, b in terms]
    widths = [(x.shape[0], x.shape[2] // n) for x in flat]
    flat = jnp.concatenate(
        [
            x.reshape(x.shape[0], rank_columns, n, -1).transpose(2, 0, 1, 3).reshape(n, -1)
            for x in flat
        ],
        axis=1,
    ).reshape(n, -1, rank_columns)
    grad_packs = spread(grad_pack, "seq", n)
    flat, *grad_packs = pin(flat, *grad_packs)
    expert_terms = [lax.dynamic_index_in_dim(flat, order[k], 0, keepdims=False) for k in range(n)]
    expert_sum = collect(expert_terms, "seq", n)
    grad_pack_all = jnp.concatenate(grad_packs, axis=0)
    grad_all = grad_pack_all[:, :full_width]
    grad_reduced_all = grad_pack_all[:, full_width : full_width + rank_columns]
    output_reduced_all = grad_pack_all[:, full_width + rank_columns :]
    grad_mixed_group = dot_t(grad_pack_all[:, : full_width + rank_columns], out_maps).astype(low)
    grad_cols = lax.dynamic_slice_in_dim(grad_all, group_start, group_width, 1)
    grad_upt_output = dot_l(grad_cols, output_reduced_all)
    grad_down_output = dot_l(mixed_group, grad_reduced_all)
    grad_raw_list = attend_back(
        (query_heads, key_heads, value_heads, stat),
        grad_mixed_group,
        raw,
        cosine,
        sine,
        gain_query,
        gain_key,
        segment,
    )
    expert_sum, *grad_raw_list = pin(expert_sum, *grad_raw_list)
    partial_reduced = jnp.concatenate(
        [dot(grad_raw_list[m], upt_group[m]) for m in range(3)], axis=1
    ).astype(low)
    partial_reduced, *grad_raw_list = pin(partial_reduced, *grad_raw_list)
    partial_reduced = partial_reduced.reshape(n, own_rows, 3 * rank_columns)
    summed_reduced = collect([partial_reduced[k] for k in range(n)], "seq", n)
    grad_reduced = (jnp.tile(own_mask, (1, 3)) * summed_reduced).astype(low)
    grad_reduced_full = jnp.concatenate(spread(grad_reduced, "seq", n), axis=0)
    partial_normed = qkv_back(grad_raw_list, w_group).reshape(n, own_rows, full_width)
    partial_normed, grad_reduced_full = pin(partial_normed, grad_reduced_full)
    summed_back = collect([partial_normed[k] for k in range(n)], "seq", n)
    summed_back, mixture, hidden = pin(summed_back, mixture, hidden)
    layer_output = (hidden + mixture.astype(f32)).astype(low)[None]
    grad_normed = summed_back + dot_t(grad_reduced, down_cat)
    unused_input, pull_input = jax.vjp(lambda values: rms_scale(values, gain_attention), tokens)
    input_grad = (grad_hidden + pull_input(grad_normed)[0]).astype(low)[None]

    grad_upt = [dot_l(grad_raw_list[m], reduced_list[m]) for m in range(3)]
    normed_cols = lax.dynamic_slice_in_dim(normed_all, group_start, group_width, 1)
    grad_down_cat = dot_l(normed_cols, grad_reduced_full)
    parts = [grad_down_cat[:, m * rank_columns : (m + 1) * rank_columns] for m in range(3)]
    parts += [grad_down_output] + grad_upt + [grad_upt_output]
    stacked = jnp.stack([x.astype(low).reshape(dp_count, piece, rank_columns) for x in parts], axis=1)
    own_parts = lax.psum_scatter(stacked, "dp", scatter_dimension=0)
    own_parts, input_grad = pin(own_parts, input_grad)
    own_parts = own_parts.astype(f32)
    grad_a_attention = own_parts[0:4]
    grad_b_attention = jnp.swapaxes(own_parts[4:8], 1, 2)

    flat = expert_sum.reshape(-1)
    pieces = []
    start = 0
    for count, width in widths:
        size = count * rank_columns * width
        pieces.append(flat[start : start + size].reshape(count, rank_columns, width))
        start += size
    per = [pieces[5 * e : 5 * e + 5] for e in range(local_count)]
    grad_a_in = jnp.stack([jnp.swapaxes(p[0], 1, 2) for p in per])
    grad_b_in = jnp.stack([jnp.concatenate([p[1], p[2]], axis=0) for p in per])
    grad_a_down = jnp.stack([p[3][0].T for p in per])
    grad_b_down = jnp.stack([p[4][0] for p in per])
    return (
        layer_output,
        input_grad,
        grad_a_attention,
        grad_b_attention,
        grad_a_in,
        grad_b_in,
        grad_a_down,
        grad_b_down,
    )


def solution(mesh):
    return jax.shard_map(
        local,
        mesh=mesh,
        in_specs=(
            P("dp", "seq", None),
            P("dp", "seq", None),
            P(),
            P(),
            P(),
            P(),
            P(None, None, ("seq", "dp")),
            P(("seq", "dp"), None),
            P(None, ("seq", "dp"), None),
            P(None, None, ("seq", "dp")),
            P("dp", None, None, None),
            P("dp", None, None),
            P("dp", None, None, None),
            P("dp", None, None, None),
            P("dp", None, None),
            P("dp", None, None),
            P("dp", "seq", None),
            P("dp", "seq", None),
            P("dp", None),
            P("dp", None),
        ),
        out_specs=(
            P("dp", "seq", None),
            P("dp", "seq", None),
            P(None, ("seq", "dp"), None),
            P(None, None, ("seq", "dp")),
            P("dp", None, "seq", None),
            P("dp", None, None, "seq"),
            P("dp", "seq", None),
            P("dp", None, "seq"),
        ),
        check_vma=False,
    )
```

```python
import functools

import jax
import jax.numpy as jnp
from jax import lax
from jax.experimental import pallas as pl
from jax.experimental.pallas import tpu as pltpu
from jax.sharding import PartitionSpec as P

H = 16
HD = 128
TOP = 8
R = 16


norm_epsilon = 1e-06
rope_base = 10000.0
masked_score = -1000000000.0
half_from = 200000


def rms_scale(values, gain_vector):
    return (
        values
        * lax.rsqrt(jnp.mean(values * values, axis=-1, keepdims=True) + norm_epsilon)
        * gain_vector
    )


def rope_tables(offset, width):
    half = width // 2
    frequency = rope_base ** (-(jnp.arange(half, dtype=jnp.float32) * 2.0) / width)
    angles = offset.astype(jnp.float32)[:, None] * frequency[None, :]
    cosine = jnp.cos(angles)
    sine = jnp.sin(angles)
    return jnp.concatenate([cosine, cosine], axis=1), jnp.concatenate([-sine, sine], axis=1)


def dot_nn(a, b):
    return lax.dot_general(a, b, (((1,), (0,)), ((), ())), preferred_element_type=jnp.float32)


def dot_nt(a, b):
    return lax.dot_general(a, b, (((1,), (1,)), ((), ())), preferred_element_type=jnp.float32)


def dot_tn(a, b):
    return lax.dot_general(a, b, (((0,), (0,)), ((), ())), preferred_element_type=jnp.float32)


def normed_head(raw, gain):
    inverse = lax.rsqrt(jnp.mean(raw * raw, axis=-1, keepdims=True) + norm_epsilon)
    return raw * inverse * gain, inverse


def turned_head(values, cosine, sine):
    return values * cosine + pltpu.roll(values, values.shape[-1] // 2, 1) * sine


def unturned_head(grad, cosine, sine):
    return grad * cosine + pltpu.roll(grad * sine, grad.shape[-1] // 2, 1)


def attend_kernel(
    tile, q_raw, k_raw, v_raw, cosine, sine, gain_q, gain_k, seg_col, seg_row, mixed, query, key, value, stat
):
    rows = q_raw.shape[0]
    scale = HD ** (-0.5)
    cos_all = cosine[...]
    sin_all = sine[...]
    normed_q, unused = normed_head(q_raw[...], gain_q[...])
    query[...] = turned_head(normed_q, cos_all, sin_all).astype(jnp.bfloat16)
    normed_k, unused = normed_head(k_raw[...], gain_k[...])
    keys = turned_head(normed_k, cos_all, sin_all).astype(jnp.bfloat16)
    key[...] = keys
    values = v_raw[...].astype(jnp.bfloat16)
    value[...] = values
    values_t = values.T
    for start in range(0, rows, tile):
        part = slice(start, start + tile)
        scores = dot_nt(keys, query[part, :]) * scale
        scores = jnp.where(seg_col[...] == seg_row[:, part], scores, masked_score)
        top = jnp.max(scores, axis=0, keepdims=True)
        weight = jnp.exp(scores - top)
        total = jnp.sum(weight, axis=0, keepdims=True)
        soft = (weight * (1.0 / total)).astype(jnp.bfloat16)
        mixed[part, :] = dot_nn(values_t, soft).T.astype(jnp.bfloat16)
        stat[0, :, part] = top + jnp.log(total)


def attend(raw, cosine, sine, gain_q, gain_k, segment):
    unused, length, width = raw.shape
    heads = width // HD
    tile = min(256, length)
    head = pl.BlockSpec((length, HD), lambda h: (0, h))
    raw_head = [pl.BlockSpec((None, length, HD), functools.partial(lambda m, h: (m, 0, h), m)) for m in range(3)]
    fixed = lambda shape: pl.BlockSpec(shape, lambda h: (0, 0))
    seg = segment.astype(jnp.float32)
    low = jax.ShapeDtypeStruct((length, width), jnp.bfloat16)
    return pl.pallas_call(
        functools.partial(attend_kernel, tile),
        grid=(heads,),
        in_specs=raw_head + [fixed((length, HD)), fixed((length, HD)), fixed((1, HD)), fixed((1, HD)),
                  fixed((length, 1)), fixed((1, length))],
        out_specs=[head, head, head, head, pl.BlockSpec((1, 1, length), lambda h: (h, 0, 0))],
        out_shape=[low, low, low, low, jax.ShapeDtypeStruct((heads, 1, length), jnp.float32)],
        cost_estimate=pl.CostEstimate(
            flops=4 * heads * length * length * HD, bytes_accessed=20 * length * width, transcendentals=heads * length * length
        ),
        name="attend",
    )(raw, raw, raw, cosine, sine, gain_q[None, :], gain_k[None, :], seg[:, None], seg[None, :])


def attend_back_kernel(
    tile, query, key, value, grad_mixed, stat, q_raw, k_raw, cosine, sine, gain_q, gain_k, seg_col, seg_row,
    grad_q, grad_k, grad_v, sum_k, sum_v
):
    rows = q_raw.shape[0]
    scale = HD ** (-0.5)
    keys = key[...]
    values = value[...]
    keys_t = keys.T

    def through(grad, raw_ref, gain_ref, part):
        grad = grad.astype(jnp.bfloat16).astype(jnp.float32)
        raw = raw_ref[part, :]
        gain = gain_ref[...]
        inverse = lax.rsqrt(jnp.mean(raw * raw, axis=-1, keepdims=True) + norm_epsilon)
        grad = unturned_head(grad, cosine[part, :], sine[part, :]) * gain
        dots = jnp.mean(grad * raw, axis=-1, keepdims=True)
        return (inverse * (grad - raw * (inverse * inverse * dots))).astype(jnp.bfloat16)

    for start in range(0, rows, tile):
        part = slice(start, start + tile)
        queries = query[part, :]
        grads = grad_mixed[part, :]
        scores = dot_nt(keys, queries) * scale
        scores = jnp.where(seg_col[...] == seg_row[:, part], scores, masked_score)
        soft = jnp.exp(scores - stat[0, :, part])
        grad_soft = dot_nt(values, grads)
        delta = jnp.sum(soft * grad_soft, axis=0, keepdims=True)
        grad_scores = (soft * (grad_soft - delta)).astype(jnp.bfloat16)
        term_k = dot_nn(grad_scores, queries)
        term_v = dot_nn(soft.astype(jnp.bfloat16), grads)
        if start == 0:
            sum_k[...] = term_k
            sum_v[...] = term_v
        else:
            sum_k[...] += term_k
            sum_v[...] += term_v
        grad_q[part, :] = through(dot_nn(keys_t, grad_scores).T * scale, q_raw, gain_q, part)
    for start in range(0, rows, tile):
        part = slice(start, start + tile)
        grad_k[part, :] = through(sum_k[part, :] * scale, k_raw, gain_k, part)
        grad_v[part, :] = sum_v[part, :].astype(jnp.bfloat16)


def attend_back(kept, grad_mixed, raw, cosine, sine, gain_q, gain_k, segment):
    query, key, value, stat = kept
    unused, length, width = raw.shape
    heads = width // HD
    tile = min(256, length)
    head = pl.BlockSpec((length, HD), lambda h: (0, h))
    raw_head = [pl.BlockSpec((None, length, HD), functools.partial(lambda m, h: (m, 0, h), m)) for m in range(3)]
    fixed = lambda shape: pl.BlockSpec(shape, lambda h: (0, 0))
    seg = segment.astype(jnp.float32)
    low = jax.ShapeDtypeStruct((length, width), jnp.bfloat16)
    return pl.pallas_call(
        functools.partial(attend_back_kernel, tile),
        grid=(heads,),
        in_specs=[head, head, head, head, pl.BlockSpec((1, 1, length), lambda h: (h, 0, 0)), raw_head[0], raw_head[1],
                  fixed((length, HD)), fixed((length, HD)), fixed((1, HD)), fixed((1, HD)),
                  fixed((length, 1)), fixed((1, length))],
        out_specs=[head, head, head],
        out_shape=[low, low, low],
        scratch_shapes=[pltpu.VMEM((length, HD), jnp.float32), pltpu.VMEM((length, HD), jnp.float32)],
        cost_estimate=pl.CostEstimate(
            flops=heads * length * HD, bytes_accessed=length * width, transcendentals=0
        ),
        name="attend_back",
    )(query, key, value, grad_mixed, stat, raw, raw, cosine, sine, gain_q[None, :], gain_k[None, :],
      seg[:, None], seg[None, :])


def doc_layout(lengths, chosen, position):
    slots = jnp.arange(lengths.shape[0], dtype=jnp.int32)
    doc_ends = jnp.sum(jnp.where(slots[:, None] >= slots[None, :], lengths[None, :], 0), axis=1)
    starts = doc_ends - lengths
    segment = jnp.sum((position[:, None] >= doc_ends[None, :]).astype(jnp.int32), axis=1)
    doc_pick = (segment[:, None] == slots[None, :]).astype(jnp.int32)
    offset = position - jnp.sum(doc_pick * starts[None, :], axis=1)
    adapter = jnp.sum(doc_pick * chosen[None, :], axis=1)
    return (segment, offset, adapter)


def column_mask(adapter, columns):
    groups = jnp.arange(columns, dtype=jnp.int32) // R
    return (groups[None, :] == adapter[:, None]).astype(jnp.float32)


def qkv_kernel(x_ref, reduced_ref, w_ref, up_ref, out_ref):
    width = w_ref.shape[0] * w_ref.shape[1]
    weights = w_ref[...].reshape(width, x_ref.shape[1])
    out_ref[0] = dot_nt(x_ref[...], weights) + dot_nt(reduced_ref[...], up_ref[0])


def qkv_project(normed_all, reduced_cat, w_group, up_group):
    length, width = normed_all.shape
    dp_count, unused, piece, unused = w_group.shape
    group = dp_count * piece
    rank = up_group.shape[2]
    half = dp_count // 2
    return pl.pallas_call(
        qkv_kernel,
        grid=(3, 2),
        in_specs=[
            pl.BlockSpec((length, width), lambda m, p: (0, 0)),
            pl.BlockSpec((length, rank), lambda m, p: (0, m)),
            pl.BlockSpec((half, None, piece, width), lambda m, p: (p, m, 0, 0)),
            pl.BlockSpec((1, group // 2, rank), lambda m, p: (m, p, 0)),
        ],
        out_specs=pl.BlockSpec((1, length, group // 2), lambda m, p: (m, 0, p)),
        out_shape=jax.ShapeDtypeStruct((3, length, group), jnp.float32),
        cost_estimate=pl.CostEstimate(
            flops=6 * length * width * group, bytes_accessed=2 * length * width + 12 * length * group + 6 * group * width,
            transcendentals=0,
        ),
        name="qkv_project",
    )(normed_all, reduced_cat, w_group, up_group)


def qkv_back_kernel(a_ref, b_ref, c_ref, w_ref, out_ref):
    dp_count, unused, piece, cols = w_ref.shape
    total = None
    for m, ref in enumerate((a_ref, b_ref, c_ref)):
        term = dot_nn(ref[...], w_ref[:, m].reshape(dp_count * piece, cols))
        total = term if total is None else total + term
    out_ref[...] = total.astype(jnp.bfloat16)


def qkv_back(grads, w_group):
    length, group = grads[0].shape
    dp_count, unused, piece, width = w_group.shape
    tile = min(256, width)
    whole = pl.BlockSpec((length, group), lambda i: (0, 0))
    return pl.pallas_call(
        qkv_back_kernel,
        grid=(width // tile,),
        in_specs=[whole, whole, whole, pl.BlockSpec((dp_count, 3, piece, tile), lambda i: (0, 0, 0, i))],
        out_specs=pl.BlockSpec((length, tile), lambda i: (0, i)),
        out_shape=jax.ShapeDtypeStruct((length, width), jnp.bfloat16),
        cost_estimate=pl.CostEstimate(flops=length * width, bytes_accessed=length * width, transcendentals=0),
        name="qkv_back",
    )(grads[0], grads[1], grads[2], w_group)


def expert_kernel(kept_in, which, *refs):
    (x_a, x_b, g_both, pick, pick_t, slot, w_in, w_down, a_in, b_in, a_down, b_down) = refs[:12]
    refs = refs[12 + kept_in:]
    (out_both, back_a, back_b, xs, ps, act_o, gate_o, up_o, reds) = refs[:9]
    (red_g, red_u, gred_d, down_acc, down_red, gx_acc, gred_g, gred_u, sum_out_a, sum_out_b, sum_back_a, sum_back_b) = refs[9:]
    low = jnp.bfloat16
    e = pl.program_id(0)
    f = pl.program_id(1)
    last = pl.num_programs(1) - 1
    cap = pick.shape[2]
    rank = a_in.shape[3]
    rows = xs.shape[1]
    groups = lax.shift_right_logical(lax.broadcasted_iota(jnp.int32, (rows, rank), 1), R.bit_length() - 1)
    mask = jnp.where(groups.astype(jnp.float32) == slot[0, :, 1:2], 1.0, 0.0)

    @pl.when(f == 0)
    def _():
        for b, x_ref in enumerate((x_a, x_b)):
            part = slice(b * cap, (b + 1) * cap)
            g_place = which[1] if b == 0 else 1 - which[1]
            xs[0, part, :] = dot_nn(pick[0, b], x_ref[...]).astype(low)
            ps[0, part, :] = (slot[0, part, 0:1] * dot_nn(pick[0, b], g_both[g_place])).astype(low)
        red_g[...] = (mask * dot_nn(xs[0], a_in[0, 0])).astype(low)
        red_u[...] = (mask * dot_nn(xs[0], a_in[0, 1])).astype(low)
        gred_d[...] = (mask * dot_nt(ps[0], b_down[0])).astype(low)

    x = xs[0]
    p = ps[0]
    gate = dot_nn(x, w_in[0, 0]) + dot_nn(red_g[...], b_in[0, 0])
    up = dot_nn(x, w_in[0, 1]) + dot_nn(red_u[...], b_in[0, 1])
    grad_act = dot_nt(p, w_down[0]) + dot_nt(gred_d[...], a_down[0])
    sigma = 1.0 / (1.0 + jnp.exp(-gate))
    silu = gate * sigma
    act = (silu * up).astype(low)
    grad_gate = (grad_act * up * (sigma * (1.0 + gate * (1.0 - sigma)))).astype(low)
    grad_up = (grad_act * silu).astype(low)
    act_o[0] = act
    gate_o[0] = grad_gate
    up_o[0] = grad_up
    down_term = dot_nn(act, w_down[0])
    down_red_term = dot_nn(act, a_down[0])
    gx_term = dot_nt(grad_gate, w_in[0, 0]) + dot_nt(grad_up, w_in[0, 1])
    gred_g_term = dot_nt(grad_gate, b_in[0, 0])
    gred_u_term = dot_nt(grad_up, b_in[0, 1])

    @pl.when(f == 0)
    def _():
        down_acc[...] = down_term
        down_red[...] = down_red_term
        gx_acc[...] = gx_term
        gred_g[...] = gred_g_term
        gred_u[...] = gred_u_term

    @pl.when(f > 0)
    def _():
        down_acc[...] += down_term
        down_red[...] += down_red_term
        gx_acc[...] += gx_term
        gred_g[...] += gred_g_term
        gred_u[...] += gred_u_term

    @pl.when(f == last)
    def _():
        reduced_d = (mask * down_red[...]).astype(low)
        back_g = (mask * gred_g[...]).astype(low)
        back_u = (mask * gred_u[...]).astype(low)
        for i, value in enumerate((red_g[...], red_u[...], reduced_d, back_g, back_u, gred_d[...])):
            reds[0, :, i * rank : (i + 1) * rank] = value
        produced = down_acc[...] + dot_nn(reduced_d, b_down[0])
        scaled = (slot[0, :, 0:1] * produced).astype(low)
        grads = (gx_acc[...] + dot_nt(back_g, a_in[0, 0]) + dot_nt(back_u, a_in[0, 1])).astype(low)
        for b, (out_sum, back_ref, back_sum) in enumerate(
            ((sum_out_a, back_a, sum_back_a), (sum_out_b, back_b, sum_back_b))
        ):
            part = slice(b * cap, (b + 1) * cap)
            out_ref = out_both.at[which[3] if b == 0 else 1 - which[3]]
            for values, total, result in ((scaled, out_sum, out_ref), (grads, back_sum, back_ref)):
                term = dot_nn(pick_t[0, b], values[part, :])

                @pl.when(e == 0)
                def _():
                    total[...] = term

                @pl.when(e > 0)
                def _():
                    total[...] += term

                @pl.when(e == pl.num_programs(0) - 1)
                def _():
                    result[...] = total[...].astype(low)


def run_experts(chunk, which, x_pair, g_all, pick, pick_t, slot, weights, kept):
    w_in, w_down, a_in, b_in, a_down, b_down = weights
    experts, unused, width, ff = w_in.shape
    unused, dp_count, cap, own_rows = pick.shape
    rank = a_down.shape[2]
    rows = 2 * cap
    tile = min(256, ff)
    low = jnp.bfloat16
    f32 = jnp.float32
    one = pl.Buffered(1)
    token = pl.BlockSpec((own_rows, width), lambda e, f, w: (0, 0), pipeline_mode=one)
    stored = [
        ((experts, dp_count * cap, width), (1, rows, width), lambda e, f, w: (e, chunk, 0)),
        ((experts, dp_count * cap, width), (1, rows, width), lambda e, f, w: (e, chunk, 0)),
        ((experts, dp_count * cap, ff), (1, rows, tile), lambda e, f, w: (e, chunk, f)),
        ((experts, dp_count * cap, ff), (1, rows, tile), lambda e, f, w: (e, chunk, f)),
        ((experts, dp_count * cap, ff), (1, rows, tile), lambda e, f, w: (e, chunk, f)),
        ((experts, dp_count * cap, 6 * rank), (1, rows, 6 * rank), lambda e, f, w: (e, chunk, 0)),
    ]
    in_specs = [
        token, token, pl.BlockSpec((2, own_rows, width), lambda e, f, w: (w[0], 0, 0), pipeline_mode=one),
        pl.BlockSpec((1, 2, cap, own_rows), lambda e, f, w: (e, chunk, 0, 0)),
        pl.BlockSpec((1, 2, own_rows, cap), lambda e, f, w: (e, chunk, 0, 0)),
        pl.BlockSpec((1, rows, 2), lambda e, f, w: (e, chunk, 0)),
        pl.BlockSpec((1, 2, width, tile), lambda e, f, w: (e, 0, 0, f)),
        pl.BlockSpec((1, tile, width), lambda e, f, w: (e, f, 0)),
        pl.BlockSpec((1, 2, width, rank), lambda e, f, w: (e, 0, 0, 0)),
        pl.BlockSpec((1, 2, rank, tile), lambda e, f, w: (e, 0, 0, f)),
        pl.BlockSpec((1, tile, rank), lambda e, f, w: (e, f, 0)),
        pl.BlockSpec((1, rank, width), lambda e, f, w: (e, 0, 0)),
    ] + [pl.BlockSpec(memory_space=pl.ANY) for unused in kept]
    part = jax.ShapeDtypeStruct((own_rows, width), low)
    results = pl.pallas_call(
        functools.partial(expert_kernel, len(kept)),
        grid_spec=pltpu.PrefetchScalarGridSpec(
            num_scalar_prefetch=1,
            grid=(experts, ff // tile),
            in_specs=in_specs,
            out_specs=[pl.BlockSpec((2, own_rows, width), lambda e, f, w: (w[2], 0, 0), pipeline_mode=one), token, token]
            + [pl.BlockSpec(block, index) for unused, block, index in stored],
            scratch_shapes=[
            pltpu.VMEM((rows, rank), low),
            pltpu.VMEM((rows, rank), low),
            pltpu.VMEM((rows, rank), low),
            pltpu.VMEM((rows, width), f32),
            pltpu.VMEM((rows, rank), f32),
            pltpu.VMEM((rows, width), f32),
            pltpu.VMEM((rows, rank), f32),
            pltpu.VMEM((rows, rank), f32),
        ] + [pltpu.VMEM((own_rows, width), f32) for unused in range(4)],
        ),
        out_shape=[jax.ShapeDtypeStruct((dp_count, own_rows, width), low)] + [part] * 2 + [jax.ShapeDtypeStruct(shape, low) for shape, unused, unused2 in stored],
        input_output_aliases={13 + i: 0 if i == 0 else 2 + i for i in range(len(kept))},
        cost_estimate=pl.CostEstimate(
            flops=experts * rows * width, bytes_accessed=experts * rows * width, transcendentals=0
        ),
        compiler_params=pltpu.CompilerParams(vmem_limit_bytes=60 * 1024 * 1024),
        name="experts",
    )(which, *x_pair, g_all, pick, pick_t, slot, *weights, *kept)
    return results[1:3], [results[0]] + list(results[3:])


def swap(values, axis, distance, count):
    return lax.ppermute(values, axis, [(i, i ^ distance) for i in range(count)])


def near(values, axis, count):
    return [swap(values, axis, 1, count), swap(values, axis, 2, count)]


def spread(values, axis, count, close=None):
    one, two = near(values, axis, count) if close is None else close
    if count == 4 and values.size >= half_from:
        half = values.shape[0] // 2
        three = [swap(two[:half], axis, 1, count), swap(one[half:], axis, 2, count)]
        return [values, one, two, jnp.concatenate(three, axis=0)]
    return [values, one, two] + [swap(values, axis, k, count) for k in range(3, count)]


def collect(blocks, axis, count, cover=None):
    f32 = jnp.float32
    if count == 4 and blocks[0].size >= half_from:
        half = blocks[0].shape[0] // 2
        over_one = swap(blocks[3][:half], axis, 1, count)
        over_two = swap(blocks[3][half:], axis, 2, count)
        top = blocks[0][:half].astype(f32) + swap(blocks[1][:half], axis, 1, count).astype(f32)
        low = blocks[0][half:].astype(f32) + swap(blocks[2][half:], axis, 2, count).astype(f32)
        if cover is not None:
            over_one, over_two, cover = pin(over_one, over_two, cover)
        to_two = (blocks[2][:half].astype(f32) + over_one.astype(f32)).astype(blocks[2].dtype)
        to_one = (blocks[1][half:].astype(f32) + over_two.astype(f32)).astype(blocks[1].dtype)
        to_two, to_one = pin(to_two, to_one)
        top = top + swap(to_two, axis, 2, count).astype(f32)
        low = low + swap(to_one, axis, 1, count).astype(f32)
        total = jnp.concatenate([top, low], axis=0)
    else:
        total = blocks[0].astype(f32)
        for k in range(1, count):
            total = total + swap(blocks[k], axis, k, count).astype(f32)
    return total if cover is None else (total, cover)


def pin(*values):
    return lax.optimization_barrier(values)


def local(
    layer_input,
    out_cotangent,
    gain_attention,
    gain_query,
    gain_key,
    gain_ffn,
    w_qkv,
    w_output,
    a_attention,
    b_attention,
    expert_w_in,
    expert_w_down,
    expert_a_in,
    expert_b_in,
    expert_a_down,
    expert_b_down,
    route_experts,
    route_gates,
    doc_lengths,
    adapter_ids,
):
    low = jnp.bfloat16
    f32 = jnp.float32
    own_rows = layer_input.shape[1]
    full_width = layer_input.shape[2]
    n = lax.axis_size("seq")
    dp_count = lax.axis_size("dp")
    s = lax.axis_index("seq")
    d = lax.axis_index("dp")
    length = own_rows * n
    rank_columns = a_attention.shape[2]
    group_width = full_width // n
    group_heads = H // n
    piece = group_width // dp_count
    group_start = s * group_width
    order = s ^ jnp.arange(n, dtype=jnp.int32)
    position = (order[:, None] * own_rows + jnp.arange(own_rows, dtype=jnp.int32)[None, :]).reshape(-1)
    segment, offset, adapter = doc_layout(doc_lengths[0], adapter_ids[0], position)
    own_adapter = adapter[:own_rows]
    own_mask = column_mask(own_adapter, rank_columns)
    full_mask = column_mask(adapter, rank_columns)

    gates = route_gates[0].T
    gates_high = gates.astype(low)
    meta = jnp.concatenate(
        [
            route_experts[0].T.astype(low),
            gates_high,
            (gates - gates_high.astype(f32)).astype(low),
            own_adapter[None, :].astype(low),
            jnp.zeros((7, own_rows), low),
        ],
        axis=0,
    )
    ab_piece = jnp.concatenate([a_attention[0:3], jnp.swapaxes(b_attention, 1, 2)], axis=0).reshape(-1, rank_columns)
    ab_rows = ab_piece.shape[0]
    ab_piece = jnp.concatenate([ab_piece, meta.reshape(-1, rank_columns)], axis=0)
    ab_got = lax.all_gather(ab_piece, "dp", axis=0)
    tokens = layer_input[0].astype(f32)
    normed = rms_scale(tokens, gain_attention).astype(low)
    wt_piece = jnp.swapaxes(w_qkv, 1, 2)
    wt_piece, ab_got, *close = pin(wt_piece, ab_got, *near(normed, "seq", n))
    w_group = lax.all_gather(wt_piece, "dp", axis=0)
    dp_order = d ^ jnp.arange(dp_count, dtype=jnp.int32)
    meta_all = ab_got[:, ab_rows:].reshape((dp_count,) + meta.shape)[dp_order].astype(f32)
    ab_group = ab_got[:, :ab_rows].reshape(dp_count, 7, piece, rank_columns)
    ab_group = jnp.swapaxes(ab_group, 0, 1).reshape(7, group_width, rank_columns)
    local_count = expert_w_in.shape[0]
    expert_count = local_count * dp_count
    capacity = own_rows * TOP // expert_count * 9 // 8
    capacity = -(-capacity // 16) * 16
    named = meta_all[:, 0:TOP, :].astype(jnp.int32)
    gates_all = meta_all[:, TOP : 2 * TOP, :] + meta_all[:, 2 * TOP : 3 * TOP, :]
    sets_all = meta_all[:, 3 * TOP, :]
    mine = d * local_count + jnp.arange(local_count, dtype=jnp.int32)
    hit = (named[None] == mine[:, None, None, None]).astype(f32)
    member = jnp.sum(hit, axis=2)
    token_gate = jnp.sum(hit * gates_all[None], axis=2)
    t_index = jnp.arange(own_rows, dtype=jnp.int32)
    upto = (t_index[:, None] <= t_index[None, :]).astype(low)
    rank = jnp.einsum("ejt,tu->eju", member.astype(low), upto, preferred_element_type=f32) - 1.0
    slots = jnp.arange(capacity, dtype=jnp.int32).astype(f32)
    rank = jnp.where(member > 0.5, rank, -1.0)
    pick = slots[None, None, :, None] == rank[:, :, None, :]
    pick_t = (rank[:, :, :, None] == slots[None, None, None, :]).astype(low)
    slot_gate = jnp.sum(jnp.where(pick, token_gate[:, :, None, :], 0.0), axis=-1)
    slot_set = jnp.sum(jnp.where(pick, sets_all[None, :, None, :], 0.0), axis=-1)
    slot = jnp.stack([slot_gate, slot_set], axis=-1).reshape(local_count, dp_count * capacity, 2)
    pick = pick.astype(low)

    cosine, sine = rope_tables(offset, HD)

    dot = lambda a, b: jnp.dot(a, b, preferred_element_type=f32)
    dot_t = lambda a, b: lax.dot_general(a, b, (((1,), (1,)), ((), ())), preferred_element_type=f32)
    dot_l = lambda a, b: lax.dot_general(a, b, (((0,), (0,)), ((), ())), preferred_element_type=f32)

    share = jnp.concatenate([ab_group[0:3], ab_group[6:7]], axis=0)
    share_full = jnp.stack(spread(share, "seq", n))[order]
    share_full = jnp.swapaxes(share_full, 0, 1).reshape(4, full_width, rank_columns)
    down_cat = jnp.swapaxes(share_full[0:3], 0, 1).reshape(full_width, 3 * rank_columns)
    upt_output = share_full[3]
    upt_group = ab_group[3:6]
    normed_all = jnp.concatenate(spread(normed, "seq", n, close), axis=0)
    reduced_cat = (jnp.tile(full_mask, (1, 3)) * dot(normed_all, down_cat)).astype(low)
    out_piece = jnp.concatenate([w_output, a_attention[3]], axis=1)
    out_piece, w_group, pick, pick_t, slot, cosine, sine, normed_all, reduced_cat, upt_group, upt_output = pin(
        out_piece, w_group, pick, pick_t, slot, cosine, sine, normed_all, reduced_cat, upt_group, upt_output
    )
    out_maps = lax.all_gather(out_piece, "dp", axis=0, tiled=True)
    reduced_list = [reduced_cat[:, m * rank_columns : (m + 1) * rank_columns] for m in range(3)]
    raw = qkv_project(normed_all, reduced_cat, w_group, upt_group)
    grad_send, raw = pin(out_cotangent[0], raw)
    grad_got = lax.all_gather(grad_send, "dp", axis=0)
    grad_own = jnp.stack([out_cotangent[0], swap(out_cotangent[0], "dp", 1, dp_count)])
    mixed_group, query_heads, key_heads, value_heads, stat = attend(
        raw, cosine, sine, gain_query, gain_key, segment
    )

    partial_out = dot(mixed_group, out_maps).astype(low).reshape(n, own_rows, full_width + rank_columns)
    summed = collect([partial_out[k] for k in range(n)], "seq", n)
    output_reduced = (own_mask * summed[:, full_width:]).astype(low)
    attended = summed[:, :full_width] + dot_t(output_reduced, upt_output)
    hidden = tokens + attended
    normed_ffn = rms_scale(hidden, gain_ffn).astype(low)
    weights = (expert_w_in, expert_w_down, expert_a_in, expert_b_in, expert_a_down, expert_b_down)
    chips = dp_count // 2
    turns = [0] + list(range(chips // 2, chips)) + list(range(1, chips // 2))
    kept = ()
    rows = normed_ffn
    here = normed_ffn
    arrived = swap(rows, "dp", 2 * turns[1], dp_count)
    other = swap(here, "dp", 1, dp_count)
    leaving = None
    flying = None
    grad_normed_ffn = None
    for i, c in enumerate(turns):
        if i > 0:
            here = arrived
            if flying is not None:
                here, flying = pin(here, flying)
                grad_normed_ffn = grad_normed_ffn + flying.astype(f32)
            other = swap(here, "dp", 1, dp_count)
            rows, here, other, leaving = pin(rows, here, other, leaving)
            if i < chips - 1:
                arrived = swap(rows, "dp", 2 * turns[i + 1], dp_count)
            if i == 1:
                grad_normed_ffn = leaving
            else:
                flying = swap(leaving, "dp", 2 * turns[i - 1], dp_count)
        block = lax.shift_right_logical(d, 1) ^ c
        place = d & 1
        which = jnp.stack([block, place, block, place] if c else [0 * d, 0 * d, block, place]).astype(jnp.int32)
        (back, back_other), kept = run_experts(
            c, which, (here, other), grad_got if c else grad_own, pick, pick_t, slot, weights, kept
        )
        if i == chips - 1 and flying is not None:
            flying, back_other = pin(flying, back_other)
        leaving = back.astype(f32) + swap(back_other, "dp", 1, dp_count).astype(f32)
        if i > 0:
            leaving = leaving.astype(low)
    if flying is not None:
        grad_normed_ffn = grad_normed_ffn + flying.astype(f32)
    outs_all, *kept = kept
    leaving, *kept = pin(leaving, *kept)
    flying = swap(leaving, "dp", 2 * turns[-1], dp_count)
    flying, *kept_later = pin(flying, *kept)
    grad_normed_ffn = grad_normed_ffn + flying.astype(f32)

    outs_all, grad_normed_ffn = pin(outs_all, grad_normed_ffn)
    mixture = lax.psum_scatter(outs_all, "dp", scatter_dimension=0)
    grad_out = out_cotangent[0].astype(f32)
    unused, pull_ffn = jax.vjp(lambda values: rms_scale(values, gain_ffn), hidden)
    grad_hidden = grad_out + pull_ffn(grad_normed_ffn)[0]
    grad_hidden_low = grad_hidden.astype(low)
    grad_reduced_output = (own_mask * dot(grad_hidden_low, upt_output)).astype(low)
    grad_pack = jnp.concatenate([grad_hidden_low, grad_reduced_output, output_reduced], axis=1)
    grad_close = near(grad_pack, "seq", n)
    *grad_close, xs, ps, act_rows, gate_rows, up_rows, reds = pin(*grad_close, *kept_later)
    kept_last = (xs, ps, act_rows, gate_rows, up_rows, reds)
    flat = []
    for e in range(local_count):
        xs, unused, unused2, gate_rows, up_rows, reds = kept if e == 0 else kept_later
        unused, ps, act_rows, unused2, unused3, reds_last = kept if e == 0 else kept_last
        red = [(reds if i in (0, 1) else reds_last)[e][:, i * rank_columns : (i + 1) * rank_columns] for i in range(6)]
        terms = [
            (reds[e][:, 3 * rank_columns : 5 * rank_columns], xs[e]),
            (red[0], gate_rows[e]),
            (red[1], up_rows[e]),
            (red[5], act_rows[e]),
            (red[2], ps[e]),
        ]
        flat += [dot_l(a, b).astype(low).reshape(-1, rank_columns, b.shape[1]) for a, b in terms]
    widths = [(x.shape[0], x.shape[2] // n) for x in flat]
    flat = jnp.concatenate(
        [
            x.reshape(x.shape[0], rank_columns, n, -1).transpose(2, 0, 1, 3).reshape(n, -1)
            for x in flat
        ],
        axis=1,
    ).reshape(n, -1, rank_columns)
    grad_packs = spread(grad_pack, "seq", n, grad_close)
    flat, *grad_packs = pin(flat, *grad_packs)
    expert_terms = [lax.dynamic_index_in_dim(flat, order[k], 0, keepdims=False) for k in range(n)]
    grad_pack_all = jnp.concatenate(grad_packs, axis=0)
    grad_all = grad_pack_all[:, :full_width]
    grad_reduced_all = grad_pack_all[:, full_width : full_width + rank_columns]
    output_reduced_all = grad_pack_all[:, full_width + rank_columns :]
    grad_mixed_group = dot_t(grad_pack_all[:, : full_width + rank_columns], out_maps).astype(low)
    expert_sum, grad_mixed_group = collect(expert_terms, "seq", n, grad_mixed_group)
    grad_cols = lax.dynamic_slice_in_dim(grad_all, group_start, group_width, 1)
    grad_upt_output = dot_l(grad_cols, output_reduced_all)
    grad_down_output = dot_l(mixed_group, grad_reduced_all)
    grad_raw_list = attend_back(
        (query_heads, key_heads, value_heads, stat),
        grad_mixed_group,
        raw,
        cosine,
        sine,
        gain_query,
        gain_key,
        segment,
    )
    expert_sum, *grad_raw_list = pin(expert_sum, *grad_raw_list)
    partial_reduced = jnp.concatenate(
        [dot(grad_raw_list[m], upt_group[m]) for m in range(3)], axis=1
    ).astype(low)
    partial_reduced, *grad_raw_list = pin(partial_reduced, *grad_raw_list)
    partial_reduced = partial_reduced.reshape(n, own_rows, 3 * rank_columns)
    summed_reduced = collect([partial_reduced[k] for k in range(n)], "seq", n)
    grad_reduced = (jnp.tile(own_mask, (1, 3)) * summed_reduced).astype(low)
    grad_reduced, *grad_raw_late = pin(grad_reduced, *grad_raw_list)
    grad_reduced_full = jnp.concatenate(spread(grad_reduced, "seq", n), axis=0)
    partial_normed = qkv_back(grad_raw_list, w_group).reshape(n, own_rows, full_width)
    partial_normed, grad_reduced_full, expert_sum = pin(partial_normed, grad_reduced_full, expert_sum)
    summed_back = collect([partial_normed[k] for k in range(n)], "seq", n)
    summed_back, mixture, hidden = pin(summed_back, mixture, hidden)
    layer_output = (hidden + mixture.astype(f32)).astype(low)[None]
    grad_normed = summed_back + dot_t(grad_reduced, down_cat)
    unused_input, pull_input = jax.vjp(lambda values: rms_scale(values, gain_attention), tokens)
    input_grad = (grad_hidden + pull_input(grad_normed)[0]).astype(low)[None]

    grad_upt = [dot_l(grad_raw_late[m], reduced_list[m]) for m in range(3)]
    normed_cols = lax.dynamic_slice_in_dim(normed_all, group_start, group_width, 1)
    grad_down_cat = dot_l(normed_cols, grad_reduced_full)
    parts = [grad_down_cat[:, m * rank_columns : (m + 1) * rank_columns] for m in range(3)]
    parts += [grad_down_output] + grad_upt + [grad_upt_output]
    stacked = jnp.stack([x.astype(low).reshape(dp_count, piece, rank_columns) for x in parts], axis=1)
    own_parts = lax.psum_scatter(stacked, "dp", scatter_dimension=0)
    own_parts, input_grad = pin(own_parts, input_grad)
    own_parts = own_parts.astype(f32)
    grad_a_attention = own_parts[0:4]
    grad_b_attention = jnp.swapaxes(own_parts[4:8], 1, 2)

    flat = expert_sum.reshape(-1)
    pieces = []
    start = 0
    for count, width in widths:
        size = count * rank_columns * width
        pieces.append(flat[start : start + size].reshape(count, rank_columns, width))
        start += size
    per = [pieces[5 * e : 5 * e + 5] for e in range(local_count)]
    grad_a_in = jnp.stack([jnp.swapaxes(p[0], 1, 2) for p in per])
    grad_b_in = jnp.stack([jnp.concatenate([p[1], p[2]], axis=0) for p in per])
    grad_a_down = jnp.stack([p[3][0].T for p in per])
    grad_b_down = jnp.stack([p[4][0] for p in per])
    return (
        layer_output,
        input_grad,
        grad_a_attention,
        grad_b_attention,
        grad_a_in,
        grad_b_in,
        grad_a_down,
        grad_b_down,
    )


def solution(mesh):
    return jax.shard_map(
        local,
        mesh=mesh,
        in_specs=(
            P("dp", "seq", None),
            P("dp", "seq", None),
            P(),
            P(),
            P(),
            P(),
            P(None, None, ("seq", "dp")),
            P(("seq", "dp"), None),
            P(None, ("seq", "dp"), None),
            P(None, None, ("seq", "dp")),
            P("dp", None, None, None),
            P("dp", None, None),
            P("dp", None, None, None),
            P("dp", None, None, None),
            P("dp", None, None),
            P("dp", None, None),
            P("dp", "seq", None),
            P("dp", "seq", None),
            P("dp", None),
            P("dp", None),
        ),
        out_specs=(
            P("dp", "seq", None),
            P("dp", "seq", None),
            P(None, ("seq", "dp"), None),
            P(None, None, ("seq", "dp")),
            P("dp", None, "seq", None),
            P("dp", None, None, "seq"),
            P("dp", "seq", None),
            P("dp", None, "seq"),
        ),
        check_vma=False,
    )
```

```python
import functools

import jax
import jax.numpy as jnp
from jax import lax
from jax.experimental import pallas as pl
from jax.experimental.pallas import tpu as pltpu
from jax.sharding import PartitionSpec as P

H = 16
HD = 128
TOP = 8
R = 16


norm_epsilon = 1e-06
rope_base = 10000.0
masked_score = -1000000000.0
half_from = 200000


def rms_scale(values, gain_vector):
    return (
        values
        * lax.rsqrt(jnp.mean(values * values, axis=-1, keepdims=True) + norm_epsilon)
        * gain_vector
    )


def rope_tables(offset, width):
    half = width // 2
    frequency = rope_base ** (-(jnp.arange(half, dtype=jnp.float32) * 2.0) / width)
    angles = offset.astype(jnp.float32)[:, None] * frequency[None, :]
    cosine = jnp.cos(angles)
    sine = jnp.sin(angles)
    return jnp.concatenate([cosine, cosine], axis=1), jnp.concatenate([-sine, sine], axis=1)


def dot_nn(a, b):
    return lax.dot_general(a, b, (((1,), (0,)), ((), ())), preferred_element_type=jnp.float32)


def dot_nt(a, b):
    return lax.dot_general(a, b, (((1,), (1,)), ((), ())), preferred_element_type=jnp.float32)


def dot_tn(a, b):
    return lax.dot_general(a, b, (((0,), (0,)), ((), ())), preferred_element_type=jnp.float32)


def normed_head(raw, gain):
    inverse = lax.rsqrt(jnp.mean(raw * raw, axis=-1, keepdims=True) + norm_epsilon)
    return raw * inverse * gain, inverse


def turned_head(values, cosine, sine):
    return values * cosine + pltpu.roll(values, values.shape[-1] // 2, 1) * sine


def unturned_head(grad, cosine, sine):
    return grad * cosine + pltpu.roll(grad * sine, grad.shape[-1] // 2, 1)


def attend_kernel(
    tile, q_raw, k_raw, v_raw, cosine, sine, gain_q, gain_k, seg_col, seg_row, mixed, query, key, value, stat
):
    rows = q_raw.shape[0]
    scale = HD ** (-0.5)
    cos_all = cosine[...]
    sin_all = sine[...]
    normed_q, unused = normed_head(q_raw[...], gain_q[...])
    query[...] = turned_head(normed_q, cos_all, sin_all).astype(jnp.bfloat16)
    normed_k, unused = normed_head(k_raw[...], gain_k[...])
    keys = turned_head(normed_k, cos_all, sin_all).astype(jnp.bfloat16)
    key[...] = keys
    values = v_raw[...].astype(jnp.bfloat16)
    value[...] = values
    values_t = values.T
    for start in range(0, rows, tile):
        part = slice(start, start + tile)
        scores = dot_nt(keys, query[part, :]) * scale
        scores = jnp.where(seg_col[...] == seg_row[:, part], scores, masked_score)
        top = jnp.max(scores, axis=0, keepdims=True)
        weight = jnp.exp(scores - top)
        total = jnp.sum(weight, axis=0, keepdims=True)
        soft = (weight * (1.0 / total)).astype(jnp.bfloat16)
        mixed[part, :] = dot_nn(values_t, soft).T.astype(jnp.bfloat16)
        stat[0, :, part] = top + jnp.log(total)


def attend(raw, cosine, sine, gain_q, gain_k, segment):
    unused, length, width = raw.shape
    heads = width // HD
    tile = min(256, length)
    head = pl.BlockSpec((length, HD), lambda h: (0, h))
    raw_head = [pl.BlockSpec((None, length, HD), functools.partial(lambda m, h: (m, 0, h), m)) for m in range(3)]
    fixed = lambda shape: pl.BlockSpec(shape, lambda h: (0, 0))
    seg = segment.astype(jnp.float32)
    low = jax.ShapeDtypeStruct((length, width), jnp.bfloat16)
    return pl.pallas_call(
        functools.partial(attend_kernel, tile),
        grid=(heads,),
        in_specs=raw_head + [fixed((length, HD)), fixed((length, HD)), fixed((1, HD)), fixed((1, HD)),
                  fixed((length, 1)), fixed((1, length))],
        out_specs=[head, head, head, head, pl.BlockSpec((1, 1, length), lambda h: (h, 0, 0))],
        out_shape=[low, low, low, low, jax.ShapeDtypeStruct((heads, 1, length), jnp.float32)],
        cost_estimate=pl.CostEstimate(
            flops=4 * heads * length * length * HD, bytes_accessed=20 * length * width, transcendentals=heads * length * length
        ),
        name="attend",
    )(raw, raw, raw, cosine, sine, gain_q[None, :], gain_k[None, :], seg[:, None], seg[None, :])


def attend_back_kernel(
    tile, query, key, value, grad_mixed, stat, q_raw, k_raw, cosine, sine, gain_q, gain_k, seg_col, seg_row,
    grad_q, grad_k, grad_v, sum_k, sum_v
):
    rows = q_raw.shape[0]
    scale = HD ** (-0.5)
    keys = key[...]
    values = value[...]
    keys_t = keys.T

    def through(grad, raw_ref, gain_ref, part):
        grad = grad.astype(jnp.bfloat16).astype(jnp.float32)
        raw = raw_ref[part, :]
        gain = gain_ref[...]
        inverse = lax.rsqrt(jnp.mean(raw * raw, axis=-1, keepdims=True) + norm_epsilon)
        grad = unturned_head(grad, cosine[part, :], sine[part, :]) * gain
        dots = jnp.mean(grad * raw, axis=-1, keepdims=True)
        return (inverse * (grad - raw * (inverse * inverse * dots))).astype(jnp.bfloat16)

    for start in range(0, rows, tile):
        part = slice(start, start + tile)
        queries = query[part, :]
        grads = grad_mixed[part, :]
        scores = dot_nt(keys, queries) * scale
        scores = jnp.where(seg_col[...] == seg_row[:, part], scores, masked_score)
        soft = jnp.exp(scores - stat[0, :, part])
        grad_soft = dot_nt(values, grads)
        delta = jnp.sum(soft * grad_soft, axis=0, keepdims=True)
        grad_scores = (soft * (grad_soft - delta)).astype(jnp.bfloat16)
        term_k = dot_nn(grad_scores, queries)
        term_v = dot_nn(soft.astype(jnp.bfloat16), grads)
        if start == 0:
            sum_k[...] = term_k
            sum_v[...] = term_v
        else:
            sum_k[...] += term_k
            sum_v[...] += term_v
        grad_q[part, :] = through(dot_nn(keys_t, grad_scores).T * scale, q_raw, gain_q, part)
    for start in range(0, rows, tile):
        part = slice(start, start + tile)
        grad_k[part, :] = through(sum_k[part, :] * scale, k_raw, gain_k, part)
        grad_v[part, :] = sum_v[part, :].astype(jnp.bfloat16)


def attend_back(kept, grad_mixed, raw, cosine, sine, gain_q, gain_k, segment):
    query, key, value, stat = kept
    unused, length, width = raw.shape
    heads = width // HD
    tile = min(256, length)
    head = pl.BlockSpec((length, HD), lambda h: (0, h))
    raw_head = [pl.BlockSpec((None, length, HD), functools.partial(lambda m, h: (m, 0, h), m)) for m in range(3)]
    fixed = lambda shape: pl.BlockSpec(shape, lambda h: (0, 0))
    seg = segment.astype(jnp.float32)
    low = jax.ShapeDtypeStruct((length, width), jnp.bfloat16)
    return pl.pallas_call(
        functools.partial(attend_back_kernel, tile),
        grid=(heads,),
        in_specs=[head, head, head, head, pl.BlockSpec((1, 1, length), lambda h: (h, 0, 0)), raw_head[0], raw_head[1],
                  fixed((length, HD)), fixed((length, HD)), fixed((1, HD)), fixed((1, HD)),
                  fixed((length, 1)), fixed((1, length))],
        out_specs=[head, head, head],
        out_shape=[low, low, low],
        scratch_shapes=[pltpu.VMEM((length, HD), jnp.float32), pltpu.VMEM((length, HD), jnp.float32)],
        cost_estimate=pl.CostEstimate(
            flops=heads * length * HD, bytes_accessed=length * width, transcendentals=0
        ),
        name="attend_back",
    )(query, key, value, grad_mixed, stat, raw, raw, cosine, sine, gain_q[None, :], gain_k[None, :],
      seg[:, None], seg[None, :])


def doc_layout(lengths, chosen, position):
    slots = jnp.arange(lengths.shape[0], dtype=jnp.int32)
    doc_ends = jnp.sum(jnp.where(slots[:, None] >= slots[None, :], lengths[None, :], 0), axis=1)
    starts = doc_ends - lengths
    segment = jnp.sum((position[:, None] >= doc_ends[None, :]).astype(jnp.int32), axis=1)
    doc_pick = (segment[:, None] == slots[None, :]).astype(jnp.int32)
    offset = position - jnp.sum(doc_pick * starts[None, :], axis=1)
    adapter = jnp.sum(doc_pick * chosen[None, :], axis=1)
    return (segment, offset, adapter)


def column_mask(adapter, columns):
    groups = jnp.arange(columns, dtype=jnp.int32) // R
    return (groups[None, :] == adapter[:, None]).astype(jnp.float32)


def qkv_kernel(x_ref, reduced_ref, w_ref, up_ref, out_ref):
    width = w_ref.shape[0] * w_ref.shape[1]
    weights = w_ref[...].reshape(width, x_ref.shape[1])
    out_ref[0] = dot_nt(x_ref[...], weights) + dot_nt(reduced_ref[...], up_ref[0])


def qkv_project(normed_all, reduced_cat, w_group, up_group):
    length, width = normed_all.shape
    dp_count, unused, piece, unused = w_group.shape
    group = dp_count * piece
    rank = up_group.shape[2]
    half = dp_count // 2
    return pl.pallas_call(
        qkv_kernel,
        grid=(3, 2),
        in_specs=[
            pl.BlockSpec((length, width), lambda m, p: (0, 0)),
            pl.BlockSpec((length, rank), lambda m, p: (0, m)),
            pl.BlockSpec((half, None, piece, width), lambda m, p: (p, m, 0, 0)),
            pl.BlockSpec((1, group // 2, rank), lambda m, p: (m, p, 0)),
        ],
        out_specs=pl.BlockSpec((1, length, group // 2), lambda m, p: (m, 0, p)),
        out_shape=jax.ShapeDtypeStruct((3, length, group), jnp.float32),
        cost_estimate=pl.CostEstimate(
            flops=6 * length * width * group, bytes_accessed=2 * length * width + 12 * length * group + 6 * group * width,
            transcendentals=0,
        ),
        name="qkv_project",
    )(normed_all, reduced_cat, w_group, up_group)


def qkv_back_kernel(a_ref, b_ref, c_ref, w_ref, out_ref):
    dp_count, unused, piece, cols = w_ref.shape
    total = None
    for m, ref in enumerate((a_ref, b_ref, c_ref)):
        term = dot_nn(ref[...], w_ref[:, m].reshape(dp_count * piece, cols))
        total = term if total is None else total + term
    out_ref[...] = total.astype(jnp.bfloat16)


def qkv_back(grads, w_group):
    length, group = grads[0].shape
    dp_count, unused, piece, width = w_group.shape
    tile = min(256, width)
    whole = pl.BlockSpec((length, group), lambda i: (0, 0))
    return pl.pallas_call(
        qkv_back_kernel,
        grid=(width // tile,),
        in_specs=[whole, whole, whole, pl.BlockSpec((dp_count, 3, piece, tile), lambda i: (0, 0, 0, i))],
        out_specs=pl.BlockSpec((length, tile), lambda i: (0, i)),
        out_shape=jax.ShapeDtypeStruct((length, width), jnp.bfloat16),
        cost_estimate=pl.CostEstimate(flops=length * width, bytes_accessed=length * width, transcendentals=0),
        name="qkv_back",
    )(grads[0], grads[1], grads[2], w_group)


def expert_kernel(kept_in, which, *refs):
    (x_a, x_b, g_both, pick, pick_t, slot, w_in, w_down, a_in, b_in, a_down, b_down) = refs[:12]
    refs = refs[12 + kept_in:]
    (out_both, back_a, back_b, xs, ps, act_o, gate_o, up_o, reds) = refs[:9]
    (red_g, red_u, gred_d, down_acc, down_red, gx_acc, gred_g, gred_u, sum_out_a, sum_out_b, sum_back_a, sum_back_b) = refs[9:]
    low = jnp.bfloat16
    e = pl.program_id(0)
    f = pl.program_id(1)
    last = pl.num_programs(1) - 1
    cap = pick.shape[2]
    rank = a_in.shape[3]
    rows = xs.shape[1]
    groups = lax.shift_right_logical(lax.broadcasted_iota(jnp.int32, (rows, rank), 1), R.bit_length() - 1)
    mask = jnp.where(groups.astype(jnp.float32) == slot[0, :, 1:2], 1.0, 0.0)

    @pl.when(f == 0)
    def _():
        for b, x_ref in enumerate((x_a, x_b)):
            part = slice(b * cap, (b + 1) * cap)
            g_place = which[1] if b == 0 else 1 - which[1]
            xs[0, part, :] = dot_nn(pick[0, b], x_ref[...]).astype(low)
            ps[0, part, :] = (slot[0, part, 0:1] * dot_nn(pick[0, b], g_both[g_place])).astype(low)
        red_g[...] = (mask * dot_nn(xs[0], a_in[0, 0])).astype(low)
        red_u[...] = (mask * dot_nn(xs[0], a_in[0, 1])).astype(low)
        gred_d[...] = (mask * dot_nt(ps[0], b_down[0])).astype(low)

    x = xs[0]
    p = ps[0]
    gate = dot_nn(x, w_in[0, 0]) + dot_nn(red_g[...], b_in[0, 0])
    up = dot_nn(x, w_in[0, 1]) + dot_nn(red_u[...], b_in[0, 1])
    grad_act = dot_nt(p, w_down[0]) + dot_nt(gred_d[...], a_down[0])
    sigma = 1.0 / (1.0 + jnp.exp(-gate))
    silu = gate * sigma
    act = (silu * up).astype(low)
    grad_gate = (grad_act * up * (sigma * (1.0 + gate * (1.0 - sigma)))).astype(low)
    grad_up = (grad_act * silu).astype(low)
    act_o[0] = act
    gate_o[0] = grad_gate
    up_o[0] = grad_up
    down_term = dot_nn(act, w_down[0])
    down_red_term = dot_nn(act, a_down[0])
    gx_term = dot_nt(grad_gate, w_in[0, 0]) + dot_nt(grad_up, w_in[0, 1])
    gred_g_term = dot_nt(grad_gate, b_in[0, 0])
    gred_u_term = dot_nt(grad_up, b_in[0, 1])

    @pl.when(f == 0)
    def _():
        down_acc[...] = down_term
        down_red[...] = down_red_term
        gx_acc[...] = gx_term
        gred_g[...] = gred_g_term
        gred_u[...] = gred_u_term

    @pl.when(f > 0)
    def _():
        down_acc[...] += down_term
        down_red[...] += down_red_term
        gx_acc[...] += gx_term
        gred_g[...] += gred_g_term
        gred_u[...] += gred_u_term

    @pl.when(f == last)
    def _():
        reduced_d = (mask * down_red[...]).astype(low)
        back_g = (mask * gred_g[...]).astype(low)
        back_u = (mask * gred_u[...]).astype(low)
        for i, value in enumerate((red_g[...], red_u[...], reduced_d, back_g, back_u, gred_d[...])):
            reds[0, :, i * rank : (i + 1) * rank] = value
        produced = down_acc[...] + dot_nn(reduced_d, b_down[0])
        scaled = (slot[0, :, 0:1] * produced).astype(low)
        grads = (gx_acc[...] + dot_nt(back_g, a_in[0, 0]) + dot_nt(back_u, a_in[0, 1])).astype(low)
        for b, (out_sum, back_ref, back_sum) in enumerate(
            ((sum_out_a, back_a, sum_back_a), (sum_out_b, back_b, sum_back_b))
        ):
            part = slice(b * cap, (b + 1) * cap)
            out_ref = out_both.at[which[3] if b == 0 else 1 - which[3]]
            for values, total, result in ((scaled, out_sum, out_ref), (grads, back_sum, back_ref)):
                term = dot_nn(pick_t[0, b], values[part, :])

                @pl.when(e == 0)
                def _():
                    total[...] = term

                @pl.when(e > 0)
                def _():
                    total[...] += term

                @pl.when(e == pl.num_programs(0) - 1)
                def _():
                    result[...] = total[...].astype(low)


def run_experts(which, x_pair, g_all, pick, pick_t, slot, weights, kept):
    w_in, w_down, a_in, b_in, a_down, b_down = weights
    experts, unused, width, ff = w_in.shape
    unused, dp_count, cap, own_rows = pick.shape
    rank = a_down.shape[2]
    rows = 2 * cap
    tile = min(256, ff)
    low = jnp.bfloat16
    f32 = jnp.float32
    one = pl.Buffered(1)
    token = pl.BlockSpec((own_rows, width), lambda e, f, w: (0, 0), pipeline_mode=one)
    stored = [
        ((experts, dp_count * cap, width), (1, rows, width), lambda e, f, w: (e, w[4], 0)),
        ((experts, dp_count * cap, width), (1, rows, width), lambda e, f, w: (e, w[4], 0)),
        ((experts, dp_count * cap, ff), (1, rows, tile), lambda e, f, w: (e, w[4], f)),
        ((experts, dp_count * cap, ff), (1, rows, tile), lambda e, f, w: (e, w[4], f)),
        ((experts, dp_count * cap, ff), (1, rows, tile), lambda e, f, w: (e, w[4], f)),
        ((experts, dp_count * cap, 6 * rank), (1, rows, 6 * rank), lambda e, f, w: (e, w[4], 0)),
    ]
    in_specs = [
        token, token, pl.BlockSpec((2, own_rows, width), lambda e, f, w: (w[0], 0, 0), pipeline_mode=one),
        pl.BlockSpec((1, 2, cap, own_rows), lambda e, f, w: (e, w[4], 0, 0)),
        pl.BlockSpec((1, 2, own_rows, cap), lambda e, f, w: (e, w[4], 0, 0)),
        pl.BlockSpec((1, rows, 2), lambda e, f, w: (e, w[4], 0)),
        pl.BlockSpec((1, 2, width, tile), lambda e, f, w: (e, 0, 0, f)),
        pl.BlockSpec((1, tile, width), lambda e, f, w: (e, f, 0)),
        pl.BlockSpec((1, 2, width, rank), lambda e, f, w: (e, 0, 0, 0)),
        pl.BlockSpec((1, 2, rank, tile), lambda e, f, w: (e, 0, 0, f)),
        pl.BlockSpec((1, tile, rank), lambda e, f, w: (e, f, 0)),
        pl.BlockSpec((1, rank, width), lambda e, f, w: (e, 0, 0)),
    ] + [pl.BlockSpec(memory_space=pl.ANY) for unused in kept]
    part = jax.ShapeDtypeStruct((own_rows, width), low)
    results = pl.pallas_call(
        functools.partial(expert_kernel, len(kept)),
        grid_spec=pltpu.PrefetchScalarGridSpec(
            num_scalar_prefetch=1,
            grid=(experts, ff // tile),
            in_specs=in_specs,
            out_specs=[pl.BlockSpec((2, own_rows, width), lambda e, f, w: (w[2], 0, 0), pipeline_mode=one), token, token]
            + [pl.BlockSpec(block, index) for unused, block, index in stored],
            scratch_shapes=[
            pltpu.VMEM((rows, rank), low),
            pltpu.VMEM((rows, rank), low),
            pltpu.VMEM((rows, rank), low),
            pltpu.VMEM((rows, width), f32),
            pltpu.VMEM((rows, rank), f32),
            pltpu.VMEM((rows, width), f32),
            pltpu.VMEM((rows, rank), f32),
            pltpu.VMEM((rows, rank), f32),
        ] + [pltpu.VMEM((own_rows, width), f32) for unused in range(4)],
        ),
        out_shape=[jax.ShapeDtypeStruct((dp_count, own_rows, width), low)] + [part] * 2 + [jax.ShapeDtypeStruct(shape, low) for shape, unused, unused2 in stored],
        input_output_aliases={13 + i: 0 if i == 0 else 2 + i for i in range(len(kept))},
        cost_estimate=pl.CostEstimate(
            flops=experts * rows * width, bytes_accessed=experts * rows * width, transcendentals=0
        ),
        compiler_params=pltpu.CompilerParams(vmem_limit_bytes=60 * 1024 * 1024),
        name="experts",
    )(which, *x_pair, g_all, pick, pick_t, slot, *weights, *kept)
    return results[1:3], [results[0]] + list(results[3:])


def adapter_kernel(which, xs, ps, act, gate, up, reds, out):
    rank = out.shape[3]
    red = [reds[0, :, i * rank : (i + 1) * rank] for i in range(6)]
    into = dot_tn(xs[0], reds[0, :, 3 * rank : 5 * rank])
    parts = [into[:, :rank], into[:, rank:], dot_tn(act[0], red[5])]
    for wide in (dot_tn(red[0], gate[0]), dot_tn(red[1], up[0]), dot_tn(red[2], ps[0])):
        parts += [wide[:, i : i + rank] for i in range(0, wide.shape[1], rank)]
    start = 0
    for part in parts:
        out[0, 0, start : start + part.shape[0], :] = part.astype(jnp.bfloat16)
        start += part.shape[0]


def adapter_grads(kept, order):
    xs, ps, act, gate, up, reds = kept
    experts, rows, width = xs.shape
    ff = act.shape[2]
    n = order.shape[0]
    rank = reds.shape[2] // 6
    total = (3 * width + 3 * ff) // n
    wide = pl.BlockSpec((1, rows, width // n), lambda e, k, w: (e, 0, w[k]))
    narrow = pl.BlockSpec((1, rows, ff // n), lambda e, k, w: (e, 0, w[k]))
    return pl.pallas_call(
        adapter_kernel,
        grid_spec=pltpu.PrefetchScalarGridSpec(
            num_scalar_prefetch=1,
            grid=(experts, n),
            in_specs=[wide, wide, narrow, narrow, narrow, pl.BlockSpec((1, rows, 6 * rank), lambda e, k, w: (e, 0, 0))],
            out_specs=pl.BlockSpec((1, 1, total, rank), lambda e, k, w: (k, e, 0, 0)),
        ),
        out_shape=jax.ShapeDtypeStruct((n, experts, total, rank), jnp.bfloat16),
        cost_estimate=pl.CostEstimate(flops=rows * width, bytes_accessed=rows * width, transcendentals=0),
        name="adapter_grads",
    )(order, xs, ps, act, gate, up, reds)


def swap(values, axis, distance, count):
    return lax.ppermute(values, axis, [(i, i ^ distance) for i in range(count)])


def near(values, axis, count):
    return [swap(values, axis, 1, count), swap(values, axis, 2, count)]


def spread(values, axis, count, close=None):
    one, two = near(values, axis, count) if close is None else close
    if count == 4 and values.size >= half_from:
        half = values.shape[0] // 2
        three = [swap(two[:half], axis, 1, count), swap(one[half:], axis, 2, count)]
        return [values, one, two, jnp.concatenate(three, axis=0)]
    return [values, one, two] + [swap(values, axis, k, count) for k in range(3, count)]


def collect_begin(blocks, axis, count):
    if count == 4 and blocks[0].size >= half_from:
        half = blocks[0].shape[0] // 2
        return [
            swap(blocks[3][:half], axis, 1, count),
            swap(blocks[3][half:], axis, 2, count),
            swap(blocks[1][:half], axis, 1, count),
            swap(blocks[2][half:], axis, 2, count),
        ]
    return [swap(blocks[k], axis, k, count) for k in range(1, count)]


def collect_end(blocks, arrived, axis, count):
    f32 = jnp.float32
    if count == 4 and blocks[0].size >= half_from:
        half = blocks[0].shape[0] // 2
        over_one, over_two, from_one, from_two = arrived
        to_two = (blocks[2][:half].astype(f32) + over_one.astype(f32)).astype(blocks[2].dtype)
        to_one = (blocks[1][half:].astype(f32) + over_two.astype(f32)).astype(blocks[1].dtype)
        to_two, to_one = pin(to_two, to_one)
        top = blocks[0][:half].astype(f32) + from_one.astype(f32) + swap(to_two, axis, 2, count).astype(f32)
        low = blocks[0][half:].astype(f32) + from_two.astype(f32) + swap(to_one, axis, 1, count).astype(f32)
        return jnp.concatenate([top, low], axis=0)
    return sum((x.astype(f32) for x in arrived), blocks[0].astype(f32))


def collect(blocks, axis, count):
    return collect_end(blocks, collect_begin(blocks, axis, count), axis, count)


def pin(*values):
    return lax.optimization_barrier(values)


def local(
    layer_input,
    out_cotangent,
    gain_attention,
    gain_query,
    gain_key,
    gain_ffn,
    w_qkv,
    w_output,
    a_attention,
    b_attention,
    expert_w_in,
    expert_w_down,
    expert_a_in,
    expert_b_in,
    expert_a_down,
    expert_b_down,
    route_experts,
    route_gates,
    doc_lengths,
    adapter_ids,
):
    low = jnp.bfloat16
    f32 = jnp.float32
    own_rows = layer_input.shape[1]
    full_width = layer_input.shape[2]
    n = lax.axis_size("seq")
    dp_count = lax.axis_size("dp")
    s = lax.axis_index("seq")
    d = lax.axis_index("dp")
    length = own_rows * n
    rank_columns = a_attention.shape[2]
    group_width = full_width // n
    group_heads = H // n
    piece = group_width // dp_count
    group_start = s * group_width
    order = s ^ jnp.arange(n, dtype=jnp.int32)
    position = (order[:, None] * own_rows + jnp.arange(own_rows, dtype=jnp.int32)[None, :]).reshape(-1)
    segment, offset, adapter = doc_layout(doc_lengths[0], adapter_ids[0], position)
    own_adapter = adapter[:own_rows]
    own_mask = column_mask(own_adapter, rank_columns)
    full_mask = column_mask(adapter, rank_columns)

    gates = route_gates[0].T
    gates_high = gates.astype(low)
    meta = jnp.concatenate(
        [
            route_experts[0].T.astype(low),
            gates_high,
            (gates - gates_high.astype(f32)).astype(low),
            own_adapter[None, :].astype(low),
            jnp.zeros((7, own_rows), low),
        ],
        axis=0,
    )
    ab_piece = jnp.concatenate([a_attention[0:3], jnp.swapaxes(b_attention, 1, 2)], axis=0).reshape(-1, rank_columns)
    ab_rows = ab_piece.shape[0]
    ab_piece = jnp.concatenate([ab_piece, meta.reshape(-1, rank_columns)], axis=0)
    ab_got = lax.all_gather(ab_piece, "dp", axis=0)
    tokens = layer_input[0].astype(f32)
    normed = rms_scale(tokens, gain_attention).astype(low)
    wt_piece = jnp.swapaxes(w_qkv, 1, 2)
    wt_piece, ab_got, *close = pin(wt_piece, ab_got, *near(normed, "seq", n))
    w_group = lax.all_gather(wt_piece, "dp", axis=0)
    dp_order = d ^ jnp.arange(dp_count, dtype=jnp.int32)
    meta_all = ab_got[:, ab_rows:].reshape((dp_count,) + meta.shape)[dp_order].astype(f32)
    ab_group = ab_got[:, :ab_rows].reshape(dp_count, 7, piece, rank_columns)
    ab_group = jnp.swapaxes(ab_group, 0, 1).reshape(7, group_width, rank_columns)
    local_count = expert_w_in.shape[0]
    expert_count = local_count * dp_count
    capacity = own_rows * TOP // expert_count * 9 // 8
    capacity = -(-capacity // 16) * 16
    named = meta_all[:, 0:TOP, :].astype(jnp.int32)
    gates_all = meta_all[:, TOP : 2 * TOP, :] + meta_all[:, 2 * TOP : 3 * TOP, :]
    sets_all = meta_all[:, 3 * TOP, :]
    mine = d * local_count + jnp.arange(local_count, dtype=jnp.int32)
    hit = (named[None] == mine[:, None, None, None]).astype(f32)
    member = jnp.sum(hit, axis=2)
    token_gate = jnp.sum(hit * gates_all[None], axis=2)
    t_index = jnp.arange(own_rows, dtype=jnp.int32)
    upto = (t_index[:, None] <= t_index[None, :]).astype(low)
    rank = jnp.einsum("ejt,tu->eju", member.astype(low), upto, preferred_element_type=f32) - 1.0
    slots = jnp.arange(capacity, dtype=jnp.int32).astype(f32)
    rank = jnp.where(member > 0.5, rank, -1.0)
    pick = slots[None, None, :, None] == rank[:, :, None, :]
    pick_t = (rank[:, :, :, None] == slots[None, None, None, :]).astype(low)
    slot_gate = jnp.sum(jnp.where(pick, token_gate[:, :, None, :], 0.0), axis=-1)
    slot_set = jnp.sum(jnp.where(pick, sets_all[None, :, None, :], 0.0), axis=-1)
    slot = jnp.stack([slot_gate, slot_set], axis=-1).reshape(local_count, dp_count * capacity, 2)
    pick = pick.astype(low)

    cosine, sine = rope_tables(offset, HD)

    dot = lambda a, b: jnp.dot(a, b, preferred_element_type=f32)
    dot_t = lambda a, b: lax.dot_general(a, b, (((1,), (1,)), ((), ())), preferred_element_type=f32)
    dot_l = lambda a, b: lax.dot_general(a, b, (((0,), (0,)), ((), ())), preferred_element_type=f32)

    share = jnp.concatenate([ab_group[0:3], ab_group[6:7]], axis=0)
    share_full = jnp.stack(spread(share, "seq", n))[order]
    share_full = jnp.swapaxes(share_full, 0, 1).reshape(4, full_width, rank_columns)
    down_cat = jnp.swapaxes(share_full[0:3], 0, 1).reshape(full_width, 3 * rank_columns)
    upt_output = share_full[3]
    upt_group = ab_group[3:6]
    normed_all = jnp.concatenate(spread(normed, "seq", n, close), axis=0)
    reduced_cat = (jnp.tile(full_mask, (1, 3)) * dot(normed_all, down_cat)).astype(low)
    out_piece = jnp.concatenate([w_output, a_attention[3]], axis=1)
    out_piece, w_group, pick, pick_t, slot, cosine, sine, normed_all, reduced_cat, upt_group, upt_output = pin(
        out_piece, w_group, pick, pick_t, slot, cosine, sine, normed_all, reduced_cat, upt_group, upt_output
    )
    out_maps = lax.all_gather(out_piece, "dp", axis=0, tiled=True)
    reduced_list = [reduced_cat[:, m * rank_columns : (m + 1) * rank_columns] for m in range(3)]
    raw = qkv_project(normed_all, reduced_cat, w_group, upt_group)
    grad_send, raw = pin(out_cotangent[0], raw)
    grad_got = lax.all_gather(grad_send, "dp", axis=0)
    grad_own = jnp.stack([out_cotangent[0], swap(out_cotangent[0], "dp", 1, dp_count)])
    mixed_group, query_heads, key_heads, value_heads, stat = attend(
        raw, cosine, sine, gain_query, gain_key, segment
    )

    partial_out = dot(mixed_group, out_maps).astype(low).reshape(n, own_rows, full_width + rank_columns)
    summed = collect([partial_out[k] for k in range(n)], "seq", n)
    output_reduced = (own_mask * summed[:, full_width:]).astype(low)
    attended = summed[:, :full_width] + dot_t(output_reduced, upt_output)
    hidden = tokens + attended
    normed_ffn = rms_scale(hidden, gain_ffn).astype(low)
    weights = (expert_w_in, expert_w_down, expert_a_in, expert_b_in, expert_a_down, expert_b_down)
    chips = dp_count // 2
    turns = [0] + list(range(chips // 2, chips)) + list(range(1, chips // 2))
    kept = ()
    rows = normed_ffn
    here = normed_ffn
    arrived = swap(rows, "dp", 2 * turns[1], dp_count)
    other = swap(here, "dp", 1, dp_count)
    leaving = None
    flying = None
    grad_normed_ffn = None
    for i, c in enumerate(turns):
        if i > 0:
            here = arrived
            if flying is not None:
                here, flying = pin(here, flying)
                grad_normed_ffn = grad_normed_ffn + flying.astype(f32)
            other = swap(here, "dp", 1, dp_count)
            rows, here, other, leaving = pin(rows, here, other, leaving)
            if i < chips - 1:
                arrived = swap(rows, "dp", 2 * turns[i + 1], dp_count)
            if i == 1:
                grad_normed_ffn = leaving
            else:
                flying = swap(leaving, "dp", 2 * turns[i - 1], dp_count)
        block = lax.shift_right_logical(d, 1) ^ c
        place = d & 1
        which = jnp.stack(([block, place] if c else [0 * d, 0 * d]) + [block, place, 0 * d + c]).astype(jnp.int32)
        (back, back_other), kept = run_experts(
            which, (here, other), grad_got if c else grad_own, pick, pick_t, slot, weights, kept
        )
        if i == chips - 1 and flying is not None:
            flying, back_other = pin(flying, back_other)
        leaving = back.astype(f32) + swap(back_other, "dp", 1, dp_count).astype(f32)
        if i > 0:
            leaving = leaving.astype(low)
    if flying is not None:
        grad_normed_ffn = grad_normed_ffn + flying.astype(f32)
    outs_all, *kept = kept
    leaving, *kept = pin(leaving, *kept)
    flying = swap(leaving, "dp", 2 * turns[-1], dp_count)
    flat = adapter_grads(kept, order)
    expert_arrived = collect_begin([flat[k] for k in range(n)], "seq", n)
    flat, flying = pin(flat, flying)
    expert_terms = [flat[k] for k in range(n)]
    grad_normed_ffn = grad_normed_ffn + flying.astype(f32)

    outs_all, grad_normed_ffn = pin(outs_all, grad_normed_ffn)
    mixture = lax.psum_scatter(outs_all, "dp", scatter_dimension=0)
    grad_out = out_cotangent[0].astype(f32)
    unused, pull_ffn = jax.vjp(lambda values: rms_scale(values, gain_ffn), hidden)
    grad_hidden = grad_out + pull_ffn(grad_normed_ffn)[0]
    grad_hidden_low = grad_hidden.astype(low)
    grad_reduced_output = (own_mask * dot(grad_hidden_low, upt_output)).astype(low)
    grad_pack = jnp.concatenate([grad_hidden_low, grad_reduced_output, output_reduced], axis=1)
    grad_pack, *expert_arrived = pin(grad_pack, *expert_arrived)
    grad_packs = spread(grad_pack, "seq", n)
    expert_arrived = list(pin(*expert_arrived, *grad_packs))
    grad_packs = expert_arrived[-n:]
    expert_sum = collect_end(expert_terms, expert_arrived[:-n], "seq", n)
    grad_pack_all = jnp.concatenate(grad_packs, axis=0)
    grad_all = grad_pack_all[:, :full_width]
    grad_reduced_all = grad_pack_all[:, full_width : full_width + rank_columns]
    output_reduced_all = grad_pack_all[:, full_width + rank_columns :]
    grad_mixed_group = dot_t(grad_pack_all[:, : full_width + rank_columns], out_maps).astype(low)
    grad_cols = lax.dynamic_slice_in_dim(grad_all, group_start, group_width, 1)
    grad_upt_output = dot_l(grad_cols, output_reduced_all)
    grad_down_output = dot_l(mixed_group, grad_reduced_all)
    grad_raw_list = attend_back(
        (query_heads, key_heads, value_heads, stat),
        grad_mixed_group,
        raw,
        cosine,
        sine,
        gain_query,
        gain_key,
        segment,
    )
    expert_sum, *grad_raw_list = pin(expert_sum, *grad_raw_list)
    partial_reduced = jnp.concatenate(
        [dot(grad_raw_list[m], upt_group[m]) for m in range(3)], axis=1
    ).astype(low)
    partial_reduced, *grad_raw_list = pin(partial_reduced, *grad_raw_list)
    partial_reduced = partial_reduced.reshape(n, own_rows, 3 * rank_columns)
    summed_reduced = collect([partial_reduced[k] for k in range(n)], "seq", n)
    grad_reduced = (jnp.tile(own_mask, (1, 3)) * summed_reduced).astype(low)
    grad_reduced, *grad_raw_late = pin(grad_reduced, *grad_raw_list)
    grad_reduced_full = jnp.concatenate(spread(grad_reduced, "seq", n), axis=0)
    partial_normed = qkv_back(grad_raw_list, w_group).reshape(n, own_rows, full_width)
    partial_normed, grad_reduced = pin(partial_normed, grad_reduced)
    grad_upt = [dot_l(grad_raw_late[m], reduced_list[m]) for m in range(3)]
    normed_cols = lax.dynamic_slice_in_dim(normed_all, group_start, group_width, 1)
    grad_down_cat = dot_l(normed_cols, grad_reduced_full)
    parts = [grad_down_cat[:, m * rank_columns : (m + 1) * rank_columns] for m in range(3)]
    parts += [grad_down_output] + grad_upt + [grad_upt_output]
    stacked = jnp.stack([x.astype(low).reshape(dp_count, piece, rank_columns) for x in parts], axis=1)
    normed_terms = [partial_normed[k] for k in range(n)]
    arrived = collect_begin(normed_terms, "seq", n)
    stacked, *arrived = pin(stacked, *arrived)
    summed_back = collect_end(normed_terms, arrived, "seq", n)
    summed_back, mixture, hidden = pin(summed_back, mixture, hidden)
    layer_output = (hidden + mixture.astype(f32)).astype(low)[None]
    grad_normed = summed_back + dot_t(grad_reduced, down_cat)
    unused_input, pull_input = jax.vjp(lambda values: rms_scale(values, gain_attention), tokens)
    input_grad = (grad_hidden + pull_input(grad_normed)[0]).astype(low)[None]

    stacked, expert_sum = pin(stacked, expert_sum)
    own_parts = lax.psum_scatter(stacked, "dp", scatter_dimension=0)
    own_parts, input_grad = pin(own_parts, input_grad)
    own_parts = own_parts.astype(f32)
    grad_a_attention = own_parts[0:4]
    grad_b_attention = jnp.swapaxes(own_parts[4:8], 1, 2)

    own_width = full_width // n
    own_ff = expert_w_down.shape[1] // n
    columns = lambda x, count: jnp.swapaxes(x.reshape(local_count, count, -1, rank_columns, rank_columns), 2, 3).reshape(
        local_count, count, rank_columns, -1
    )
    ends = [2 * own_width, 2 * own_width + own_ff, 2 * own_width + 3 * own_ff]
    grad_a_in = expert_sum[:, : ends[0]].reshape(local_count, 2, own_width, rank_columns)
    grad_a_down = expert_sum[:, ends[0] : ends[1]]
    grad_b_in = columns(expert_sum[:, ends[1] : ends[2]], 2)
    grad_b_down = columns(expert_sum[:, ends[2] :], 1)[:, 0]
    return (
        layer_output,
        input_grad,
        grad_a_attention,
        grad_b_attention,
        grad_a_in,
        grad_b_in,
        grad_a_down,
        grad_b_down,
    )


def solution(mesh):
    return jax.shard_map(
        local,
        mesh=mesh,
        in_specs=(
            P("dp", "seq", None),
            P("dp", "seq", None),
            P(),
            P(),
            P(),
            P(),
            P(None, None, ("seq", "dp")),
            P(("seq", "dp"), None),
            P(None, ("seq", "dp"), None),
            P(None, None, ("seq", "dp")),
            P("dp", None, None, None),
            P("dp", None, None),
            P("dp", None, None, None),
            P("dp", None, None, None),
            P("dp", None, None),
            P("dp", None, None),
            P("dp", "seq", None),
            P("dp", "seq", None),
            P("dp", None),
            P("dp", None),
        ),
        out_specs=(
            P("dp", "seq", None),
            P("dp", "seq", None),
            P(None, ("seq", "dp"), None),
            P(None, None, ("seq", "dp")),
            P("dp", None, "seq", None),
            P("dp", None, None, "seq"),
            P("dp", "seq", None),
            P("dp", None, "seq"),
        ),
        check_vma=False,
    )
```

```python
import functools

import jax
import jax.numpy as jnp
from jax import lax
from jax.experimental import pallas as pl
from jax.experimental.pallas import tpu as pltpu
from jax.sharding import PartitionSpec as P

H = 16
HD = 128
TOP = 8
R = 16


norm_epsilon = 1e-06
rope_base = 10000.0
masked_score = -1000000000.0
half_from = 200000


def rms_scale(values, gain_vector):
    return (
        values
        * lax.rsqrt(jnp.mean(values * values, axis=-1, keepdims=True) + norm_epsilon)
        * gain_vector
    )


def rope_tables(offset, width):
    half = width // 2
    frequency = rope_base ** (-(jnp.arange(half, dtype=jnp.float32) * 2.0) / width)
    angles = offset.astype(jnp.float32)[:, None] * frequency[None, :]
    cosine = jnp.cos(angles)
    sine = jnp.sin(angles)
    return jnp.concatenate([cosine, cosine], axis=1), jnp.concatenate([-sine, sine], axis=1)


def dot_nn(a, b):
    return lax.dot_general(a, b, (((1,), (0,)), ((), ())), preferred_element_type=jnp.float32)


def dot_nt(a, b):
    return lax.dot_general(a, b, (((1,), (1,)), ((), ())), preferred_element_type=jnp.float32)


def dot_tn(a, b):
    return lax.dot_general(a, b, (((0,), (0,)), ((), ())), preferred_element_type=jnp.float32)


def normed_head(raw, gain):
    inverse = lax.rsqrt(jnp.mean(raw * raw, axis=-1, keepdims=True) + norm_epsilon)
    return raw * inverse * gain, inverse


def turned_head(values, cosine, sine):
    return values * cosine + pltpu.roll(values, values.shape[-1] // 2, 1) * sine


def unturned_head(grad, cosine, sine):
    return grad * cosine + pltpu.roll(grad * sine, grad.shape[-1] // 2, 1)


def attend_kernel(
    tile, q_raw, k_raw, v_raw, cosine, sine, gain_q, gain_k, seg_col, seg_row, mixed, query, key, value, stat
):
    rows = q_raw.shape[0]
    scale = HD ** (-0.5)
    cos_all = cosine[...]
    sin_all = sine[...]
    normed_q, unused = normed_head(q_raw[...], gain_q[...])
    query[...] = turned_head(normed_q, cos_all, sin_all).astype(jnp.bfloat16)
    normed_k, unused = normed_head(k_raw[...], gain_k[...])
    keys = turned_head(normed_k, cos_all, sin_all).astype(jnp.bfloat16)
    key[...] = keys
    values = v_raw[...].astype(jnp.bfloat16)
    value[...] = values
    values_t = values.T
    for start in range(0, rows, tile):
        part = slice(start, start + tile)
        scores = dot_nt(keys, query[part, :]) * scale
        scores = jnp.where(seg_col[...] == seg_row[:, part], scores, masked_score)
        top = jnp.max(scores, axis=0, keepdims=True)
        weight = jnp.exp(scores - top)
        total = jnp.sum(weight, axis=0, keepdims=True)
        soft = (weight * (1.0 / total)).astype(jnp.bfloat16)
        mixed[part, :] = dot_nn(values_t, soft).T.astype(jnp.bfloat16)
        stat[0, :, part] = top + jnp.log(total)


def attend(raw, cosine, sine, gain_q, gain_k, segment):
    unused, length, width = raw.shape
    heads = width // HD
    tile = min(256, length)
    head = pl.BlockSpec((length, HD), lambda h: (0, h))
    raw_head = [pl.BlockSpec((None, length, HD), functools.partial(lambda m, h: (m, 0, h), m)) for m in range(3)]
    fixed = lambda shape: pl.BlockSpec(shape, lambda h: (0, 0))
    seg = segment.astype(jnp.float32)
    low = jax.ShapeDtypeStruct((length, width), jnp.bfloat16)
    return pl.pallas_call(
        functools.partial(attend_kernel, tile),
        grid=(heads,),
        in_specs=raw_head + [fixed((length, HD)), fixed((length, HD)), fixed((1, HD)), fixed((1, HD)),
                  fixed((length, 1)), fixed((1, length))],
        out_specs=[head, head, head, head, pl.BlockSpec((1, 1, length), lambda h: (h, 0, 0))],
        out_shape=[low, low, low, low, jax.ShapeDtypeStruct((heads, 1, length), jnp.float32)],
        cost_estimate=pl.CostEstimate(
            flops=4 * heads * length * length * HD, bytes_accessed=20 * length * width, transcendentals=heads * length * length
        ),
        name="attend",
    )(raw, raw, raw, cosine, sine, gain_q[None, :], gain_k[None, :], seg[:, None], seg[None, :])


def attend_back_kernel(
    tile, query, key, value, grad_mixed, stat, q_raw, k_raw, cosine, sine, gain_q, gain_k, seg_col, seg_row,
    grad_q, grad_k, grad_v, sum_k, sum_v
):
    rows = q_raw.shape[0]
    scale = HD ** (-0.5)
    keys = key[...]
    values = value[...]
    keys_t = keys.T

    def through(grad, raw_ref, gain_ref, part):
        grad = grad.astype(jnp.bfloat16).astype(jnp.float32)
        raw = raw_ref[part, :]
        gain = gain_ref[...]
        inverse = lax.rsqrt(jnp.mean(raw * raw, axis=-1, keepdims=True) + norm_epsilon)
        grad = unturned_head(grad, cosine[part, :], sine[part, :]) * gain
        dots = jnp.mean(grad * raw, axis=-1, keepdims=True)
        return (inverse * (grad - raw * (inverse * inverse * dots))).astype(jnp.bfloat16)

    for start in range(0, rows, tile):
        part = slice(start, start + tile)
        queries = query[part, :]
        grads = grad_mixed[part, :]
        scores = dot_nt(keys, queries) * scale
        scores = jnp.where(seg_col[...] == seg_row[:, part], scores, masked_score)
        soft = jnp.exp(scores - stat[0, :, part])
        grad_soft = dot_nt(values, grads)
        delta = jnp.sum(soft * grad_soft, axis=0, keepdims=True)
        grad_scores = (soft * (grad_soft - delta)).astype(jnp.bfloat16)
        term_k = dot_nn(grad_scores, queries)
        term_v = dot_nn(soft.astype(jnp.bfloat16), grads)
        if start == 0:
            sum_k[...] = term_k
            sum_v[...] = term_v
        else:
            sum_k[...] += term_k
            sum_v[...] += term_v
        grad_q[part, :] = through(dot_nn(keys_t, grad_scores).T * scale, q_raw, gain_q, part)
    for start in range(0, rows, tile):
        part = slice(start, start + tile)
        grad_k[part, :] = through(sum_k[part, :] * scale, k_raw, gain_k, part)
        grad_v[part, :] = sum_v[part, :].astype(jnp.bfloat16)


def attend_back(kept, grad_mixed, raw, cosine, sine, gain_q, gain_k, segment):
    query, key, value, stat = kept
    unused, length, width = raw.shape
    heads = width // HD
    tile = min(256, length)
    head = pl.BlockSpec((length, HD), lambda h: (0, h))
    raw_head = [pl.BlockSpec((None, length, HD), functools.partial(lambda m, h: (m, 0, h), m)) for m in range(3)]
    fixed = lambda shape: pl.BlockSpec(shape, lambda h: (0, 0))
    seg = segment.astype(jnp.float32)
    low = jax.ShapeDtypeStruct((length, width), jnp.bfloat16)
    return pl.pallas_call(
        functools.partial(attend_back_kernel, tile),
        grid=(heads,),
        in_specs=[head, head, head, head, pl.BlockSpec((1, 1, length), lambda h: (h, 0, 0)), raw_head[0], raw_head[1],
                  fixed((length, HD)), fixed((length, HD)), fixed((1, HD)), fixed((1, HD)),
                  fixed((length, 1)), fixed((1, length))],
        out_specs=[head, head, head],
        out_shape=[low, low, low],
        scratch_shapes=[pltpu.VMEM((length, HD), jnp.float32), pltpu.VMEM((length, HD), jnp.float32)],
        cost_estimate=pl.CostEstimate(
            flops=heads * length * HD, bytes_accessed=length * width, transcendentals=0
        ),
        name="attend_back",
    )(query, key, value, grad_mixed, stat, raw, raw, cosine, sine, gain_q[None, :], gain_k[None, :],
      seg[:, None], seg[None, :])


def doc_layout(lengths, chosen, position):
    slots = jnp.arange(lengths.shape[0], dtype=jnp.int32)
    doc_ends = jnp.sum(jnp.where(slots[:, None] >= slots[None, :], lengths[None, :], 0), axis=1)
    starts = doc_ends - lengths
    segment = jnp.sum((position[:, None] >= doc_ends[None, :]).astype(jnp.int32), axis=1)
    doc_pick = (segment[:, None] == slots[None, :]).astype(jnp.int32)
    offset = position - jnp.sum(doc_pick * starts[None, :], axis=1)
    adapter = jnp.sum(doc_pick * chosen[None, :], axis=1)
    return (segment, offset, adapter)


def column_mask(adapter, columns):
    groups = jnp.arange(columns, dtype=jnp.int32) // R
    return (groups[None, :] == adapter[:, None]).astype(jnp.float32)


def qkv_kernel(x_ref, reduced_ref, w_ref, up_ref, out_ref):
    width = w_ref.shape[0] * w_ref.shape[1]
    weights = w_ref[...].reshape(width, x_ref.shape[1])
    out_ref[0] = dot_nt(x_ref[...], weights) + dot_nt(reduced_ref[...], up_ref[0])


def qkv_project(normed_all, reduced_cat, w_group, up_group):
    length, width = normed_all.shape
    dp_count, unused, piece, unused = w_group.shape
    group = dp_count * piece
    rank = up_group.shape[2]
    half = dp_count // 2
    return pl.pallas_call(
        qkv_kernel,
        grid=(3, 2),
        in_specs=[
            pl.BlockSpec((length, width), lambda m, p: (0, 0)),
            pl.BlockSpec((length, rank), lambda m, p: (0, m)),
            pl.BlockSpec((half, None, piece, width), lambda m, p: (p, m, 0, 0)),
            pl.BlockSpec((1, group // 2, rank), lambda m, p: (m, p, 0)),
        ],
        out_specs=pl.BlockSpec((1, length, group // 2), lambda m, p: (m, 0, p)),
        out_shape=jax.ShapeDtypeStruct((3, length, group), jnp.float32),
        cost_estimate=pl.CostEstimate(
            flops=6 * length * width * group, bytes_accessed=2 * length * width + 12 * length * group + 6 * group * width,
            transcendentals=0,
        ),
        name="qkv_project",
    )(normed_all, reduced_cat, w_group, up_group)


def qkv_back_kernel(a_ref, b_ref, c_ref, w_ref, out_ref):
    dp_count, unused, piece, cols = w_ref.shape
    total = None
    for m, ref in enumerate((a_ref, b_ref, c_ref)):
        term = dot_nn(ref[...], w_ref[:, m].reshape(dp_count * piece, cols))
        total = term if total is None else total + term
    out_ref[...] = total.astype(jnp.bfloat16)


def qkv_back(grads, w_group):
    length, group = grads[0].shape
    dp_count, unused, piece, width = w_group.shape
    tile = min(256, width)
    whole = pl.BlockSpec((length, group), lambda i: (0, 0))
    return pl.pallas_call(
        qkv_back_kernel,
        grid=(width // tile,),
        in_specs=[whole, whole, whole, pl.BlockSpec((dp_count, 3, piece, tile), lambda i: (0, 0, 0, i))],
        out_specs=pl.BlockSpec((length, tile), lambda i: (0, i)),
        out_shape=jax.ShapeDtypeStruct((length, width), jnp.bfloat16),
        cost_estimate=pl.CostEstimate(flops=length * width, bytes_accessed=length * width, transcendentals=0),
        name="qkv_back",
    )(grads[0], grads[1], grads[2], w_group)


def expert_kernel(kept_in, which, *refs):
    (x_a, x_b, g_both, pick, pick_t, slot, w_in, w_down, a_in, b_in, a_down, b_down) = refs[:12]
    refs = refs[12 + kept_in:]
    (out_both, back_a, back_b, xs, ps, act_o, gate_o, up_o, reds) = refs[:9]
    (red_g, red_u, gred_d, down_acc, down_red, gx_acc, gred_g, gred_u, sum_out_a, sum_out_b, sum_back_a, sum_back_b) = refs[9:]
    low = jnp.bfloat16
    e = pl.program_id(0)
    f = pl.program_id(1)
    last = pl.num_programs(1) - 1
    cap = pick.shape[2]
    rank = a_in.shape[3]
    rows = xs.shape[1]
    groups = lax.shift_right_logical(lax.broadcasted_iota(jnp.int32, (rows, rank), 1), R.bit_length() - 1)
    mask = jnp.where(groups.astype(jnp.float32) == slot[0, :, 1:2], 1.0, 0.0)

    @pl.when(f == 0)
    def _():
        for b, x_ref in enumerate((x_a, x_b)):
            part = slice(b * cap, (b + 1) * cap)
            g_place = which[1] if b == 0 else 1 - which[1]
            xs[0, part, :] = dot_nn(pick[0, b], x_ref[...]).astype(low)
            ps[0, part, :] = (slot[0, part, 0:1] * dot_nn(pick[0, b], g_both[g_place])).astype(low)
        red_g[...] = (mask * dot_nn(xs[0], a_in[0, 0])).astype(low)
        red_u[...] = (mask * dot_nn(xs[0], a_in[0, 1])).astype(low)
        gred_d[...] = (mask * dot_nt(ps[0], b_down[0])).astype(low)

    x = xs[0]
    p = ps[0]
    gate = dot_nn(x, w_in[0, 0]) + dot_nn(red_g[...], b_in[0, 0])
    up = dot_nn(x, w_in[0, 1]) + dot_nn(red_u[...], b_in[0, 1])
    grad_act = dot_nt(p, w_down[0]) + dot_nt(gred_d[...], a_down[0])
    sigma = 1.0 / (1.0 + jnp.exp(-gate))
    silu = gate * sigma
    act = (silu * up).astype(low)
    grad_gate = (grad_act * up * (sigma * (1.0 + gate * (1.0 - sigma)))).astype(low)
    grad_up = (grad_act * silu).astype(low)
    act_o[0] = act
    gate_o[0] = grad_gate
    up_o[0] = grad_up
    down_term = dot_nn(act, w_down[0])
    down_red_term = dot_nn(act, a_down[0])
    gx_term = dot_nt(grad_gate, w_in[0, 0]) + dot_nt(grad_up, w_in[0, 1])
    gred_g_term = dot_nt(grad_gate, b_in[0, 0])
    gred_u_term = dot_nt(grad_up, b_in[0, 1])

    @pl.when(f == 0)
    def _():
        down_acc[...] = down_term
        down_red[...] = down_red_term
        gx_acc[...] = gx_term
        gred_g[...] = gred_g_term
        gred_u[...] = gred_u_term

    @pl.when(f > 0)
    def _():
        down_acc[...] += down_term
        down_red[...] += down_red_term
        gx_acc[...] += gx_term
        gred_g[...] += gred_g_term
        gred_u[...] += gred_u_term

    @pl.when(f == last)
    def _():
        reduced_d = (mask * down_red[...]).astype(low)
        back_g = (mask * gred_g[...]).astype(low)
        back_u = (mask * gred_u[...]).astype(low)
        for i, value in enumerate((red_g[...], red_u[...], reduced_d, back_g, back_u, gred_d[...])):
            reds[0, :, i * rank : (i + 1) * rank] = value
        produced = down_acc[...] + dot_nn(reduced_d, b_down[0])
        scaled = (slot[0, :, 0:1] * produced).astype(low)
        grads = (gx_acc[...] + dot_nt(back_g, a_in[0, 0]) + dot_nt(back_u, a_in[0, 1])).astype(low)
        for b, (out_sum, back_ref, back_sum) in enumerate(
            ((sum_out_a, back_a, sum_back_a), (sum_out_b, back_b, sum_back_b))
        ):
            part = slice(b * cap, (b + 1) * cap)
            out_ref = out_both.at[which[3] if b == 0 else 1 - which[3]]
            for values, total, result in ((scaled, out_sum, out_ref), (grads, back_sum, back_ref)):
                term = dot_nn(pick_t[0, b], values[part, :])

                @pl.when(e == 0)
                def _():
                    total[...] = term

                @pl.when(e > 0)
                def _():
                    total[...] += term

                @pl.when(e == pl.num_programs(0) - 1)
                def _():
                    result[...] = total[...].astype(low)


def run_experts(which, x_pair, g_all, pick, pick_t, slot, weights, kept):
    w_in, w_down, a_in, b_in, a_down, b_down = weights
    experts, unused, width, ff = w_in.shape
    unused, dp_count, cap, own_rows = pick.shape
    rank = a_down.shape[2]
    rows = 2 * cap
    tile = min(256, ff)
    low = jnp.bfloat16
    f32 = jnp.float32
    one = pl.Buffered(1)
    token = pl.BlockSpec((own_rows, width), lambda e, f, w: (0, 0), pipeline_mode=one)
    stored = [
        ((experts, dp_count * cap, width), (1, rows, width), lambda e, f, w: (e, w[4], 0)),
        ((experts, dp_count * cap, width), (1, rows, width), lambda e, f, w: (e, w[4], 0)),
        ((experts, dp_count * cap, ff), (1, rows, tile), lambda e, f, w: (e, w[4], f)),
        ((experts, dp_count * cap, ff), (1, rows, tile), lambda e, f, w: (e, w[4], f)),
        ((experts, dp_count * cap, ff), (1, rows, tile), lambda e, f, w: (e, w[4], f)),
        ((experts, dp_count * cap, 6 * rank), (1, rows, 6 * rank), lambda e, f, w: (e, w[4], 0)),
    ]
    in_specs = [
        token, token, pl.BlockSpec((2, own_rows, width), lambda e, f, w: (w[0], 0, 0), pipeline_mode=one),
        pl.BlockSpec((1, 2, cap, own_rows), lambda e, f, w: (e, w[4], 0, 0)),
        pl.BlockSpec((1, 2, own_rows, cap), lambda e, f, w: (e, w[4], 0, 0)),
        pl.BlockSpec((1, rows, 2), lambda e, f, w: (e, w[4], 0)),
        pl.BlockSpec((1, 2, width, tile), lambda e, f, w: (e, 0, 0, f)),
        pl.BlockSpec((1, tile, width), lambda e, f, w: (e, f, 0)),
        pl.BlockSpec((1, 2, width, rank), lambda e, f, w: (e, 0, 0, 0)),
        pl.BlockSpec((1, 2, rank, tile), lambda e, f, w: (e, 0, 0, f)),
        pl.BlockSpec((1, tile, rank), lambda e, f, w: (e, f, 0)),
        pl.BlockSpec((1, rank, width), lambda e, f, w: (e, 0, 0)),
    ] + [pl.BlockSpec(memory_space=pl.ANY) for unused in kept]
    part = jax.ShapeDtypeStruct((own_rows, width), low)
    results = pl.pallas_call(
        functools.partial(expert_kernel, len(kept)),
        grid_spec=pltpu.PrefetchScalarGridSpec(
            num_scalar_prefetch=1,
            grid=(experts, ff // tile),
            in_specs=in_specs,
            out_specs=[pl.BlockSpec((2, own_rows, width), lambda e, f, w: (w[2], 0, 0), pipeline_mode=one), token, token]
            + [pl.BlockSpec(block, index) for unused, block, index in stored],
            scratch_shapes=[
            pltpu.VMEM((rows, rank), low),
            pltpu.VMEM((rows, rank), low),
            pltpu.VMEM((rows, rank), low),
            pltpu.VMEM((rows, width), f32),
            pltpu.VMEM((rows, rank), f32),
            pltpu.VMEM((rows, width), f32),
            pltpu.VMEM((rows, rank), f32),
            pltpu.VMEM((rows, rank), f32),
        ] + [pltpu.VMEM((own_rows, width), f32) for unused in range(4)],
        ),
        out_shape=[jax.ShapeDtypeStruct((dp_count, own_rows, width), low)] + [part] * 2 + [jax.ShapeDtypeStruct(shape, low) for shape, unused, unused2 in stored],
        input_output_aliases={13 + i: 0 if i == 0 else 2 + i for i in range(len(kept))},
        cost_estimate=pl.CostEstimate(
            flops=experts * rows * width, bytes_accessed=experts * rows * width, transcendentals=0
        ),
        compiler_params=pltpu.CompilerParams(vmem_limit_bytes=60 * 1024 * 1024),
        name="experts",
    )(which, *x_pair, g_all, pick, pick_t, slot, *weights, *kept)
    return results[1:3], [results[0]] + list(results[3:])


def adapter_kernel(which, xs, ps, act, gate, up, reds, out):
    rank = out.shape[3]
    red = [reds[0, :, i * rank : (i + 1) * rank] for i in range(6)]
    into = dot_tn(xs[0], reds[0, :, 3 * rank : 5 * rank])
    parts = [into[:, :rank], into[:, rank:], dot_tn(act[0], red[5])]
    for wide in (dot_tn(red[0], gate[0]), dot_tn(red[1], up[0]), dot_tn(red[2], ps[0])):
        parts += [wide[:, i : i + rank] for i in range(0, wide.shape[1], rank)]
    start = 0
    for part in parts:
        out[0, 0, start : start + part.shape[0], :] = part.astype(jnp.bfloat16)
        start += part.shape[0]


def adapter_grads(kept, order):
    xs, ps, act, gate, up, reds = kept
    experts, rows, width = xs.shape
    ff = act.shape[2]
    n = order.shape[0]
    rank = reds.shape[2] // 6
    total = (3 * width + 3 * ff) // n
    wide = pl.BlockSpec((1, rows, width // n), lambda e, k, w: (e, 0, w[k]))
    narrow = pl.BlockSpec((1, rows, ff // n), lambda e, k, w: (e, 0, w[k]))
    return pl.pallas_call(
        adapter_kernel,
        grid_spec=pltpu.PrefetchScalarGridSpec(
            num_scalar_prefetch=1,
            grid=(experts, n),
            in_specs=[wide, wide, narrow, narrow, narrow, pl.BlockSpec((1, rows, 6 * rank), lambda e, k, w: (e, 0, 0))],
            out_specs=pl.BlockSpec((1, 1, total, rank), lambda e, k, w: (k, e, 0, 0)),
        ),
        out_shape=jax.ShapeDtypeStruct((n, experts, total, rank), jnp.bfloat16),
        cost_estimate=pl.CostEstimate(flops=rows * width, bytes_accessed=rows * width, transcendentals=0),
        name="adapter_grads",
    )(order, xs, ps, act, gate, up, reds)


def swap(values, axis, distance, count):
    return lax.ppermute(values, axis, [(i, i ^ distance) for i in range(count)])


def near(values, axis, count):
    return [swap(values, axis, 1, count), swap(values, axis, 2, count)]


def spread(values, axis, count, close=None):
    one, two = near(values, axis, count) if close is None else close
    if count == 4 and values.size >= half_from:
        half = values.shape[0] // 2
        three = [swap(two[:half], axis, 1, count), swap(one[half:], axis, 2, count)]
        return [values, one, two, jnp.concatenate(three, axis=0)]
    return [values, one, two] + [swap(values, axis, k, count) for k in range(3, count)]


def collect_begin(blocks, axis, count):
    if count == 4 and blocks[0].size >= half_from:
        half = blocks[0].shape[0] // 2
        return [
            swap(blocks[3][:half], axis, 1, count),
            swap(blocks[3][half:], axis, 2, count),
            swap(blocks[1][:half], axis, 1, count),
            swap(blocks[2][half:], axis, 2, count),
        ]
    return [swap(blocks[k], axis, k, count) for k in range(1, count)]


def collect_turn(blocks, arrived, axis, count):
    if count == 4 and blocks[0].size >= half_from:
        half = blocks[0].shape[0] // 2
        to_two = (blocks[2][:half].astype(jnp.float32) + arrived[0].astype(jnp.float32)).astype(blocks[2].dtype)
        to_one = (blocks[1][half:].astype(jnp.float32) + arrived[1].astype(jnp.float32)).astype(blocks[1].dtype)
        to_two, to_one = pin(to_two, to_one)
        return [swap(to_two, axis, 2, count), swap(to_one, axis, 1, count)]
    return []


def collect_end(blocks, arrived, turned, axis, count):
    f32 = jnp.float32
    if turned:
        half = blocks[0].shape[0] // 2
        top = blocks[0][:half].astype(f32) + arrived[2].astype(f32) + turned[0].astype(f32)
        low = blocks[0][half:].astype(f32) + arrived[3].astype(f32) + turned[1].astype(f32)
        return jnp.concatenate([top, low], axis=0)
    return sum((x.astype(f32) for x in arrived), blocks[0].astype(f32))


def collect(blocks, axis, count):
    arrived = collect_begin(blocks, axis, count)
    return collect_end(blocks, arrived, collect_turn(blocks, arrived, axis, count), axis, count)


def collect_chips(blocks, count):
    pairs = blocks.reshape((count // 2, 2) + blocks.shape[1:])
    summed = pairs[:, 0].astype(jnp.float32) + swap(pairs[:, 1], "dp", 1, count).astype(jnp.float32)
    total = summed[0]
    summed = summed.astype(blocks.dtype)
    for c in range(1, count // 2):
        total = total + swap(summed[c], "dp", 2 * c, count).astype(jnp.float32)
    return total


def pin(*values):
    return lax.optimization_barrier(values)


def local(
    layer_input,
    out_cotangent,
    gain_attention,
    gain_query,
    gain_key,
    gain_ffn,
    w_qkv,
    w_output,
    a_attention,
    b_attention,
    expert_w_in,
    expert_w_down,
    expert_a_in,
    expert_b_in,
    expert_a_down,
    expert_b_down,
    route_experts,
    route_gates,
    doc_lengths,
    adapter_ids,
):
    low = jnp.bfloat16
    f32 = jnp.float32
    own_rows = layer_input.shape[1]
    full_width = layer_input.shape[2]
    n = lax.axis_size("seq")
    dp_count = lax.axis_size("dp")
    s = lax.axis_index("seq")
    d = lax.axis_index("dp")
    length = own_rows * n
    rank_columns = a_attention.shape[2]
    group_width = full_width // n
    group_heads = H // n
    piece = group_width // dp_count
    group_start = s * group_width
    order = s ^ jnp.arange(n, dtype=jnp.int32)
    position = (order[:, None] * own_rows + jnp.arange(own_rows, dtype=jnp.int32)[None, :]).reshape(-1)
    segment, offset, adapter = doc_layout(doc_lengths[0], adapter_ids[0], position)
    own_adapter = adapter[:own_rows]
    own_mask = column_mask(own_adapter, rank_columns)
    full_mask = column_mask(adapter, rank_columns)

    gates = route_gates[0].T
    gates_high = gates.astype(low)
    meta = jnp.concatenate(
        [
            route_experts[0].T.astype(low),
            gates_high,
            (gates - gates_high.astype(f32)).astype(low),
            own_adapter[None, :].astype(low),
            jnp.zeros((7, own_rows), low),
        ],
        axis=0,
    )
    ab_piece = jnp.concatenate([a_attention[0:3], jnp.swapaxes(b_attention, 1, 2)], axis=0).reshape(-1, rank_columns)
    ab_rows = ab_piece.shape[0]
    ab_piece = jnp.concatenate([ab_piece, meta.reshape(-1, rank_columns)], axis=0)
    ab_got = lax.all_gather(ab_piece, "dp", axis=0)
    tokens = layer_input[0].astype(f32)
    normed = rms_scale(tokens, gain_attention).astype(low)
    wt_piece = jnp.swapaxes(w_qkv, 1, 2)
    wt_piece, ab_got, *close = pin(wt_piece, ab_got, *near(normed, "seq", n))
    w_group = lax.all_gather(wt_piece, "dp", axis=0)
    dp_order = d ^ jnp.arange(dp_count, dtype=jnp.int32)
    meta_all = ab_got[:, ab_rows:].reshape((dp_count,) + meta.shape)[dp_order].astype(f32)
    ab_group = ab_got[:, :ab_rows].reshape(dp_count, 7, piece, rank_columns)
    ab_group = jnp.swapaxes(ab_group, 0, 1).reshape(7, group_width, rank_columns)
    local_count = expert_w_in.shape[0]
    expert_count = local_count * dp_count
    capacity = own_rows * TOP // expert_count * 9 // 8
    capacity = -(-capacity // 16) * 16
    named = meta_all[:, 0:TOP, :].astype(jnp.int32)
    gates_all = meta_all[:, TOP : 2 * TOP, :] + meta_all[:, 2 * TOP : 3 * TOP, :]
    sets_all = meta_all[:, 3 * TOP, :]
    mine = d * local_count + jnp.arange(local_count, dtype=jnp.int32)
    hit = (named[None] == mine[:, None, None, None]).astype(f32)
    member = jnp.sum(hit, axis=2)
    token_gate = jnp.sum(hit * gates_all[None], axis=2)
    t_index = jnp.arange(own_rows, dtype=jnp.int32)
    upto = (t_index[:, None] <= t_index[None, :]).astype(low)
    rank = jnp.einsum("ejt,tu->eju", member.astype(low), upto, preferred_element_type=f32) - 1.0
    slots = jnp.arange(capacity, dtype=jnp.int32).astype(f32)
    rank = jnp.where(member > 0.5, rank, -1.0)
    pick = slots[None, None, :, None] == rank[:, :, None, :]
    pick_t = (rank[:, :, :, None] == slots[None, None, None, :]).astype(low)
    slot_gate = jnp.sum(jnp.where(pick, token_gate[:, :, None, :], 0.0), axis=-1)
    slot_set = jnp.sum(jnp.where(pick, sets_all[None, :, None, :], 0.0), axis=-1)
    slot = jnp.stack([slot_gate, slot_set], axis=-1).reshape(local_count, dp_count * capacity, 2)
    pick = pick.astype(low)

    cosine, sine = rope_tables(offset, HD)

    dot = lambda a, b: jnp.dot(a, b, preferred_element_type=f32)
    dot_t = lambda a, b: lax.dot_general(a, b, (((1,), (1,)), ((), ())), preferred_element_type=f32)
    dot_l = lambda a, b: lax.dot_general(a, b, (((0,), (0,)), ((), ())), preferred_element_type=f32)

    share = jnp.concatenate([ab_group[0:3], ab_group[6:7]], axis=0)
    share_full = jnp.stack(spread(share, "seq", n))[order]
    share_full = jnp.swapaxes(share_full, 0, 1).reshape(4, full_width, rank_columns)
    down_cat = jnp.swapaxes(share_full[0:3], 0, 1).reshape(full_width, 3 * rank_columns)
    upt_output = share_full[3]
    upt_group = ab_group[3:6]
    normed_all = jnp.concatenate(spread(normed, "seq", n, close), axis=0)
    reduced_cat = (jnp.tile(full_mask, (1, 3)) * dot(normed_all, down_cat)).astype(low)
    out_piece = jnp.concatenate([w_output, a_attention[3]], axis=1)
    out_piece, w_group, pick, pick_t, slot, cosine, sine, normed_all, reduced_cat, upt_group, upt_output = pin(
        out_piece, w_group, pick, pick_t, slot, cosine, sine, normed_all, reduced_cat, upt_group, upt_output
    )
    out_maps = lax.all_gather(out_piece, "dp", axis=0, tiled=True)
    reduced_list = [reduced_cat[:, m * rank_columns : (m + 1) * rank_columns] for m in range(3)]
    raw = qkv_project(normed_all, reduced_cat, w_group, upt_group)
    grad_send, raw = pin(out_cotangent[0], raw)
    grad_got = lax.all_gather(grad_send, "dp", axis=0)
    grad_own = jnp.stack([out_cotangent[0], swap(out_cotangent[0], "dp", 1, dp_count)])
    mixed_group, query_heads, key_heads, value_heads, stat = attend(
        raw, cosine, sine, gain_query, gain_key, segment
    )

    partial_out = dot(mixed_group, out_maps).astype(low).reshape(n, own_rows, full_width + rank_columns)
    summed = collect([partial_out[k] for k in range(n)], "seq", n)
    output_reduced = (own_mask * summed[:, full_width:]).astype(low)
    attended = summed[:, :full_width] + dot_t(output_reduced, upt_output)
    hidden = tokens + attended
    normed_ffn = rms_scale(hidden, gain_ffn).astype(low)
    weights = (expert_w_in, expert_w_down, expert_a_in, expert_b_in, expert_a_down, expert_b_down)
    chips = dp_count // 2
    turns = [0] + list(range(chips // 2, chips)) + list(range(1, chips // 2))
    kept = ()
    rows = normed_ffn
    here = normed_ffn
    arrived = swap(rows, "dp", 2 * turns[1], dp_count)
    other = swap(here, "dp", 1, dp_count)
    leaving = None
    flying = None
    grad_normed_ffn = None
    for i, c in enumerate(turns):
        if i > 0:
            here = arrived
            if flying is not None:
                here, flying = pin(here, flying)
                grad_normed_ffn = grad_normed_ffn + flying.astype(f32)
            other = swap(here, "dp", 1, dp_count)
            rows, here, other, leaving = pin(rows, here, other, leaving)
            if i < chips - 1:
                arrived = swap(rows, "dp", 2 * turns[i + 1], dp_count)
            if i == 1:
                grad_normed_ffn = leaving
            else:
                flying = swap(leaving, "dp", 2 * turns[i - 1], dp_count)
        block = lax.shift_right_logical(d, 1) ^ c
        place = d & 1
        which = jnp.stack(([block, place] if c else [0 * d, 0 * d]) + [block, place, 0 * d + c]).astype(jnp.int32)
        (back, back_other), kept = run_experts(
            which, (here, other), grad_got if c else grad_own, pick, pick_t, slot, weights, kept
        )
        if i == chips - 1 and flying is not None:
            flying, back_other = pin(flying, back_other)
        leaving = back.astype(f32) + swap(back_other, "dp", 1, dp_count).astype(f32)
        if i > 0:
            leaving = leaving.astype(low)
    if flying is not None:
        grad_normed_ffn = grad_normed_ffn + flying.astype(f32)
    outs_all, *kept = kept
    leaving, *kept = pin(leaving, *kept)
    flying = swap(leaving, "dp", 2 * turns[-1], dp_count)
    flat = adapter_grads(kept, order)
    flat, flying = pin(flat, flying)
    grad_normed_ffn = grad_normed_ffn + flying.astype(f32)

    outs_all, grad_normed_ffn = pin(outs_all, grad_normed_ffn)
    mixture = lax.psum_scatter(outs_all, "dp", scatter_dimension=0)
    grad_out = out_cotangent[0].astype(f32)
    unused, pull_ffn = jax.vjp(lambda values: rms_scale(values, gain_ffn), hidden)
    grad_hidden = grad_out + pull_ffn(grad_normed_ffn)[0]
    grad_hidden_low = grad_hidden.astype(low)
    grad_reduced_output = (own_mask * dot(grad_hidden_low, upt_output)).astype(low)
    grad_pack = jnp.concatenate([grad_hidden_low, grad_reduced_output, output_reduced], axis=1)
    flat, *grad_packs = pin(flat, *spread(grad_pack, "seq", n))
    expert_terms = [flat[k] for k in range(n)]
    expert_arrived = collect_begin(expert_terms, "seq", n)
    grad_pack_all = jnp.concatenate(grad_packs, axis=0)
    grad_all = grad_pack_all[:, :full_width]
    grad_reduced_all = grad_pack_all[:, full_width : full_width + rank_columns]
    output_reduced_all = grad_pack_all[:, full_width + rank_columns :]
    grad_mixed_group = dot_t(grad_pack_all[:, : full_width + rank_columns], out_maps).astype(low)
    grad_cols = lax.dynamic_slice_in_dim(grad_all, group_start, group_width, 1)
    grad_upt_output = dot_l(grad_cols, output_reduced_all)
    grad_down_output = dot_l(mixed_group, grad_reduced_all)
    grad_raw_list = attend_back(
        (query_heads, key_heads, value_heads, stat),
        grad_mixed_group,
        raw,
        cosine,
        sine,
        gain_query,
        gain_key,
        segment,
    )
    pinned = pin(*grad_raw_list, *expert_arrived)
    grad_raw_list = list(pinned[:3])
    expert_arrived = pinned[3:]
    expert_turned = collect_turn(expert_terms, expert_arrived, "seq", n)
    partial_reduced = jnp.concatenate(
        [dot(grad_raw_list[m], upt_group[m]) for m in range(3)], axis=1
    ).astype(low)
    partial_reduced, *grad_raw_list = pin(partial_reduced, *grad_raw_list)
    partial_reduced = partial_reduced.reshape(n, own_rows, 3 * rank_columns)
    summed_reduced = collect([partial_reduced[k] for k in range(n)], "seq", n)
    grad_reduced = (jnp.tile(own_mask, (1, 3)) * summed_reduced).astype(low)
    grad_reduced, *grad_raw_late = pin(grad_reduced, *grad_raw_list)
    grad_reduced_full = jnp.concatenate(spread(grad_reduced, "seq", n), axis=0)
    partial_normed = qkv_back(grad_raw_list, w_group).reshape(n, own_rows, full_width)
    partial_normed, grad_reduced, *expert_turned = pin(partial_normed, grad_reduced, *expert_turned)
    expert_sum = collect_end(expert_terms, expert_arrived, expert_turned, "seq", n)
    grad_upt = [dot_l(grad_raw_late[m], reduced_list[m]) for m in range(3)]
    normed_cols = lax.dynamic_slice_in_dim(normed_all, group_start, group_width, 1)
    grad_down_cat = dot_l(normed_cols, grad_reduced_full)
    parts = [grad_down_cat[:, m * rank_columns : (m + 1) * rank_columns] for m in range(3)]
    piled = lambda some: jnp.stack([x.astype(low).reshape(dp_count, piece, rank_columns) for x in some], axis=1)
    early_parts = piled([grad_down_output] + grad_upt + [grad_upt_output])
    early_parts = lax.psum_scatter(early_parts, "dp", scatter_dimension=0)
    late_parts = collect_chips(piled(parts)[dp_order], dp_count)
    normed_terms = [partial_normed[k] for k in range(n)]
    arrived = collect_begin(normed_terms, "seq", n)
    summed_back = collect_end(normed_terms, arrived, collect_turn(normed_terms, arrived, "seq", n), "seq", n)
    summed_back, mixture, hidden = pin(summed_back, mixture, hidden)
    layer_output = (hidden + mixture.astype(f32)).astype(low)[None]
    grad_normed = summed_back + dot_t(grad_reduced, down_cat)
    unused_input, pull_input = jax.vjp(lambda values: rms_scale(values, gain_attention), tokens)
    input_grad = (grad_hidden + pull_input(grad_normed)[0]).astype(low)[None]

    early_parts, input_grad = pin(early_parts, input_grad)
    early_parts = early_parts.astype(f32)
    grad_a_attention = jnp.concatenate([late_parts, early_parts[:1]], axis=0)
    grad_b_attention = jnp.swapaxes(early_parts[1:], 1, 2)
    own_width = full_width // n
    own_ff = expert_w_down.shape[1] // n
    columns = lambda x, count: jnp.swapaxes(x.reshape(local_count, count, -1, rank_columns, rank_columns), 2, 3).reshape(
        local_count, count, rank_columns, -1
    )
    ends = [2 * own_width, 2 * own_width + own_ff, 2 * own_width + 3 * own_ff]
    grad_a_in = expert_sum[:, : ends[0]].reshape(local_count, 2, own_width, rank_columns)
    grad_a_down = expert_sum[:, ends[0] : ends[1]]
    grad_b_in = columns(expert_sum[:, ends[1] : ends[2]], 2)
    grad_b_down = columns(expert_sum[:, ends[2] :], 1)[:, 0]
    return (
        layer_output,
        input_grad,
        grad_a_attention,
        grad_b_attention,
        grad_a_in,
        grad_b_in,
        grad_a_down,
        grad_b_down,
    )


def solution(mesh):
    return jax.shard_map(
        local,
        mesh=mesh,
        in_specs=(
            P("dp", "seq", None),
            P("dp", "seq", None),
            P(),
            P(),
            P(),
            P(),
            P(None, None, ("seq", "dp")),
            P(("seq", "dp"), None),
            P(None, ("seq", "dp"), None),
            P(None, None, ("seq", "dp")),
            P("dp", None, None, None),
            P("dp", None, None),
            P("dp", None, None, None),
            P("dp", None, None, None),
            P("dp", None, None),
            P("dp", None, None),
            P("dp", "seq", None),
            P("dp", "seq", None),
            P("dp", None),
            P("dp", None),
        ),
        out_specs=(
            P("dp", "seq", None),
            P("dp", "seq", None),
            P(None, ("seq", "dp"), None),
            P(None, None, ("seq", "dp")),
            P("dp", None, "seq", None),
            P("dp", None, None, "seq"),
            P("dp", "seq", None),
            P("dp", None, "seq"),
        ),
        check_vma=False,
    )
```

```python
import functools

import jax
import jax.numpy as jnp
from jax import lax
from jax.experimental import pallas as pl
from jax.experimental.pallas import tpu as pltpu
from jax.sharding import PartitionSpec as P

H = 16
HD = 128
TOP = 8
R = 16


norm_epsilon = 1e-06
rope_base = 10000.0
masked_score = -1000000000.0
half_from = 200000


def rms_scale(values, gain_vector):
    return (
        values
        * lax.rsqrt(jnp.mean(values * values, axis=-1, keepdims=True) + norm_epsilon)
        * gain_vector
    )


def rope_tables(offset, width):
    half = width // 2
    frequency = rope_base ** (-(jnp.arange(half, dtype=jnp.float32) * 2.0) / width)
    angles = offset.astype(jnp.float32)[:, None] * frequency[None, :]
    cosine = jnp.cos(angles)
    sine = jnp.sin(angles)
    return jnp.concatenate([cosine, cosine], axis=1), jnp.concatenate([-sine, sine], axis=1)


def dot_nn(a, b):
    return lax.dot_general(a, b, (((1,), (0,)), ((), ())), preferred_element_type=jnp.float32)


def dot_nt(a, b):
    return lax.dot_general(a, b, (((1,), (1,)), ((), ())), preferred_element_type=jnp.float32)


def dot_tn(a, b):
    return lax.dot_general(a, b, (((0,), (0,)), ((), ())), preferred_element_type=jnp.float32)


def normed_head(raw, gain):
    inverse = lax.rsqrt(jnp.mean(raw * raw, axis=-1, keepdims=True) + norm_epsilon)
    return raw * inverse * gain, inverse


def turned_head(values, cosine, sine):
    return values * cosine + pltpu.roll(values, values.shape[-1] // 2, 1) * sine


def unturned_head(grad, cosine, sine):
    return grad * cosine + pltpu.roll(grad * sine, grad.shape[-1] // 2, 1)


def attend_kernel(
    tile, q_raw, k_raw, v_raw, cosine, sine, gain_q, gain_k, seg_col, seg_row, mixed, query, key, value, stat
):
    rows = q_raw.shape[0]
    scale = HD ** (-0.5)
    cos_all = cosine[...]
    sin_all = sine[...]
    normed_q, unused = normed_head(q_raw[...], gain_q[...])
    query[...] = turned_head(normed_q, cos_all, sin_all).astype(jnp.bfloat16)
    normed_k, unused = normed_head(k_raw[...], gain_k[...])
    keys = turned_head(normed_k, cos_all, sin_all).astype(jnp.bfloat16)
    key[...] = keys
    values = v_raw[...].astype(jnp.bfloat16)
    value[...] = values
    values_t = values.T
    for start in range(0, rows, tile):
        part = slice(start, start + tile)
        scores = dot_nt(keys, query[part, :]) * scale
        scores = jnp.where(seg_col[...] == seg_row[:, part], scores, masked_score)
        top = jnp.max(scores, axis=0, keepdims=True)
        weight = jnp.exp(scores - top)
        total = jnp.sum(weight, axis=0, keepdims=True)
        soft = (weight * (1.0 / total)).astype(jnp.bfloat16)
        mixed[part, :] = dot_nn(values_t, soft).T.astype(jnp.bfloat16)
        stat[0, :, part] = top + jnp.log(total)


def attend(raw, cosine, sine, gain_q, gain_k, segment):
    unused, length, width = raw.shape
    heads = width // HD
    tile = min(256, length)
    head = pl.BlockSpec((length, HD), lambda h: (0, h))
    raw_head = [pl.BlockSpec((None, length, HD), functools.partial(lambda m, h: (m, 0, h), m)) for m in range(3)]
    fixed = lambda shape: pl.BlockSpec(shape, lambda h: (0, 0))
    seg = segment.astype(jnp.float32)
    low = jax.ShapeDtypeStruct((length, width), jnp.bfloat16)
    return pl.pallas_call(
        functools.partial(attend_kernel, tile),
        grid=(heads,),
        in_specs=raw_head + [fixed((length, HD)), fixed((length, HD)), fixed((1, HD)), fixed((1, HD)),
                  fixed((length, 1)), fixed((1, length))],
        out_specs=[head, head, head, head, pl.BlockSpec((1, 1, length), lambda h: (h, 0, 0))],
        out_shape=[low, low, low, low, jax.ShapeDtypeStruct((heads, 1, length), jnp.float32)],
        cost_estimate=pl.CostEstimate(
            flops=4 * heads * length * length * HD, bytes_accessed=20 * length * width, transcendentals=heads * length * length
        ),
        name="attend",
    )(raw, raw, raw, cosine, sine, gain_q[None, :], gain_k[None, :], seg[:, None], seg[None, :])


def attend_back_kernel(
    tile, query, key, value, grad_mixed, stat, q_raw, k_raw, cosine, sine, gain_q, gain_k, seg_col, seg_row,
    grad_q, grad_k, grad_v, sum_k, sum_v
):
    rows = q_raw.shape[0]
    scale = HD ** (-0.5)
    keys = key[...]
    values = value[...]
    keys_t = keys.T

    def through(grad, raw_ref, gain_ref, part):
        grad = grad.astype(jnp.bfloat16).astype(jnp.float32)
        raw = raw_ref[part, :]
        gain = gain_ref[...]
        inverse = lax.rsqrt(jnp.mean(raw * raw, axis=-1, keepdims=True) + norm_epsilon)
        grad = unturned_head(grad, cosine[part, :], sine[part, :]) * gain
        dots = jnp.mean(grad * raw, axis=-1, keepdims=True)
        return (inverse * (grad - raw * (inverse * inverse * dots))).astype(jnp.bfloat16)

    for start in range(0, rows, tile):
        part = slice(start, start + tile)
        queries = query[part, :]
        grads = grad_mixed[part, :]
        scores = dot_nt(keys, queries) * scale
        scores = jnp.where(seg_col[...] == seg_row[:, part], scores, masked_score)
        soft = jnp.exp(scores - stat[0, :, part])
        grad_soft = dot_nt(values, grads)
        delta = jnp.sum(soft * grad_soft, axis=0, keepdims=True)
        grad_scores = (soft * (grad_soft - delta)).astype(jnp.bfloat16)
        term_k = dot_nn(grad_scores, queries)
        term_v = dot_nn(soft.astype(jnp.bfloat16), grads)
        if start == 0:
            sum_k[...] = term_k
            sum_v[...] = term_v
        else:
            sum_k[...] += term_k
            sum_v[...] += term_v
        grad_q[part, :] = through(dot_nn(keys_t, grad_scores).T * scale, q_raw, gain_q, part)
    for start in range(0, rows, tile):
        part = slice(start, start + tile)
        grad_k[part, :] = through(sum_k[part, :] * scale, k_raw, gain_k, part)
        grad_v[part, :] = sum_v[part, :].astype(jnp.bfloat16)


def attend_back(kept, grad_mixed, raw, cosine, sine, gain_q, gain_k, segment):
    query, key, value, stat = kept
    unused, length, width = raw.shape
    heads = width // HD
    tile = min(256, length)
    head = pl.BlockSpec((length, HD), lambda h: (0, h))
    raw_head = [pl.BlockSpec((None, length, HD), functools.partial(lambda m, h: (m, 0, h), m)) for m in range(3)]
    fixed = lambda shape: pl.BlockSpec(shape, lambda h: (0, 0))
    seg = segment.astype(jnp.float32)
    low = jax.ShapeDtypeStruct((length, width), jnp.bfloat16)
    return pl.pallas_call(
        functools.partial(attend_back_kernel, tile),
        grid=(heads,),
        in_specs=[head, head, head, head, pl.BlockSpec((1, 1, length), lambda h: (h, 0, 0)), raw_head[0], raw_head[1],
                  fixed((length, HD)), fixed((length, HD)), fixed((1, HD)), fixed((1, HD)),
                  fixed((length, 1)), fixed((1, length))],
        out_specs=[head, head, head],
        out_shape=[low, low, low],
        scratch_shapes=[pltpu.VMEM((length, HD), jnp.float32), pltpu.VMEM((length, HD), jnp.float32)],
        cost_estimate=pl.CostEstimate(
            flops=heads * length * HD, bytes_accessed=length * width, transcendentals=0
        ),
        name="attend_back",
    )(query, key, value, grad_mixed, stat, raw, raw, cosine, sine, gain_q[None, :], gain_k[None, :],
      seg[:, None], seg[None, :])


def doc_layout(lengths, chosen, position):
    slots = jnp.arange(lengths.shape[0], dtype=jnp.int32)
    doc_ends = jnp.sum(jnp.where(slots[:, None] >= slots[None, :], lengths[None, :], 0), axis=1)
    starts = doc_ends - lengths
    segment = jnp.sum((position[:, None] >= doc_ends[None, :]).astype(jnp.int32), axis=1)
    doc_pick = (segment[:, None] == slots[None, :]).astype(jnp.int32)
    offset = position - jnp.sum(doc_pick * starts[None, :], axis=1)
    adapter = jnp.sum(doc_pick * chosen[None, :], axis=1)
    return (segment, offset, adapter)


def column_mask(adapter, columns):
    groups = jnp.arange(columns, dtype=jnp.int32) // R
    return (groups[None, :] == adapter[:, None]).astype(jnp.float32)


def qkv_kernel(x_ref, reduced_ref, w_ref, up_ref, out_ref):
    width = w_ref.shape[0] * w_ref.shape[1]
    weights = w_ref[...].reshape(width, x_ref.shape[1])
    out_ref[0] = dot_nt(x_ref[...], weights) + dot_nt(reduced_ref[...], up_ref[0])


def qkv_project(normed_all, reduced_cat, w_group, up_group):
    length, width = normed_all.shape
    dp_count, unused, piece, unused = w_group.shape
    group = dp_count * piece
    rank = up_group.shape[2]
    half = dp_count // 2
    return pl.pallas_call(
        qkv_kernel,
        grid=(3, 2),
        in_specs=[
            pl.BlockSpec((length, width), lambda m, p: (0, 0)),
            pl.BlockSpec((length, rank), lambda m, p: (0, m)),
            pl.BlockSpec((half, None, piece, width), lambda m, p: (p, m, 0, 0)),
            pl.BlockSpec((1, group // 2, rank), lambda m, p: (m, p, 0)),
        ],
        out_specs=pl.BlockSpec((1, length, group // 2), lambda m, p: (m, 0, p)),
        out_shape=jax.ShapeDtypeStruct((3, length, group), jnp.float32),
        cost_estimate=pl.CostEstimate(
            flops=6 * length * width * group, bytes_accessed=2 * length * width + 12 * length * group + 6 * group * width,
            transcendentals=0,
        ),
        name="qkv_project",
    )(normed_all, reduced_cat, w_group, up_group)


def qkv_back_kernel(a_ref, b_ref, c_ref, w_ref, out_ref):
    dp_count, unused, piece, cols = w_ref.shape
    total = None
    for m, ref in enumerate((a_ref, b_ref, c_ref)):
        term = dot_nn(ref[...], w_ref[:, m].reshape(dp_count * piece, cols))
        total = term if total is None else total + term
    out_ref[...] = total.astype(jnp.bfloat16)


def qkv_back(grads, w_group):
    length, group = grads[0].shape
    dp_count, unused, piece, width = w_group.shape
    tile = min(256, width)
    whole = pl.BlockSpec((length, group), lambda i: (0, 0))
    return pl.pallas_call(
        qkv_back_kernel,
        grid=(width // tile,),
        in_specs=[whole, whole, whole, pl.BlockSpec((dp_count, 3, piece, tile), lambda i: (0, 0, 0, i))],
        out_specs=pl.BlockSpec((length, tile), lambda i: (0, i)),
        out_shape=jax.ShapeDtypeStruct((length, width), jnp.bfloat16),
        cost_estimate=pl.CostEstimate(flops=length * width, bytes_accessed=length * width, transcendentals=0),
        name="qkv_back",
    )(grads[0], grads[1], grads[2], w_group)


def expert_kernel(kept_in, which, *refs):
    (x_a, x_b, g_both, pick, pick_t, slot, w_in, w_down, a_in, b_in, a_down, b_down) = refs[:12]
    refs = refs[12 + kept_in:]
    (out_both, back_a, back_b, xs, ps, act_o, gate_o, up_o, reds) = refs[:9]
    (red_g, red_u, gred_d, down_acc, down_red, gx_acc, gred_g, gred_u, sum_out_a, sum_out_b, sum_back_a, sum_back_b) = refs[9:]
    low = jnp.bfloat16
    e = pl.program_id(0)
    f = pl.program_id(1)
    last = pl.num_programs(1) - 1
    cap = pick.shape[2]
    rank = a_in.shape[3]
    rows = xs.shape[1]
    groups = lax.shift_right_logical(lax.broadcasted_iota(jnp.int32, (rows, rank), 1), R.bit_length() - 1)
    mask = jnp.where(groups.astype(jnp.float32) == slot[0, :, 1:2], 1.0, 0.0)

    @pl.when(f == 0)
    def _():
        for b, x_ref in enumerate((x_a, x_b)):
            part = slice(b * cap, (b + 1) * cap)
            g_place = which[1] if b == 0 else 1 - which[1]
            xs[0, part, :] = dot_nn(pick[0, b], x_ref[...]).astype(low)
            ps[0, part, :] = (slot[0, part, 0:1] * dot_nn(pick[0, b], g_both[g_place])).astype(low)
        red_g[...] = (mask * dot_nn(xs[0], a_in[0, 0])).astype(low)
        red_u[...] = (mask * dot_nn(xs[0], a_in[0, 1])).astype(low)
        gred_d[...] = (mask * dot_nt(ps[0], b_down[0])).astype(low)

    x = xs[0]
    p = ps[0]
    gate = dot_nn(x, w_in[0, 0]) + dot_nn(red_g[...], b_in[0, 0])
    up = dot_nn(x, w_in[0, 1]) + dot_nn(red_u[...], b_in[0, 1])
    grad_act = dot_nt(p, w_down[0]) + dot_nt(gred_d[...], a_down[0])
    sigma = 1.0 / (1.0 + jnp.exp(-gate))
    silu = gate * sigma
    act = (silu * up).astype(low)
    grad_gate = (grad_act * up * (sigma * (1.0 + gate * (1.0 - sigma)))).astype(low)
    grad_up = (grad_act * silu).astype(low)
    act_o[0] = act
    gate_o[0] = grad_gate
    up_o[0] = grad_up
    down_term = dot_nn(act, w_down[0])
    down_red_term = dot_nn(act, a_down[0])
    gx_term = dot_nt(grad_gate, w_in[0, 0]) + dot_nt(grad_up, w_in[0, 1])
    gred_g_term = dot_nt(grad_gate, b_in[0, 0])
    gred_u_term = dot_nt(grad_up, b_in[0, 1])

    @pl.when(f == 0)
    def _():
        down_acc[...] = down_term
        down_red[...] = down_red_term
        gx_acc[...] = gx_term
        gred_g[...] = gred_g_term
        gred_u[...] = gred_u_term

    @pl.when(f > 0)
    def _():
        down_acc[...] += down_term
        down_red[...] += down_red_term
        gx_acc[...] += gx_term
        gred_g[...] += gred_g_term
        gred_u[...] += gred_u_term

    @pl.when(f == last)
    def _():
        reduced_d = (mask * down_red[...]).astype(low)
        back_g = (mask * gred_g[...]).astype(low)
        back_u = (mask * gred_u[...]).astype(low)
        for i, value in enumerate((red_g[...], red_u[...], reduced_d, back_g, back_u, gred_d[...])):
            reds[0, :, i * rank : (i + 1) * rank] = value
        produced = down_acc[...] + dot_nn(reduced_d, b_down[0])
        scaled = (slot[0, :, 0:1] * produced).astype(low)
        grads = (gx_acc[...] + dot_nt(back_g, a_in[0, 0]) + dot_nt(back_u, a_in[0, 1])).astype(low)
        for b, (out_sum, back_ref, back_sum) in enumerate(
            ((sum_out_a, back_a, sum_back_a), (sum_out_b, back_b, sum_back_b))
        ):
            part = slice(b * cap, (b + 1) * cap)
            out_ref = out_both.at[which[3] if b == 0 else 1 - which[3]]
            for values, total, result in ((scaled, out_sum, out_ref), (grads, back_sum, back_ref)):
                term = dot_nn(pick_t[0, b], values[part, :])

                @pl.when(e == 0)
                def _():
                    total[...] = term

                @pl.when(e > 0)
                def _():
                    total[...] += term

                @pl.when(e == pl.num_programs(0) - 1)
                def _():
                    result[...] = total[...].astype(low)


def run_experts(which, x_pair, g_all, pick, pick_t, slot, weights, kept):
    w_in, w_down, a_in, b_in, a_down, b_down = weights
    experts, unused, width, ff = w_in.shape
    unused, dp_count, cap, own_rows = pick.shape
    rank = a_down.shape[2]
    rows = 2 * cap
    tile = min(512, ff)
    low = jnp.bfloat16
    f32 = jnp.float32
    one = pl.Buffered(1)
    token = pl.BlockSpec((own_rows, width), lambda e, f, w: (0, 0), pipeline_mode=one)
    stored = [
        ((experts, dp_count * cap, width), (1, rows, width), lambda e, f, w: (e, w[4], 0)),
        ((experts, dp_count * cap, width), (1, rows, width), lambda e, f, w: (e, w[4], 0)),
        ((experts, dp_count * cap, ff), (1, rows, tile), lambda e, f, w: (e, w[4], f)),
        ((experts, dp_count * cap, ff), (1, rows, tile), lambda e, f, w: (e, w[4], f)),
        ((experts, dp_count * cap, ff), (1, rows, tile), lambda e, f, w: (e, w[4], f)),
        ((experts, dp_count * cap, 6 * rank), (1, rows, 6 * rank), lambda e, f, w: (e, w[4], 0)),
    ]
    in_specs = [
        token, token, pl.BlockSpec((2, own_rows, width), lambda e, f, w: (w[0], 0, 0), pipeline_mode=one),
        pl.BlockSpec((1, 2, cap, own_rows), lambda e, f, w: (e, w[4], 0, 0)),
        pl.BlockSpec((1, 2, own_rows, cap), lambda e, f, w: (e, w[4], 0, 0)),
        pl.BlockSpec((1, rows, 2), lambda e, f, w: (e, w[4], 0)),
        pl.BlockSpec((1, 2, width, tile), lambda e, f, w: (e, 0, 0, f)),
        pl.BlockSpec((1, tile, width), lambda e, f, w: (e, f, 0)),
        pl.BlockSpec((1, 2, width, rank), lambda e, f, w: (e, 0, 0, 0)),
        pl.BlockSpec((1, 2, rank, tile), lambda e, f, w: (e, 0, 0, f)),
        pl.BlockSpec((1, tile, rank), lambda e, f, w: (e, f, 0)),
        pl.BlockSpec((1, rank, width), lambda e, f, w: (e, 0, 0)),
    ] + [pl.BlockSpec(memory_space=pl.ANY) for unused in kept]
    part = jax.ShapeDtypeStruct((own_rows, width), low)
    results = pl.pallas_call(
        functools.partial(expert_kernel, len(kept)),
        grid_spec=pltpu.PrefetchScalarGridSpec(
            num_scalar_prefetch=1,
            grid=(experts, ff // tile),
            in_specs=in_specs,
            out_specs=[pl.BlockSpec((2, own_rows, width), lambda e, f, w: (w[2], 0, 0), pipeline_mode=one), token, token]
            + [pl.BlockSpec(block, index) for unused, block, index in stored],
            scratch_shapes=[
            pltpu.VMEM((rows, rank), low),
            pltpu.VMEM((rows, rank), low),
            pltpu.VMEM((rows, rank), low),
            pltpu.VMEM((rows, width), f32),
            pltpu.VMEM((rows, rank), f32),
            pltpu.VMEM((rows, width), f32),
            pltpu.VMEM((rows, rank), f32),
            pltpu.VMEM((rows, rank), f32),
        ] + [pltpu.VMEM((own_rows, width), f32) for unused in range(4)],
        ),
        out_shape=[jax.ShapeDtypeStruct((dp_count, own_rows, width), low)] + [part] * 2 + [jax.ShapeDtypeStruct(shape, low) for shape, unused, unused2 in stored],
        input_output_aliases={13 + i: 0 if i == 0 else 2 + i for i in range(len(kept))},
        cost_estimate=pl.CostEstimate(
            flops=experts * rows * width, bytes_accessed=experts * rows * width, transcendentals=0
        ),
        compiler_params=pltpu.CompilerParams(vmem_limit_bytes=60 * 1024 * 1024),
        name="experts",
    )(which, *x_pair, g_all, pick, pick_t, slot, *weights, *kept)
    return results[1:3], [results[0]] + list(results[3:])


def adapter_kernel(which, xs, ps, act, gate, up, reds, out):
    rank = out.shape[3]
    red = [reds[0, :, i * rank : (i + 1) * rank] for i in range(6)]
    into = dot_tn(xs[0], reds[0, :, 3 * rank : 5 * rank])
    parts = [into[:, :rank], into[:, rank:], dot_tn(act[0], red[5])]
    for wide in (dot_tn(red[0], gate[0]), dot_tn(red[1], up[0]), dot_tn(red[2], ps[0])):
        parts += [wide[:, i : i + rank] for i in range(0, wide.shape[1], rank)]
    start = 0
    for part in parts:
        out[0, 0, start : start + part.shape[0], :] = part.astype(jnp.bfloat16)
        start += part.shape[0]


def adapter_grads(kept, order):
    xs, ps, act, gate, up, reds = kept
    experts, rows, width = xs.shape
    ff = act.shape[2]
    n = order.shape[0]
    rank = reds.shape[2] // 6
    total = (3 * width + 3 * ff) // n
    wide = pl.BlockSpec((1, rows, width // n), lambda e, k, w: (e, 0, w[k]))
    narrow = pl.BlockSpec((1, rows, ff // n), lambda e, k, w: (e, 0, w[k]))
    return pl.pallas_call(
        adapter_kernel,
        grid_spec=pltpu.PrefetchScalarGridSpec(
            num_scalar_prefetch=1,
            grid=(experts, n),
            in_specs=[wide, wide, narrow, narrow, narrow, pl.BlockSpec((1, rows, 6 * rank), lambda e, k, w: (e, 0, 0))],
            out_specs=pl.BlockSpec((1, 1, total, rank), lambda e, k, w: (k, e, 0, 0)),
        ),
        out_shape=jax.ShapeDtypeStruct((n, experts, total, rank), jnp.bfloat16),
        cost_estimate=pl.CostEstimate(flops=rows * width, bytes_accessed=rows * width, transcendentals=0),
        name="adapter_grads",
    )(order, xs, ps, act, gate, up, reds)


def swap(values, axis, distance, count):
    return lax.ppermute(values, axis, [(i, i ^ distance) for i in range(count)])


def near(values, axis, count):
    return [swap(values, axis, 1, count), swap(values, axis, 2, count)]


def spread(values, axis, count, close=None):
    one, two = near(values, axis, count) if close is None else close
    if count == 4 and values.size >= half_from:
        half = values.shape[0] // 2
        three = [swap(two[:half], axis, 1, count), swap(one[half:], axis, 2, count)]
        return [values, one, two, jnp.concatenate(three, axis=0)]
    return [values, one, two] + [swap(values, axis, k, count) for k in range(3, count)]


def collect_begin(blocks, axis, count):
    if count == 4 and blocks[0].size >= half_from:
        half = blocks[0].shape[0] // 2
        return [
            swap(blocks[3][:half], axis, 1, count),
            swap(blocks[3][half:], axis, 2, count),
            swap(blocks[1][:half], axis, 1, count),
            swap(blocks[2][half:], axis, 2, count),
        ]
    return [swap(blocks[k], axis, k, count) for k in range(1, count)]


def collect_turn(blocks, arrived, axis, count):
    if count == 4 and blocks[0].size >= half_from:
        half = blocks[0].shape[0] // 2
        to_two = (blocks[2][:half].astype(jnp.float32) + arrived[0].astype(jnp.float32)).astype(blocks[2].dtype)
        to_one = (blocks[1][half:].astype(jnp.float32) + arrived[1].astype(jnp.float32)).astype(blocks[1].dtype)
        to_two, to_one = pin(to_two, to_one)
        return [swap(to_two, axis, 2, count), swap(to_one, axis, 1, count)]
    return []


def collect_end(blocks, arrived, turned, axis, count):
    f32 = jnp.float32
    if turned:
        half = blocks[0].shape[0] // 2
        top = blocks[0][:half].astype(f32) + arrived[2].astype(f32) + turned[0].astype(f32)
        low = blocks[0][half:].astype(f32) + arrived[3].astype(f32) + turned[1].astype(f32)
        return jnp.concatenate([top, low], axis=0)
    return sum((x.astype(f32) for x in arrived), blocks[0].astype(f32))


def collect(blocks, axis, count):
    arrived = collect_begin(blocks, axis, count)
    return collect_end(blocks, arrived, collect_turn(blocks, arrived, axis, count), axis, count)


def collect_chips(blocks, count):
    pairs = blocks.reshape((count // 2, 2) + blocks.shape[1:])
    summed = pairs[:, 0].astype(jnp.float32) + swap(pairs[:, 1], "dp", 1, count).astype(jnp.float32)
    total = summed[0]
    summed = summed.astype(blocks.dtype)
    for c in range(1, count // 2):
        total = total + swap(summed[c], "dp", 2 * c, count).astype(jnp.float32)
    return total


def pin(*values):
    return lax.optimization_barrier(values)


def local(
    layer_input,
    out_cotangent,
    gain_attention,
    gain_query,
    gain_key,
    gain_ffn,
    w_qkv,
    w_output,
    a_attention,
    b_attention,
    expert_w_in,
    expert_w_down,
    expert_a_in,
    expert_b_in,
    expert_a_down,
    expert_b_down,
    route_experts,
    route_gates,
    doc_lengths,
    adapter_ids,
):
    low = jnp.bfloat16
    f32 = jnp.float32
    own_rows = layer_input.shape[1]
    full_width = layer_input.shape[2]
    n = lax.axis_size("seq")
    dp_count = lax.axis_size("dp")
    s = lax.axis_index("seq")
    d = lax.axis_index("dp")
    length = own_rows * n
    rank_columns = a_attention.shape[2]
    group_width = full_width // n
    group_heads = H // n
    piece = group_width // dp_count
    group_start = s * group_width
    order = s ^ jnp.arange(n, dtype=jnp.int32)
    position = (order[:, None] * own_rows + jnp.arange(own_rows, dtype=jnp.int32)[None, :]).reshape(-1)
    segment, offset, adapter = doc_layout(doc_lengths[0], adapter_ids[0], position)
    own_adapter = adapter[:own_rows]
    own_mask = column_mask(own_adapter, rank_columns)
    full_mask = column_mask(adapter, rank_columns)

    gates = route_gates[0].T
    gates_high = gates.astype(low)
    meta = jnp.concatenate(
        [
            route_experts[0].T.astype(low),
            gates_high,
            (gates - gates_high.astype(f32)).astype(low),
            own_adapter[None, :].astype(low),
            jnp.zeros((7, own_rows), low),
        ],
        axis=0,
    )
    ab_piece = jnp.concatenate([a_attention[0:3], jnp.swapaxes(b_attention, 1, 2)], axis=0).reshape(-1, rank_columns)
    ab_rows = ab_piece.shape[0]
    ab_piece = jnp.concatenate([ab_piece, meta.reshape(-1, rank_columns)], axis=0)
    ab_got = lax.all_gather(ab_piece, "dp", axis=0)
    tokens = layer_input[0].astype(f32)
    normed = rms_scale(tokens, gain_attention).astype(low)
    wt_piece = jnp.swapaxes(w_qkv, 1, 2)
    wt_piece, ab_got, *close = pin(wt_piece, ab_got, *near(normed, "seq", n))
    w_group = lax.all_gather(wt_piece, "dp", axis=0)
    dp_order = d ^ jnp.arange(dp_count, dtype=jnp.int32)
    meta_all = ab_got[:, ab_rows:].reshape((dp_count,) + meta.shape)[dp_order].astype(f32)
    ab_group = ab_got[:, :ab_rows].reshape(dp_count, 7, piece, rank_columns)
    ab_group = jnp.swapaxes(ab_group, 0, 1).reshape(7, group_width, rank_columns)
    local_count = expert_w_in.shape[0]
    expert_count = local_count * dp_count
    capacity = own_rows * TOP // expert_count * 9 // 8
    capacity = -(-capacity // 16) * 16
    named = meta_all[:, 0:TOP, :].astype(jnp.int32)
    gates_all = meta_all[:, TOP : 2 * TOP, :] + meta_all[:, 2 * TOP : 3 * TOP, :]
    sets_all = meta_all[:, 3 * TOP, :]
    mine = d * local_count + jnp.arange(local_count, dtype=jnp.int32)
    hit = (named[None] == mine[:, None, None, None]).astype(f32)
    member = jnp.sum(hit, axis=2)
    token_gate = jnp.sum(hit * gates_all[None], axis=2)
    t_index = jnp.arange(own_rows, dtype=jnp.int32)
    upto = (t_index[:, None] <= t_index[None, :]).astype(low)
    rank = jnp.einsum("ejt,tu->eju", member.astype(low), upto, preferred_element_type=f32) - 1.0
    slots = jnp.arange(capacity, dtype=jnp.int32).astype(f32)
    rank = jnp.where(member > 0.5, rank, -1.0)
    pick = slots[None, None, :, None] == rank[:, :, None, :]
    pick_t = (rank[:, :, :, None] == slots[None, None, None, :]).astype(low)
    slot_gate = jnp.sum(jnp.where(pick, token_gate[:, :, None, :], 0.0), axis=-1)
    slot_set = jnp.sum(jnp.where(pick, sets_all[None, :, None, :], 0.0), axis=-1)
    slot = jnp.stack([slot_gate, slot_set], axis=-1).reshape(local_count, dp_count * capacity, 2)
    pick = pick.astype(low)

    cosine, sine = rope_tables(offset, HD)

    dot = lambda a, b: jnp.dot(a, b, preferred_element_type=f32)
    dot_t = lambda a, b: lax.dot_general(a, b, (((1,), (1,)), ((), ())), preferred_element_type=f32)
    dot_l = lambda a, b: lax.dot_general(a, b, (((0,), (0,)), ((), ())), preferred_element_type=f32)

    share = jnp.concatenate([ab_group[0:3], ab_group[6:7]], axis=0)
    share_full = jnp.stack(spread(share, "seq", n))[order]
    share_full = jnp.swapaxes(share_full, 0, 1).reshape(4, full_width, rank_columns)
    down_cat = jnp.swapaxes(share_full[0:3], 0, 1).reshape(full_width, 3 * rank_columns)
    upt_output = share_full[3]
    upt_group = ab_group[3:6]
    normed_all = jnp.concatenate(spread(normed, "seq", n, close), axis=0)
    reduced_cat = (jnp.tile(full_mask, (1, 3)) * dot(normed_all, down_cat)).astype(low)
    out_piece = jnp.concatenate([w_output, a_attention[3]], axis=1)
    out_piece, w_group, pick, pick_t, slot, cosine, sine, normed_all, reduced_cat, upt_group, upt_output = pin(
        out_piece, w_group, pick, pick_t, slot, cosine, sine, normed_all, reduced_cat, upt_group, upt_output
    )
    out_maps = lax.all_gather(out_piece, "dp", axis=0, tiled=True)
    reduced_list = [reduced_cat[:, m * rank_columns : (m + 1) * rank_columns] for m in range(3)]
    raw = qkv_project(normed_all, reduced_cat, w_group, upt_group)
    grad_send, raw = pin(out_cotangent[0], raw)
    grad_got = lax.all_gather(grad_send, "dp", axis=0)
    grad_own = jnp.stack([out_cotangent[0], swap(out_cotangent[0], "dp", 1, dp_count)])
    mixed_group, query_heads, key_heads, value_heads, stat = attend(
        raw, cosine, sine, gain_query, gain_key, segment
    )

    partial_out = dot(mixed_group, out_maps).astype(low).reshape(n, own_rows, full_width + rank_columns)
    summed = collect([partial_out[k] for k in range(n)], "seq", n)
    output_reduced = (own_mask * summed[:, full_width:]).astype(low)
    attended = summed[:, :full_width] + dot_t(output_reduced, upt_output)
    hidden = tokens + attended
    normed_ffn = rms_scale(hidden, gain_ffn).astype(low)
    weights = (expert_w_in, expert_w_down, expert_a_in, expert_b_in, expert_a_down, expert_b_down)
    chips = dp_count // 2
    turns = [0] + list(range(chips // 2, chips)) + list(range(1, chips // 2))
    kept = ()
    rows = normed_ffn
    here = normed_ffn
    arrived = swap(rows, "dp", 2 * turns[1], dp_count)
    other = swap(here, "dp", 1, dp_count)
    leaving = None
    flying = None
    grad_normed_ffn = None
    for i, c in enumerate(turns):
        if i > 0:
            here = arrived
            if flying is not None:
                here, flying = pin(here, flying)
                grad_normed_ffn = grad_normed_ffn + flying.astype(f32)
            other = swap(here, "dp", 1, dp_count)
            rows, here, other, leaving = pin(rows, here, other, leaving)
            if i < chips - 1:
                arrived = swap(rows, "dp", 2 * turns[i + 1], dp_count)
            if i == 1:
                grad_normed_ffn = leaving
            else:
                flying = swap(leaving, "dp", 2 * turns[i - 1], dp_count)
        block = lax.shift_right_logical(d, 1) ^ c
        place = d & 1
        which = jnp.stack(([block, place] if c else [0 * d, 0 * d]) + [block, place, 0 * d + c]).astype(jnp.int32)
        (back, back_other), kept = run_experts(
            which, (here, other), grad_got if c else grad_own, pick, pick_t, slot, weights, kept
        )
        if i == chips - 1 and flying is not None:
            flying, back_other = pin(flying, back_other)
        leaving = back.astype(f32) + swap(back_other, "dp", 1, dp_count).astype(f32)
        if i > 0:
            leaving = leaving.astype(low)
    if flying is not None:
        grad_normed_ffn = grad_normed_ffn + flying.astype(f32)
    outs_all, *kept = kept
    leaving, *kept = pin(leaving, *kept)
    flying = swap(leaving, "dp", 2 * turns[-1], dp_count)
    flat = adapter_grads(kept, order)
    flat, flying = pin(flat, flying)
    grad_normed_ffn = grad_normed_ffn + flying.astype(f32)

    outs_all, grad_normed_ffn = pin(outs_all, grad_normed_ffn)
    mixture = lax.psum_scatter(outs_all, "dp", scatter_dimension=0)
    grad_out = out_cotangent[0].astype(f32)
    unused, pull_ffn = jax.vjp(lambda values: rms_scale(values, gain_ffn), hidden)
    grad_hidden = grad_out + pull_ffn(grad_normed_ffn)[0]
    grad_hidden_low = grad_hidden.astype(low)
    grad_reduced_output = (own_mask * dot(grad_hidden_low, upt_output)).astype(low)
    grad_pack = jnp.concatenate([grad_hidden_low, grad_reduced_output, output_reduced], axis=1)
    flat, *grad_packs = pin(flat, *spread(grad_pack, "seq", n))
    expert_terms = [flat[k] for k in range(n)]
    expert_arrived = collect_begin(expert_terms, "seq", n)
    grad_pack_all = jnp.concatenate(grad_packs, axis=0)
    grad_all = grad_pack_all[:, :full_width]
    grad_reduced_all = grad_pack_all[:, full_width : full_width + rank_columns]
    output_reduced_all = grad_pack_all[:, full_width + rank_columns :]
    grad_mixed_group = dot_t(grad_pack_all[:, : full_width + rank_columns], out_maps).astype(low)
    grad_cols = lax.dynamic_slice_in_dim(grad_all, group_start, group_width, 1)
    grad_upt_output = dot_l(grad_cols, output_reduced_all)
    grad_down_output = dot_l(mixed_group, grad_reduced_all)
    grad_raw_list = attend_back(
        (query_heads, key_heads, value_heads, stat),
        grad_mixed_group,
        raw,
        cosine,
        sine,
        gain_query,
        gain_key,
        segment,
    )
    pinned = pin(*grad_raw_list, *expert_arrived)
    grad_raw_list = list(pinned[:3])
    expert_arrived = pinned[3:]
    expert_turned = collect_turn(expert_terms, expert_arrived, "seq", n)
    partial_reduced = jnp.concatenate(
        [dot(grad_raw_list[m], upt_group[m]) for m in range(3)], axis=1
    ).astype(low)
    partial_reduced, *grad_raw_list = pin(partial_reduced, *grad_raw_list)
    partial_reduced = partial_reduced.reshape(n, own_rows, 3 * rank_columns)
    summed_reduced = collect([partial_reduced[k] for k in range(n)], "seq", n)
    grad_reduced = (jnp.tile(own_mask, (1, 3)) * summed_reduced).astype(low)
    grad_reduced, *grad_raw_late = pin(grad_reduced, *grad_raw_list)
    grad_reduced_full = jnp.concatenate(spread(grad_reduced, "seq", n), axis=0)
    partial_normed = qkv_back(grad_raw_list, w_group).reshape(n, own_rows, full_width)
    partial_normed, grad_reduced, *expert_turned = pin(partial_normed, grad_reduced, *expert_turned)
    expert_sum = collect_end(expert_terms, expert_arrived, expert_turned, "seq", n)
    grad_upt = [dot_l(grad_raw_late[m], reduced_list[m]) for m in range(3)]
    normed_cols = lax.dynamic_slice_in_dim(normed_all, group_start, group_width, 1)
    grad_down_cat = dot_l(normed_cols, grad_reduced_full)
    parts = [grad_down_cat[:, m * rank_columns : (m + 1) * rank_columns] for m in range(3)]
    piled = lambda some: jnp.stack([x.astype(low).reshape(dp_count, piece, rank_columns) for x in some], axis=1)
    early_parts = piled([grad_down_output] + grad_upt + [grad_upt_output])
    early_parts = lax.psum_scatter(early_parts, "dp", scatter_dimension=0)
    late_parts = collect_chips(piled(parts)[dp_order], dp_count)
    normed_terms = [partial_normed[k] for k in range(n)]
    arrived = collect_begin(normed_terms, "seq", n)
    summed_back = collect_end(normed_terms, arrived, collect_turn(normed_terms, arrived, "seq", n), "seq", n)
    summed_back, mixture, hidden = pin(summed_back, mixture, hidden)
    layer_output = (hidden + mixture.astype(f32)).astype(low)[None]
    grad_normed = summed_back + dot_t(grad_reduced, down_cat)
    unused_input, pull_input = jax.vjp(lambda values: rms_scale(values, gain_attention), tokens)
    input_grad = (grad_hidden + pull_input(grad_normed)[0]).astype(low)[None]

    early_parts, input_grad = pin(early_parts, input_grad)
    early_parts = early_parts.astype(f32)
    grad_a_attention = jnp.concatenate([late_parts, early_parts[:1]], axis=0)
    grad_b_attention = jnp.swapaxes(early_parts[1:], 1, 2)
    own_width = full_width // n
    own_ff = expert_w_down.shape[1] // n
    columns = lambda x, count: jnp.swapaxes(x.reshape(local_count, count, -1, rank_columns, rank_columns), 2, 3).reshape(
        local_count, count, rank_columns, -1
    )
    ends = [2 * own_width, 2 * own_width + own_ff, 2 * own_width + 3 * own_ff]
    grad_a_in = expert_sum[:, : ends[0]].reshape(local_count, 2, own_width, rank_columns)
    grad_a_down = expert_sum[:, ends[0] : ends[1]]
    grad_b_in = columns(expert_sum[:, ends[1] : ends[2]], 2)
    grad_b_down = columns(expert_sum[:, ends[2] :], 1)[:, 0]
    return (
        layer_output,
        input_grad,
        grad_a_attention,
        grad_b_attention,
        grad_a_in,
        grad_b_in,
        grad_a_down,
        grad_b_down,
    )


def solution(mesh):
    return jax.shard_map(
        local,
        mesh=mesh,
        in_specs=(
            P("dp", "seq", None),
            P("dp", "seq", None),
            P(),
            P(),
            P(),
            P(),
            P(None, None, ("seq", "dp")),
            P(("seq", "dp"), None),
            P(None, ("seq", "dp"), None),
            P(None, None, ("seq", "dp")),
            P("dp", None, None, None),
            P("dp", None, None),
            P("dp", None, None, None),
            P("dp", None, None, None),
            P("dp", None, None),
            P("dp", None, None),
            P("dp", "seq", None),
            P("dp", "seq", None),
            P("dp", None),
            P("dp", None),
        ),
        out_specs=(
            P("dp", "seq", None),
            P("dp", "seq", None),
            P(None, ("seq", "dp"), None),
            P(None, None, ("seq", "dp")),
            P("dp", None, "seq", None),
            P("dp", None, None, "seq"),
            P("dp", "seq", None),
            P("dp", None, "seq"),
        ),
        check_vma=False,
    )
```

```python
import functools

import jax
import jax.numpy as jnp
from jax import lax
from jax.experimental import pallas as pl
from jax.experimental.pallas import tpu as pltpu
from jax.sharding import PartitionSpec as P

H = 16
HD = 128
TOP = 8
R = 16


norm_epsilon = 1e-06
rope_base = 10000.0
masked_score = -1000000000.0
half_from = 200000


def rms_scale(values, gain_vector):
    return (
        values
        * lax.rsqrt(jnp.mean(values * values, axis=-1, keepdims=True) + norm_epsilon)
        * gain_vector
    )


def rope_tables(offset, width):
    half = width // 2
    frequency = rope_base ** (-(jnp.arange(half, dtype=jnp.float32) * 2.0) / width)
    angles = offset.astype(jnp.float32)[:, None] * frequency[None, :]
    cosine = jnp.cos(angles)
    sine = jnp.sin(angles)
    return jnp.concatenate([cosine, cosine], axis=1), jnp.concatenate([-sine, sine], axis=1)


def dot_nn(a, b):
    return lax.dot_general(a, b, (((1,), (0,)), ((), ())), preferred_element_type=jnp.float32)


def dot_nt(a, b):
    return lax.dot_general(a, b, (((1,), (1,)), ((), ())), preferred_element_type=jnp.float32)


def dot_tn(a, b):
    return lax.dot_general(a, b, (((0,), (0,)), ((), ())), preferred_element_type=jnp.float32)


def normed_head(raw, gain):
    inverse = lax.rsqrt(jnp.mean(raw * raw, axis=-1, keepdims=True) + norm_epsilon)
    return raw * inverse * gain, inverse


def turned_head(values, cosine, sine):
    return values * cosine + pltpu.roll(values, values.shape[-1] // 2, 1) * sine


def unturned_head(grad, cosine, sine):
    return grad * cosine + pltpu.roll(grad * sine, grad.shape[-1] // 2, 1)


def attend_kernel(
    tile, q_raw, k_raw, v_raw, cosine, sine, gain_q, gain_k, seg_col, seg_row, mixed, query, key, value, stat
):
    rows = q_raw.shape[0]
    scale = HD ** (-0.5)
    cos_all = cosine[...]
    sin_all = sine[...]
    normed_q, unused = normed_head(q_raw[...], gain_q[...])
    query[...] = turned_head(normed_q, cos_all, sin_all).astype(jnp.bfloat16)
    normed_k, unused = normed_head(k_raw[...], gain_k[...])
    keys = turned_head(normed_k, cos_all, sin_all).astype(jnp.bfloat16)
    key[...] = keys
    values = v_raw[...].astype(jnp.bfloat16)
    value[...] = values
    values_t = values.T
    for start in range(0, rows, tile):
        part = slice(start, start + tile)
        scores = dot_nt(keys, query[part, :]) * scale
        scores = jnp.where(seg_col[...] == seg_row[:, part], scores, masked_score)
        top = jnp.max(scores, axis=0, keepdims=True)
        weight = jnp.exp(scores - top)
        total = jnp.sum(weight, axis=0, keepdims=True)
        soft = (weight * (1.0 / total)).astype(jnp.bfloat16)
        mixed[part, :] = dot_nn(values_t, soft).T.astype(jnp.bfloat16)
        stat[0, :, part] = top + jnp.log(total)


def attend(raw, cosine, sine, gain_q, gain_k, segment):
    unused, length, width = raw.shape
    heads = width // HD
    tile = min(512, length)
    head = pl.BlockSpec((length, HD), lambda h: (0, h))
    raw_head = [pl.BlockSpec((None, length, HD), functools.partial(lambda m, h: (m, 0, h), m)) for m in range(3)]
    fixed = lambda shape: pl.BlockSpec(shape, lambda h: (0, 0))
    seg = segment.astype(jnp.float32)
    low = jax.ShapeDtypeStruct((length, width), jnp.bfloat16)
    return pl.pallas_call(
        functools.partial(attend_kernel, tile),
        grid=(heads,),
        in_specs=raw_head + [fixed((length, HD)), fixed((length, HD)), fixed((1, HD)), fixed((1, HD)),
                  fixed((length, 1)), fixed((1, length))],
        out_specs=[head, head, head, head, pl.BlockSpec((1, 1, length), lambda h: (h, 0, 0))],
        out_shape=[low, low, low, low, jax.ShapeDtypeStruct((heads, 1, length), jnp.float32)],
        cost_estimate=pl.CostEstimate(
            flops=4 * heads * length * length * HD, bytes_accessed=20 * length * width, transcendentals=heads * length * length
        ),
        name="attend",
    )(raw, raw, raw, cosine, sine, gain_q[None, :], gain_k[None, :], seg[:, None], seg[None, :])


def attend_back_kernel(
    tile, query, key, value, grad_mixed, stat, q_raw, k_raw, cosine, sine, gain_q, gain_k, seg_col, seg_row,
    grad_q, grad_k, grad_v, sum_k, sum_v
):
    rows = q_raw.shape[0]
    scale = HD ** (-0.5)
    keys = key[...]
    values = value[...]
    keys_t = keys.T

    def through(grad, raw_ref, gain_ref, part):
        grad = grad.astype(jnp.bfloat16).astype(jnp.float32)
        raw = raw_ref[part, :]
        gain = gain_ref[...]
        inverse = lax.rsqrt(jnp.mean(raw * raw, axis=-1, keepdims=True) + norm_epsilon)
        grad = unturned_head(grad, cosine[part, :], sine[part, :]) * gain
        dots = jnp.mean(grad * raw, axis=-1, keepdims=True)
        return (inverse * (grad - raw * (inverse * inverse * dots))).astype(jnp.bfloat16)

    for start in range(0, rows, tile):
        part = slice(start, start + tile)
        queries = query[part, :]
        grads = grad_mixed[part, :]
        scores = dot_nt(keys, queries) * scale
        scores = jnp.where(seg_col[...] == seg_row[:, part], scores, masked_score)
        soft = jnp.exp(scores - stat[0, :, part])
        grad_soft = dot_nt(values, grads)
        delta = jnp.sum(soft * grad_soft, axis=0, keepdims=True)
        grad_scores = (soft * (grad_soft - delta)).astype(jnp.bfloat16)
        term_k = dot_nn(grad_scores, queries)
        term_v = dot_nn(soft.astype(jnp.bfloat16), grads)
        if start == 0:
            sum_k[...] = term_k
            sum_v[...] = term_v
        else:
            sum_k[...] += term_k
            sum_v[...] += term_v
        grad_q[part, :] = through(dot_nn(keys_t, grad_scores).T * scale, q_raw, gain_q, part)
    for start in range(0, rows, tile):
        part = slice(start, start + tile)
        grad_k[part, :] = through(sum_k[part, :] * scale, k_raw, gain_k, part)
        grad_v[part, :] = sum_v[part, :].astype(jnp.bfloat16)


def attend_back(kept, grad_mixed, raw, cosine, sine, gain_q, gain_k, segment):
    query, key, value, stat = kept
    unused, length, width = raw.shape
    heads = width // HD
    tile = min(512, length)
    head = pl.BlockSpec((length, HD), lambda h: (0, h))
    raw_head = [pl.BlockSpec((None, length, HD), functools.partial(lambda m, h: (m, 0, h), m)) for m in range(3)]
    fixed = lambda shape: pl.BlockSpec(shape, lambda h: (0, 0))
    seg = segment.astype(jnp.float32)
    low = jax.ShapeDtypeStruct((length, width), jnp.bfloat16)
    return pl.pallas_call(
        functools.partial(attend_back_kernel, tile),
        grid=(heads,),
        in_specs=[head, head, head, head, pl.BlockSpec((1, 1, length), lambda h: (h, 0, 0)), raw_head[0], raw_head[1],
                  fixed((length, HD)), fixed((length, HD)), fixed((1, HD)), fixed((1, HD)),
                  fixed((length, 1)), fixed((1, length))],
        out_specs=[head, head, head],
        out_shape=[low, low, low],
        scratch_shapes=[pltpu.VMEM((length, HD), jnp.float32), pltpu.VMEM((length, HD), jnp.float32)],
        cost_estimate=pl.CostEstimate(
            flops=heads * length * HD, bytes_accessed=length * width, transcendentals=0
        ),
        name="attend_back",
    )(query, key, value, grad_mixed, stat, raw, raw, cosine, sine, gain_q[None, :], gain_k[None, :],
      seg[:, None], seg[None, :])


def doc_layout(lengths, chosen, position):
    slots = jnp.arange(lengths.shape[0], dtype=jnp.int32)
    doc_ends = jnp.sum(jnp.where(slots[:, None] >= slots[None, :], lengths[None, :], 0), axis=1)
    starts = doc_ends - lengths
    segment = jnp.sum((position[:, None] >= doc_ends[None, :]).astype(jnp.int32), axis=1)
    doc_pick = (segment[:, None] == slots[None, :]).astype(jnp.int32)
    offset = position - jnp.sum(doc_pick * starts[None, :], axis=1)
    adapter = jnp.sum(doc_pick * chosen[None, :], axis=1)
    return (segment, offset, adapter)


def column_mask(adapter, columns):
    groups = jnp.arange(columns, dtype=jnp.int32) // R
    return (groups[None, :] == adapter[:, None]).astype(jnp.float32)


def qkv_kernel(x_ref, reduced_ref, w_ref, up_ref, out_ref):
    width = w_ref.shape[0] * w_ref.shape[1]
    weights = w_ref[...].reshape(width, x_ref.shape[1])
    out_ref[0] = dot_nt(x_ref[...], weights) + dot_nt(reduced_ref[...], up_ref[0])


def qkv_project(normed_all, reduced_cat, w_group, up_group):
    length, width = normed_all.shape
    dp_count, unused, piece, unused = w_group.shape
    group = dp_count * piece
    rank = up_group.shape[2]
    half = dp_count // 2
    return pl.pallas_call(
        qkv_kernel,
        grid=(3, 2),
        in_specs=[
            pl.BlockSpec((length, width), lambda m, p: (0, 0)),
            pl.BlockSpec((length, rank), lambda m, p: (0, m)),
            pl.BlockSpec((half, None, piece, width), lambda m, p: (p, m, 0, 0)),
            pl.BlockSpec((1, group // 2, rank), lambda m, p: (m, p, 0)),
        ],
        out_specs=pl.BlockSpec((1, length, group // 2), lambda m, p: (m, 0, p)),
        out_shape=jax.ShapeDtypeStruct((3, length, group), jnp.float32),
        cost_estimate=pl.CostEstimate(
            flops=6 * length * width * group, bytes_accessed=2 * length * width + 12 * length * group + 6 * group * width,
            transcendentals=0,
        ),
        name="qkv_project",
    )(normed_all, reduced_cat, w_group, up_group)


def qkv_back_kernel(a_ref, b_ref, c_ref, w_ref, out_ref):
    dp_count, unused, piece, cols = w_ref.shape
    total = None
    for m, ref in enumerate((a_ref, b_ref, c_ref)):
        term = dot_nn(ref[...], w_ref[:, m].reshape(dp_count * piece, cols))
        total = term if total is None else total + term
    out_ref[...] = total.astype(jnp.bfloat16)


def qkv_back(grads, w_group):
    length, group = grads[0].shape
    dp_count, unused, piece, width = w_group.shape
    tile = min(256, width)
    whole = pl.BlockSpec((length, group), lambda i: (0, 0))
    return pl.pallas_call(
        qkv_back_kernel,
        grid=(width // tile,),
        in_specs=[whole, whole, whole, pl.BlockSpec((dp_count, 3, piece, tile), lambda i: (0, 0, 0, i))],
        out_specs=pl.BlockSpec((length, tile), lambda i: (0, i)),
        out_shape=jax.ShapeDtypeStruct((length, width), jnp.bfloat16),
        cost_estimate=pl.CostEstimate(flops=length * width, bytes_accessed=length * width, transcendentals=0),
        name="qkv_back",
    )(grads[0], grads[1], grads[2], w_group)


def expert_kernel(kept_in, which, *refs):
    (x_a, x_b, g_both, pick, pick_t, slot, w_in, w_down, a_in, b_in, a_down, b_down) = refs[:12]
    refs = refs[12 + kept_in:]
    (out_both, back_a, back_b, xs, ps, act_o, gate_o, up_o, reds) = refs[:9]
    (red_g, red_u, gred_d, down_acc, down_red, gx_acc, gred_g, gred_u, sum_out_a, sum_out_b, sum_back_a, sum_back_b) = refs[9:]
    low = jnp.bfloat16
    e = pl.program_id(0)
    f = pl.program_id(1)
    last = pl.num_programs(1) - 1
    cap = pick.shape[2]
    rank = a_in.shape[3]
    rows = xs.shape[1]
    groups = lax.shift_right_logical(lax.broadcasted_iota(jnp.int32, (rows, rank), 1), R.bit_length() - 1)
    mask = jnp.where(groups.astype(jnp.float32) == slot[0, :, 1:2], 1.0, 0.0)

    @pl.when(f == 0)
    def _():
        for b, x_ref in enumerate((x_a, x_b)):
            part = slice(b * cap, (b + 1) * cap)
            g_place = which[1] if b == 0 else 1 - which[1]
            xs[0, part, :] = dot_nn(pick[0, b], x_ref[...]).astype(low)
            ps[0, part, :] = (slot[0, part, 0:1] * dot_nn(pick[0, b], g_both[g_place])).astype(low)
        red_g[...] = (mask * dot_nn(xs[0], a_in[0, 0])).astype(low)
        red_u[...] = (mask * dot_nn(xs[0], a_in[0, 1])).astype(low)
        gred_d[...] = (mask * dot_nt(ps[0], b_down[0])).astype(low)

    x = xs[0]
    p = ps[0]
    gate = dot_nn(x, w_in[0, 0]) + dot_nn(red_g[...], b_in[0, 0])
    up = dot_nn(x, w_in[0, 1]) + dot_nn(red_u[...], b_in[0, 1])
    grad_act = dot_nt(p, w_down[0]) + dot_nt(gred_d[...], a_down[0])
    sigma = 1.0 / (1.0 + jnp.exp(-gate))
    silu = gate * sigma
    act = (silu * up).astype(low)
    grad_gate = (grad_act * up * (sigma * (1.0 + gate * (1.0 - sigma)))).astype(low)
    grad_up = (grad_act * silu).astype(low)
    act_o[0] = act
    gate_o[0] = grad_gate
    up_o[0] = grad_up
    down_term = dot_nn(act, w_down[0])
    down_red_term = dot_nn(act, a_down[0])
    gx_term = dot_nt(grad_gate, w_in[0, 0]) + dot_nt(grad_up, w_in[0, 1])
    gred_g_term = dot_nt(grad_gate, b_in[0, 0])
    gred_u_term = dot_nt(grad_up, b_in[0, 1])

    @pl.when(f == 0)
    def _():
        down_acc[...] = down_term
        down_red[...] = down_red_term
        gx_acc[...] = gx_term
        gred_g[...] = gred_g_term
        gred_u[...] = gred_u_term

    @pl.when(f > 0)
    def _():
        down_acc[...] += down_term
        down_red[...] += down_red_term
        gx_acc[...] += gx_term
        gred_g[...] += gred_g_term
        gred_u[...] += gred_u_term

    @pl.when(f == last)
    def _():
        reduced_d = (mask * down_red[...]).astype(low)
        back_g = (mask * gred_g[...]).astype(low)
        back_u = (mask * gred_u[...]).astype(low)
        for i, value in enumerate((red_g[...], red_u[...], reduced_d, back_g, back_u, gred_d[...])):
            reds[0, :, i * rank : (i + 1) * rank] = value
        produced = down_acc[...] + dot_nn(reduced_d, b_down[0])
        scaled = (slot[0, :, 0:1] * produced).astype(low)
        grads = (gx_acc[...] + dot_nt(back_g, a_in[0, 0]) + dot_nt(back_u, a_in[0, 1])).astype(low)
        for b, (out_sum, back_ref, back_sum) in enumerate(
            ((sum_out_a, back_a, sum_back_a), (sum_out_b, back_b, sum_back_b))
        ):
            part = slice(b * cap, (b + 1) * cap)
            out_ref = out_both.at[which[3] if b == 0 else 1 - which[3]]
            for values, total, result in ((scaled, out_sum, out_ref), (grads, back_sum, back_ref)):
                term = dot_nn(pick_t[0, b], values[part, :])

                @pl.when(e == 0)
                def _():
                    total[...] = term

                @pl.when(e > 0)
                def _():
                    total[...] += term

                @pl.when(e == pl.num_programs(0) - 1)
                def _():
                    result[...] = total[...].astype(low)


def run_experts(which, x_pair, g_all, pick, pick_t, slot, weights, kept):
    w_in, w_down, a_in, b_in, a_down, b_down = weights
    experts, unused, width, ff = w_in.shape
    unused, dp_count, cap, own_rows = pick.shape
    rank = a_down.shape[2]
    rows = 2 * cap
    tile = min(512, ff)
    low = jnp.bfloat16
    f32 = jnp.float32
    one = pl.Buffered(1)
    token = pl.BlockSpec((own_rows, width), lambda e, f, w: (0, 0), pipeline_mode=one)
    stored = [
        ((experts, dp_count * cap, width), (1, rows, width), lambda e, f, w: (e, w[4], 0)),
        ((experts, dp_count * cap, width), (1, rows, width), lambda e, f, w: (e, w[4], 0)),
        ((experts, dp_count * cap, ff), (1, rows, tile), lambda e, f, w: (e, w[4], f)),
        ((experts, dp_count * cap, ff), (1, rows, tile), lambda e, f, w: (e, w[4], f)),
        ((experts, dp_count * cap, ff), (1, rows, tile), lambda e, f, w: (e, w[4], f)),
        ((experts, dp_count * cap, 6 * rank), (1, rows, 6 * rank), lambda e, f, w: (e, w[4], 0)),
    ]
    in_specs = [
        token, token, pl.BlockSpec((2, own_rows, width), lambda e, f, w: (w[0], 0, 0), pipeline_mode=one),
        pl.BlockSpec((1, 2, cap, own_rows), lambda e, f, w: (e, w[4], 0, 0)),
        pl.BlockSpec((1, 2, own_rows, cap), lambda e, f, w: (e, w[4], 0, 0)),
        pl.BlockSpec((1, rows, 2), lambda e, f, w: (e, w[4], 0)),
        pl.BlockSpec((1, 2, width, tile), lambda e, f, w: (e, 0, 0, f)),
        pl.BlockSpec((1, tile, width), lambda e, f, w: (e, f, 0)),
        pl.BlockSpec((1, 2, width, rank), lambda e, f, w: (e, 0, 0, 0)),
        pl.BlockSpec((1, 2, rank, tile), lambda e, f, w: (e, 0, 0, f)),
        pl.BlockSpec((1, tile, rank), lambda e, f, w: (e, f, 0)),
        pl.BlockSpec((1, rank, width), lambda e, f, w: (e, 0, 0)),
    ] + [pl.BlockSpec(memory_space=pl.ANY) for unused in kept]
    part = jax.ShapeDtypeStruct((own_rows, width), low)
    results = pl.pallas_call(
        functools.partial(expert_kernel, len(kept)),
        grid_spec=pltpu.PrefetchScalarGridSpec(
            num_scalar_prefetch=1,
            grid=(experts, ff // tile),
            in_specs=in_specs,
            out_specs=[pl.BlockSpec((2, own_rows, width), lambda e, f, w: (w[2], 0, 0), pipeline_mode=one), token, token]
            + [pl.BlockSpec(block, index) for unused, block, index in stored],
            scratch_shapes=[
            pltpu.VMEM((rows, rank), low),
            pltpu.VMEM((rows, rank), low),
            pltpu.VMEM((rows, rank), low),
            pltpu.VMEM((rows, width), f32),
            pltpu.VMEM((rows, rank), f32),
            pltpu.VMEM((rows, width), f32),
            pltpu.VMEM((rows, rank), f32),
            pltpu.VMEM((rows, rank), f32),
        ] + [pltpu.VMEM((own_rows, width), f32) for unused in range(4)],
        ),
        out_shape=[jax.ShapeDtypeStruct((dp_count, own_rows, width), low)] + [part] * 2 + [jax.ShapeDtypeStruct(shape, low) for shape, unused, unused2 in stored],
        input_output_aliases={13 + i: 0 if i == 0 else 2 + i for i in range(len(kept))},
        cost_estimate=pl.CostEstimate(
            flops=experts * rows * width, bytes_accessed=experts * rows * width, transcendentals=0
        ),
        compiler_params=pltpu.CompilerParams(vmem_limit_bytes=60 * 1024 * 1024),
        name="experts",
    )(which, *x_pair, g_all, pick, pick_t, slot, *weights, *kept)
    return results[1:3], [results[0]] + list(results[3:])


def adapter_kernel(which, xs, ps, act, gate, up, reds, out):
    rank = out.shape[3]
    red = [reds[0, :, i * rank : (i + 1) * rank] for i in range(6)]
    into = dot_tn(xs[0], reds[0, :, 3 * rank : 5 * rank])
    parts = [into[:, :rank], into[:, rank:], dot_tn(act[0], red[5])]
    for wide in (dot_tn(red[0], gate[0]), dot_tn(red[1], up[0]), dot_tn(red[2], ps[0])):
        parts += [wide[:, i : i + rank] for i in range(0, wide.shape[1], rank)]
    start = 0
    for part in parts:
        out[0, 0, start : start + part.shape[0], :] = part.astype(jnp.bfloat16)
        start += part.shape[0]


def adapter_grads(kept, order):
    xs, ps, act, gate, up, reds = kept
    experts, rows, width = xs.shape
    ff = act.shape[2]
    n = order.shape[0]
    rank = reds.shape[2] // 6
    total = (3 * width + 3 * ff) // n
    wide = pl.BlockSpec((1, rows, width // n), lambda e, k, w: (e, 0, w[k]))
    narrow = pl.BlockSpec((1, rows, ff // n), lambda e, k, w: (e, 0, w[k]))
    return pl.pallas_call(
        adapter_kernel,
        grid_spec=pltpu.PrefetchScalarGridSpec(
            num_scalar_prefetch=1,
            grid=(experts, n),
            in_specs=[wide, wide, narrow, narrow, narrow, pl.BlockSpec((1, rows, 6 * rank), lambda e, k, w: (e, 0, 0))],
            out_specs=pl.BlockSpec((1, 1, total, rank), lambda e, k, w: (k, e, 0, 0)),
        ),
        out_shape=jax.ShapeDtypeStruct((n, experts, total, rank), jnp.bfloat16),
        cost_estimate=pl.CostEstimate(flops=rows * width, bytes_accessed=rows * width, transcendentals=0),
        name="adapter_grads",
    )(order, xs, ps, act, gate, up, reds)


def swap(values, axis, distance, count):
    return lax.ppermute(values, axis, [(i, i ^ distance) for i in range(count)])


def near(values, axis, count):
    return [swap(values, axis, 1, count), swap(values, axis, 2, count)]


def spread(values, axis, count, close=None):
    one, two = near(values, axis, count) if close is None else close
    if count == 4 and values.size >= half_from:
        half = values.shape[0] // 2
        three = [swap(two[:half], axis, 1, count), swap(one[half:], axis, 2, count)]
        return [values, one, two, jnp.concatenate(three, axis=0)]
    return [values, one, two] + [swap(values, axis, k, count) for k in range(3, count)]


def collect_begin(blocks, axis, count):
    if count == 4 and blocks[0].size >= half_from:
        half = blocks[0].shape[0] // 2
        return [
            swap(blocks[3][:half], axis, 1, count),
            swap(blocks[3][half:], axis, 2, count),
            swap(blocks[1][:half], axis, 1, count),
            swap(blocks[2][half:], axis, 2, count),
        ]
    return [swap(blocks[k], axis, k, count) for k in range(1, count)]


def collect_turn(blocks, arrived, axis, count):
    if count == 4 and blocks[0].size >= half_from:
        half = blocks[0].shape[0] // 2
        to_two = (blocks[2][:half].astype(jnp.float32) + arrived[0].astype(jnp.float32)).astype(blocks[2].dtype)
        to_one = (blocks[1][half:].astype(jnp.float32) + arrived[1].astype(jnp.float32)).astype(blocks[1].dtype)
        to_two, to_one = pin(to_two, to_one)
        return [swap(to_two, axis, 2, count), swap(to_one, axis, 1, count)]
    return []


def collect_end(blocks, arrived, turned, axis, count):
    f32 = jnp.float32
    if turned:
        half = blocks[0].shape[0] // 2
        top = blocks[0][:half].astype(f32) + arrived[2].astype(f32) + turned[0].astype(f32)
        low = blocks[0][half:].astype(f32) + arrived[3].astype(f32) + turned[1].astype(f32)
        return jnp.concatenate([top, low], axis=0)
    return sum((x.astype(f32) for x in arrived), blocks[0].astype(f32))


def collect(blocks, axis, count):
    arrived = collect_begin(blocks, axis, count)
    return collect_end(blocks, arrived, collect_turn(blocks, arrived, axis, count), axis, count)


def collect_chips(blocks, count):
    pairs = blocks.reshape((count // 2, 2) + blocks.shape[1:])
    summed = pairs[:, 0].astype(jnp.float32) + swap(pairs[:, 1], "dp", 1, count).astype(jnp.float32)
    total = summed[0]
    summed = summed.astype(blocks.dtype)
    for c in range(1, count // 2):
        total = total + swap(summed[c], "dp", 2 * c, count).astype(jnp.float32)
    return total


def pin(*values):
    return lax.optimization_barrier(values)


def local(
    layer_input,
    out_cotangent,
    gain_attention,
    gain_query,
    gain_key,
    gain_ffn,
    w_qkv,
    w_output,
    a_attention,
    b_attention,
    expert_w_in,
    expert_w_down,
    expert_a_in,
    expert_b_in,
    expert_a_down,
    expert_b_down,
    route_experts,
    route_gates,
    doc_lengths,
    adapter_ids,
):
    low = jnp.bfloat16
    f32 = jnp.float32
    own_rows = layer_input.shape[1]
    full_width = layer_input.shape[2]
    n = lax.axis_size("seq")
    dp_count = lax.axis_size("dp")
    s = lax.axis_index("seq")
    d = lax.axis_index("dp")
    length = own_rows * n
    rank_columns = a_attention.shape[2]
    group_width = full_width // n
    group_heads = H // n
    piece = group_width // dp_count
    group_start = s * group_width
    order = s ^ jnp.arange(n, dtype=jnp.int32)
    position = (order[:, None] * own_rows + jnp.arange(own_rows, dtype=jnp.int32)[None, :]).reshape(-1)
    segment, offset, adapter = doc_layout(doc_lengths[0], adapter_ids[0], position)
    own_adapter = adapter[:own_rows]
    own_mask = column_mask(own_adapter, rank_columns)
    full_mask = column_mask(adapter, rank_columns)

    gates = route_gates[0].T
    gates_high = gates.astype(low)
    meta = jnp.concatenate(
        [
            route_experts[0].T.astype(low),
            gates_high,
            (gates - gates_high.astype(f32)).astype(low),
            own_adapter[None, :].astype(low),
            jnp.zeros((7, own_rows), low),
        ],
        axis=0,
    )
    ab_piece = jnp.concatenate([a_attention[0:3], jnp.swapaxes(b_attention, 1, 2)], axis=0).reshape(-1, rank_columns)
    ab_rows = ab_piece.shape[0]
    ab_piece = jnp.concatenate([ab_piece, meta.reshape(-1, rank_columns)], axis=0)
    ab_got = lax.all_gather(ab_piece, "dp", axis=0)
    tokens = layer_input[0].astype(f32)
    normed = rms_scale(tokens, gain_attention).astype(low)
    wt_piece = jnp.swapaxes(w_qkv, 1, 2)
    wt_piece, ab_got, *close = pin(wt_piece, ab_got, *near(normed, "seq", n))
    w_group = lax.all_gather(wt_piece, "dp", axis=0)
    dp_order = d ^ jnp.arange(dp_count, dtype=jnp.int32)
    meta_all = ab_got[:, ab_rows:].reshape((dp_count,) + meta.shape)[dp_order].astype(f32)
    ab_group = ab_got[:, :ab_rows].reshape(dp_count, 7, piece, rank_columns)
    ab_group = jnp.swapaxes(ab_group, 0, 1).reshape(7, group_width, rank_columns)
    local_count = expert_w_in.shape[0]
    expert_count = local_count * dp_count
    capacity = own_rows * TOP // expert_count * 9 // 8
    capacity = -(-capacity // 16) * 16
    named = meta_all[:, 0:TOP, :].astype(jnp.int32)
    gates_all = meta_all[:, TOP : 2 * TOP, :] + meta_all[:, 2 * TOP : 3 * TOP, :]
    sets_all = meta_all[:, 3 * TOP, :]
    mine = d * local_count + jnp.arange(local_count, dtype=jnp.int32)
    hit = (named[None] == mine[:, None, None, None]).astype(f32)
    member = jnp.sum(hit, axis=2)
    token_gate = jnp.sum(hit * gates_all[None], axis=2)
    t_index = jnp.arange(own_rows, dtype=jnp.int32)
    upto = (t_index[:, None] <= t_index[None, :]).astype(low)
    rank = jnp.einsum("ejt,tu->eju", member.astype(low), upto, preferred_element_type=f32) - 1.0
    slots = jnp.arange(capacity, dtype=jnp.int32).astype(f32)
    rank = jnp.where(member > 0.5, rank, -1.0)
    pick = slots[None, None, :, None] == rank[:, :, None, :]
    pick_t = (rank[:, :, :, None] == slots[None, None, None, :]).astype(low)
    slot_gate = jnp.sum(jnp.where(pick, token_gate[:, :, None, :], 0.0), axis=-1)
    slot_set = jnp.sum(jnp.where(pick, sets_all[None, :, None, :], 0.0), axis=-1)
    slot = jnp.stack([slot_gate, slot_set], axis=-1).reshape(local_count, dp_count * capacity, 2)
    pick = pick.astype(low)

    cosine, sine = rope_tables(offset, HD)

    dot = lambda a, b: jnp.dot(a, b, preferred_element_type=f32)
    dot_t = lambda a, b: lax.dot_general(a, b, (((1,), (1,)), ((), ())), preferred_element_type=f32)
    dot_l = lambda a, b: lax.dot_general(a, b, (((0,), (0,)), ((), ())), preferred_element_type=f32)

    share = jnp.concatenate([ab_group[0:3], ab_group[6:7]], axis=0)
    share_full = jnp.stack(spread(share, "seq", n))[order]
    share_full = jnp.swapaxes(share_full, 0, 1).reshape(4, full_width, rank_columns)
    down_cat = jnp.swapaxes(share_full[0:3], 0, 1).reshape(full_width, 3 * rank_columns)
    upt_output = share_full[3]
    upt_group = ab_group[3:6]
    normed_all = jnp.concatenate(spread(normed, "seq", n, close), axis=0)
    reduced_cat = (jnp.tile(full_mask, (1, 3)) * dot(normed_all, down_cat)).astype(low)
    out_piece = jnp.concatenate([w_output, a_attention[3]], axis=1)
    out_piece, w_group, pick, pick_t, slot, cosine, sine, normed_all, reduced_cat, upt_group, upt_output = pin(
        out_piece, w_group, pick, pick_t, slot, cosine, sine, normed_all, reduced_cat, upt_group, upt_output
    )
    out_maps = lax.all_gather(out_piece, "dp", axis=0, tiled=True)
    reduced_list = [reduced_cat[:, m * rank_columns : (m + 1) * rank_columns] for m in range(3)]
    raw = qkv_project(normed_all, reduced_cat, w_group, upt_group)
    grad_send, raw = pin(out_cotangent[0], raw)
    grad_got = lax.all_gather(grad_send, "dp", axis=0)
    grad_own = jnp.stack([out_cotangent[0], swap(out_cotangent[0], "dp", 1, dp_count)])
    mixed_group, query_heads, key_heads, value_heads, stat = attend(
        raw, cosine, sine, gain_query, gain_key, segment
    )

    partial_out = dot(mixed_group, out_maps).astype(low).reshape(n, own_rows, full_width + rank_columns)
    summed = collect([partial_out[k] for k in range(n)], "seq", n)
    output_reduced = (own_mask * summed[:, full_width:]).astype(low)
    attended = summed[:, :full_width] + dot_t(output_reduced, upt_output)
    hidden = tokens + attended
    normed_ffn = rms_scale(hidden, gain_ffn).astype(low)
    weights = (expert_w_in, expert_w_down, expert_a_in, expert_b_in, expert_a_down, expert_b_down)
    chips = dp_count // 2
    turns = [0] + list(range(chips // 2, chips)) + list(range(1, chips // 2))
    kept = ()
    rows = normed_ffn
    here = normed_ffn
    arrived = swap(rows, "dp", 2 * turns[1], dp_count)
    other = swap(here, "dp", 1, dp_count)
    leaving = None
    flying = None
    grad_normed_ffn = None
    for i, c in enumerate(turns):
        if i > 0:
            here = arrived
            if flying is not None:
                here, flying = pin(here, flying)
                grad_normed_ffn = grad_normed_ffn + flying.astype(f32)
            other = swap(here, "dp", 1, dp_count)
            rows, here, other, leaving = pin(rows, here, other, leaving)
            if i < chips - 1:
                arrived = swap(rows, "dp", 2 * turns[i + 1], dp_count)
            if i == 1:
                grad_normed_ffn = leaving
            else:
                flying = swap(leaving, "dp", 2 * turns[i - 1], dp_count)
        block = lax.shift_right_logical(d, 1) ^ c
        place = d & 1
        which = jnp.stack(([block, place] if c else [0 * d, 0 * d]) + [block, place, 0 * d + c]).astype(jnp.int32)
        (back, back_other), kept = run_experts(
            which, (here, other), grad_got if c else grad_own, pick, pick_t, slot, weights, kept
        )
        if i == chips - 1 and flying is not None:
            flying, back_other = pin(flying, back_other)
        leaving = back.astype(f32) + swap(back_other, "dp", 1, dp_count).astype(f32)
        if i > 0:
            leaving = leaving.astype(low)
    if flying is not None:
        grad_normed_ffn = grad_normed_ffn + flying.astype(f32)
    outs_all, *kept = kept
    leaving, *kept = pin(leaving, *kept)
    flying = swap(leaving, "dp", 2 * turns[-1], dp_count)
    flat = adapter_grads(kept, order)
    flat, flying = pin(flat, flying)
    grad_normed_ffn = grad_normed_ffn + flying.astype(f32)

    outs_all, grad_normed_ffn = pin(outs_all, grad_normed_ffn)
    mixture = lax.psum_scatter(outs_all, "dp", scatter_dimension=0)
    grad_out = out_cotangent[0].astype(f32)
    unused, pull_ffn = jax.vjp(lambda values: rms_scale(values, gain_ffn), hidden)
    grad_hidden = grad_out + pull_ffn(grad_normed_ffn)[0]
    grad_hidden_low = grad_hidden.astype(low)
    grad_reduced_output = (own_mask * dot(grad_hidden_low, upt_output)).astype(low)
    grad_pack = jnp.concatenate([grad_hidden_low, grad_reduced_output, output_reduced], axis=1)
    flat, *grad_packs = pin(flat, *spread(grad_pack, "seq", n))
    expert_terms = [flat[k] for k in range(n)]
    expert_arrived = collect_begin(expert_terms, "seq", n)
    grad_pack_all = jnp.concatenate(grad_packs, axis=0)
    grad_all = grad_pack_all[:, :full_width]
    grad_reduced_all = grad_pack_all[:, full_width : full_width + rank_columns]
    output_reduced_all = grad_pack_all[:, full_width + rank_columns :]
    grad_mixed_group = dot_t(grad_pack_all[:, : full_width + rank_columns], out_maps).astype(low)
    grad_cols = lax.dynamic_slice_in_dim(grad_all, group_start, group_width, 1)
    grad_upt_output = dot_l(grad_cols, output_reduced_all)
    grad_down_output = dot_l(mixed_group, grad_reduced_all)
    grad_raw_list = attend_back(
        (query_heads, key_heads, value_heads, stat),
        grad_mixed_group,
        raw,
        cosine,
        sine,
        gain_query,
        gain_key,
        segment,
    )
    pinned = pin(*grad_raw_list, *expert_arrived)
    grad_raw_list = list(pinned[:3])
    expert_arrived = pinned[3:]
    expert_turned = collect_turn(expert_terms, expert_arrived, "seq", n)
    partial_reduced = jnp.concatenate(
        [dot(grad_raw_list[m], upt_group[m]) for m in range(3)], axis=1
    ).astype(low)
    partial_reduced, *grad_raw_list = pin(partial_reduced, *grad_raw_list)
    partial_reduced = partial_reduced.reshape(n, own_rows, 3 * rank_columns)
    summed_reduced = collect([partial_reduced[k] for k in range(n)], "seq", n)
    grad_reduced = (jnp.tile(own_mask, (1, 3)) * summed_reduced).astype(low)
    grad_reduced, *grad_raw_late = pin(grad_reduced, *grad_raw_list)
    grad_reduced_full = jnp.concatenate(spread(grad_reduced, "seq", n), axis=0)
    partial_normed = qkv_back(grad_raw_list, w_group).reshape(n, own_rows, full_width)
    partial_normed, grad_reduced, *expert_turned = pin(partial_normed, grad_reduced, *expert_turned)
    expert_sum = collect_end(expert_terms, expert_arrived, expert_turned, "seq", n)
    grad_upt = [dot_l(grad_raw_late[m], reduced_list[m]) for m in range(3)]
    normed_cols = lax.dynamic_slice_in_dim(normed_all, group_start, group_width, 1)
    grad_down_cat = dot_l(normed_cols, grad_reduced_full)
    parts = [grad_down_cat[:, m * rank_columns : (m + 1) * rank_columns] for m in range(3)]
    piled = lambda some: jnp.stack([x.astype(low).reshape(dp_count, piece, rank_columns) for x in some], axis=1)
    early_parts = piled([grad_down_output] + grad_upt + [grad_upt_output])
    early_parts = lax.psum_scatter(early_parts, "dp", scatter_dimension=0)
    late_parts = collect_chips(piled(parts)[dp_order], dp_count)
    normed_terms = [partial_normed[k] for k in range(n)]
    arrived = collect_begin(normed_terms, "seq", n)
    summed_back = collect_end(normed_terms, arrived, collect_turn(normed_terms, arrived, "seq", n), "seq", n)
    summed_back, mixture, hidden = pin(summed_back, mixture, hidden)
    layer_output = (hidden + mixture.astype(f32)).astype(low)[None]
    grad_normed = summed_back + dot_t(grad_reduced, down_cat)
    unused_input, pull_input = jax.vjp(lambda values: rms_scale(values, gain_attention), tokens)
    input_grad = (grad_hidden + pull_input(grad_normed)[0]).astype(low)[None]

    early_parts, input_grad = pin(early_parts, input_grad)
    early_parts = early_parts.astype(f32)
    grad_a_attention = jnp.concatenate([late_parts, early_parts[:1]], axis=0)
    grad_b_attention = jnp.swapaxes(early_parts[1:], 1, 2)
    own_width = full_width // n
    own_ff = expert_w_down.shape[1] // n
    columns = lambda x, count: jnp.swapaxes(x.reshape(local_count, count, -1, rank_columns, rank_columns), 2, 3).reshape(
        local_count, count, rank_columns, -1
    )
    ends = [2 * own_width, 2 * own_width + own_ff, 2 * own_width + 3 * own_ff]
    grad_a_in = expert_sum[:, : ends[0]].reshape(local_count, 2, own_width, rank_columns)
    grad_a_down = expert_sum[:, ends[0] : ends[1]]
    grad_b_in = columns(expert_sum[:, ends[1] : ends[2]], 2)
    grad_b_down = columns(expert_sum[:, ends[2] :], 1)[:, 0]
    return (
        layer_output,
        input_grad,
        grad_a_attention,
        grad_b_attention,
        grad_a_in,
        grad_b_in,
        grad_a_down,
        grad_b_down,
    )


def solution(mesh):
    return jax.shard_map(
        local,
        mesh=mesh,
        in_specs=(
            P("dp", "seq", None),
            P("dp", "seq", None),
            P(),
            P(),
            P(),
            P(),
            P(None, None, ("seq", "dp")),
            P(("seq", "dp"), None),
            P(None, ("seq", "dp"), None),
            P(None, None, ("seq", "dp")),
            P("dp", None, None, None),
            P("dp", None, None),
            P("dp", None, None, None),
            P("dp", None, None, None),
            P("dp", None, None),
            P("dp", None, None),
            P("dp", "seq", None),
            P("dp", "seq", None),
            P("dp", None),
            P("dp", None),
        ),
        out_specs=(
            P("dp", "seq", None),
            P("dp", "seq", None),
            P(None, ("seq", "dp"), None),
            P(None, None, ("seq", "dp")),
            P("dp", None, "seq", None),
            P("dp", None, None, "seq"),
            P("dp", "seq", None),
            P("dp", None, "seq"),
        ),
        check_vma=False,
    )
```
